32 devices in a mesh: gx: 4 (over y, x), gy: 8 (over z, core).
Axes of the slice: x: 2, y: 2, z: 4, core: 2. Of those that a mesh axis runs over, the one named last changes fastest.
Arguments:
- atom_cell: int32 [4, 8, 4096], P('gx', 'gy'), may hold values from 0 to 49151
- atom_frac: float32 [3, 4, 8, 4096], P(None, 'gx', 'gy'), may hold values from 0 to 1
- atom_charge: float32 [4, 8, 4096], P('gx', 'gy'), may hold values from -6 to 6
- atom_count: int32 [4, 8], P('gx', 'gy'), may hold values from 1024 to 4096, as said below
- fine_kernel: float32 [9, 9, 9], replicated, may hold values from -1.8 to 1.8
- middle_kernel: float32 [9, 9, 9], replicated, may hold values from -0.9 to 0.9
- coarse_kernel: float32 [9, 9, 9], replicated, may hold values from -0.36 to 0.36
Outputs:
- potential: float32 [64, 192, 128], P('gx', 'gy')
- forces: float32 [3, 4, 8, 4096], P(None, 'gx', 'gy')
The draws below stay inside these ranges and needn't reach their ends.
Inputs may be any that keep to these rules, and one draw needn't show every extreme that they name: `atom_count`: slots at or past a block's count hold no atom. At least one block is full in every draw; about a quarter of the blocks are nearly full and the rest hold a quarter to a half of 4096.
All inputs are finite; a program needn't handle non-finite values.
Results may differ from the reference program's by a relative error of at most 0.0003.
Values sent between devices are 32-bit elements; how exact they have to be, the bound alone decides.
A program may use at most 128 MiB of HBM per device.

```python
import jax
import jax.numpy as jnp
from jax import lax

CX = 16
CY = 24
NZ = 128
ATOMS_DEV = 4096
KERNEL = 9
NX = 64
NY = 192
N_GX = 4
N_GY = 8


def draw_atom_count(key, part):
    key_low = jax.random.fold_in(key, 11)
    key_high = jax.random.fold_in(key, 12)
    key_pick = jax.random.fold_in(key, 13)
    key_full = jax.random.fold_in(key, 14)
    light = jax.random.randint(key_low, (N_GX, N_GY), ATOMS_DEV // 4, ATOMS_DEV // 2 + 1)
    heavy = ATOMS_DEV - jax.random.randint(key_high, (N_GX, N_GY), 0, ATOMS_DEV // 8)
    chosen = jax.random.randint(key_pick, (N_GX, N_GY), 0, 4) == 0
    counts = jnp.where(chosen, heavy, light).reshape(-1)
    fullest = jax.random.randint(key_full, (), 0, N_GX * N_GY)
    counts = jnp.where(jnp.arange(N_GX * N_GY) == fullest, ATOMS_DEV, counts)
    return counts.reshape(N_GX, N_GY).astype(jnp.int32)


def set_ends(entries, rng, least, high):
    spot = [jax.random.randint(jax.random.fold_in(rng, axis), (), 0, length) for axis, length in enumerate(entries.shape)]
    main_axis = entries.shape.index(max(entries.shape))
    next_to = spot[:main_axis] + [(spot[main_axis] + 1) % entries.shape[main_axis]] + spot[main_axis + 1:]
    return entries.at[tuple(spot)].set(least).at[tuple(next_to)].set(high)


def block_scale(own_key, extent, shards, least, high):
    gain, own = 1.0, jax.random.fold_in(own_key, 6)
    for axis_at, blocks in shards:
        steps = jnp.exp(jax.random.uniform(jax.random.fold_in(own, axis_at), (blocks,), jnp.float32, least / len(shards), high / len(shards)))
        gain = gain * jnp.repeat(steps, extent[axis_at] // blocks).reshape([-1 if axis == axis_at else 1 for axis in range(len(extent))])
    return gain


def normal_values(stream_key, shape, spread, reach, split=(), held_as=jnp.bfloat16):
    result = jax.random.normal(stream_key, shape, jnp.float32) * spread
    if len(split) > 0:
        result = block_scale(stream_key, shape, split, -0.22, 0.18) * result
    return jnp.clip(result, min=-reach, max=reach).astype(held_as)


def setup_inputs(seed: int = 0) -> dict:
    keys = jax.random.split(jax.random.key(seed), 8)
    atom_cell = set_ends(jax.random.randint(keys[0], (N_GX, N_GY, ATOMS_DEV), 0, CX * CY * NZ), jax.random.fold_in(keys[0], 1), 0, (CX * CY * NZ) - 1).astype(jnp.int32)
    atom_frac = jnp.clip(1.0 * jax.random.uniform(keys[1], (3, N_GX, N_GY, ATOMS_DEV), jnp.float32) ** block_scale(keys[1], (3, N_GX, N_GY, ATOMS_DEV), ((1, 4), (2, 8)), -0.2, 0.2), 0.0, 1.0)
    atom_charge = normal_values(keys[2], (N_GX, N_GY, ATOMS_DEV), 1.0, 6.0, ((0, 4), (1, 8)), jnp.float32)
    atom_count = draw_atom_count(jax.random.fold_in(keys[7], 71), 0)
    fine_kernel = normal_values(keys[4], (KERNEL, KERNEL, KERNEL), 0.3, 1.8, (), jnp.float32)
    middle_kernel = normal_values(keys[5], (KERNEL, KERNEL, KERNEL), 0.15, 0.9, (), jnp.float32)
    coarse_kernel = normal_values(keys[6], (KERNEL, KERNEL, KERNEL), 0.06, 0.36, (), jnp.float32)
    return dict(atom_cell=atom_cell, atom_frac=atom_frac, atom_charge=atom_charge, atom_count=atom_count, fine_kernel=fine_kernel, middle_kernel=middle_kernel, coarse_kernel=coarse_kernel)


def kernel_grid(kernel, grid_shape):
    half_width = KERNEL // 2
    offsets = jnp.arange(KERNEL, dtype=jnp.int32)
    place_x = jnp.mod(half_width - offsets, grid_shape[0])
    place_y = jnp.mod(half_width - offsets, grid_shape[1])
    place_z = jnp.mod(half_width - offsets, grid_shape[2])
    empty = jnp.zeros(grid_shape, jnp.float32)
    return empty.at[place_x[:, None, None], place_y[None, :, None], place_z[None, None, :]].add(kernel)


def convolve_whole(grid_in, kernel):
    spectrum = jnp.fft.rfftn(grid_in) * jnp.fft.rfftn(kernel_grid(kernel, grid_in.shape).astype(grid_in.dtype))
    return jnp.fft.irfftn(spectrum, s=grid_in.shape).astype(grid_in.dtype)


def restrict_whole(grid_in):
    for dimension in range(3):
        grid_in = 0.5 * jnp.roll(grid_in, 1, dimension) + grid_in + 0.5 * jnp.roll(grid_in, -1, dimension)
        grid_in = lax.slice_in_dim(grid_in, 0, grid_in.shape[dimension], 2, dimension)
    return grid_in


def prolong_whole(grid_in):
    for dimension in range(3):
        paired = jnp.stack([grid_in, 0.5 * (grid_in + jnp.roll(grid_in, -1, dimension))], axis=dimension + 1)
        new_shape = list(grid_in.shape)
        new_shape[dimension] = 2 * new_shape[dimension]
        grid_in = paired.reshape(new_shape)
    return grid_in


def reference(atom_cell, atom_frac, atom_charge, atom_count, fine_kernel, middle_kernel, coarse_kernel):
    block_x = jnp.arange(N_GX, dtype=jnp.int32)[:, None, None]
    block_y = jnp.arange(N_GY, dtype=jnp.int32)[None, :, None]
    base_x = block_x * CX + atom_cell // (CY * NZ)
    base_y = block_y * CY + (atom_cell // NZ) % CY
    base_z = atom_cell % NZ
    slot_index = jnp.arange(ATOMS_DEV, dtype=jnp.int32)[None, None, :]
    is_live = slot_index < atom_count[:, :, None]
    live_charge = jnp.where(is_live, atom_charge, 0.0)
    corner_ids = []
    weights = []
    slopes = []
    for corner in range(8):
        raised = [(corner >> 2) & 1, (corner >> 1) & 1, corner & 1]
        factors = [atom_frac[dimension] if raised[dimension] else 1.0 - atom_frac[dimension] for dimension in range(3)]
        sign_list = [1.0 if raised[dimension] else -1.0 for dimension in range(3)]
        flat_index = ((base_x + raised[0]) % NX * NY + (base_y + raised[1]) % NY) * NZ + (base_z + raised[2]) % NZ
        corner_ids.append(flat_index.astype(jnp.int32))
        weights.append(factors[0] * factors[1] * factors[2])
        slopes.append(jnp.stack([sign_list[0] * factors[1] * factors[2], factors[0] * sign_list[1] * factors[2], factors[0] * factors[1] * sign_list[2]]))
    corner_ids = jnp.stack(corner_ids)
    weights = jnp.stack(weights)
    spread_values = weights * live_charge[None]
    fine_charge = jax.ops.segment_sum(spread_values.reshape(-1), corner_ids.reshape(-1), num_segments=NX * NY * NZ).reshape(NX, NY, NZ)
    middle_charge = restrict_whole(fine_charge)
    coarse_charge = restrict_whole(middle_charge)
    coarse_potential = convolve_whole(coarse_charge, coarse_kernel)
    middle_potential = convolve_whole(middle_charge, middle_kernel) + prolong_whole(coarse_potential)
    potential = convolve_whole(fine_charge, fine_kernel) + prolong_whole(middle_potential)
    flat_potential = potential.reshape(-1)
    running = jnp.zeros((3, N_GX, N_GY, ATOMS_DEV), potential.dtype)
    for corner in range(8):
        running = running + slopes[corner] * flat_potential[corner_ids[corner]][None]
    forces = -live_charge[None] * running
    return potential, forces
```

```python
import jax
import jax.numpy as jnp
import ml_dtypes
import numpy as np
from jax import lax
from jax.experimental import pallas as pl
from jax.experimental.pallas import tpu as pltpu
from jax.sharding import PartitionSpec as P

CX = 16
CY = 24
NZ = 128
KERNEL = 9
HALF = KERNEL // 2
REACH = HALF + 1
LANES = 128
CHUNK = 512
LEVELS = 3
MESH = pl.DeviceIdType.MESH

BX = tuple(CX >> k for k in range(LEVELS))
BY = tuple(CY >> k for k in range(LEVELS))
ZS = tuple(NZ >> k for k in range(LEVELS))
PAIR = tuple((size + 2) // 2 for size in BX)
PERIOD = tuple(-(-(size + 1 + 2 * HALF) // 8) * 8 for size in BY)
WINDOW = tuple(2 * size + 2 * HALF for size in PAIR)
SPECTRA = tuple(size + 2 * HALF for size in PAIR)
ROWS = (32, 16, 8)
FIRST_LANE = (0, 0, ZS[1])
GRID_ROWS = (CX + 2) * CY
LOW_ROWS = ((BX[1] + 1) * ROWS[1], (BX[2] + 1) * ROWS[2])


def strip_row(x):
    return x if x < 12 else x + 4


def np_hat(distance):
    return np.maximum(1.0 - np.abs(distance), 0.0)


def np_ring_hat(distance, period):
    distance = np.abs(distance)
    return np.maximum(1.0 - np.minimum(distance, period - distance), 0.0)


def np_split(value):
    high = value.astype(np.float32).astype(ml_dtypes.bfloat16)
    low = (value - high.astype(np.float64)).astype(ml_dtypes.bfloat16)
    return high, low


def fine_places():
    xs, ys = np.full(GRID_ROWS, -1e6), np.full(GRID_ROWS, -1e6)
    for x in range(CX + 1):
        for y in range(CY):
            xs[x * CY + y], ys[x * CY + y] = x, y
        xs[(CX + 1) * CY + strip_row(x)], ys[(CX + 1) * CY + strip_row(x)] = x, CY
    return xs, ys


def transfer_xy():
    xs, ys = fine_places()
    parts = []
    for level in (1, 2):
        scale = 0.5**level
        layers = np.repeat(np.arange(BX[level] + 1), ROWS[level])
        rows = np.tile(np.arange(ROWS[level]), BX[level] + 1)
        weight = np_hat(xs[:, None] * scale - layers[None, :]) * np_hat(ys[:, None] * scale - rows[None, :])
        parts.append(weight * (rows <= BY[level])[None, :])
    return np.concatenate(parts, axis=1)


def transfer_z():
    weight = np.zeros((NZ, LANES))
    for level in (1, 2):
        z, low = np.arange(NZ)[:, None], np.arange(ZS[level])[None, :]
        weight[:, FIRST_LANE[level] : FIRST_LANE[level] + ZS[level]] = np_ring_hat(z * 0.5**level - low, ZS[level])
    return weight


def z_forward(level):
    size = ZS[level]
    angle = 2 * np.pi * np.arange(size)[:, None] * np.arange(size)[None, :] / size
    c, s = np.cos(angle), np.sin(angle)
    table = np.zeros((LANES, 2 * LANES))
    first = FIRST_LANE[level]
    if level == 0:
        table[:, :LANES], table[:, LANES:] = c, -s
    else:
        rows = slice(first, first + size)
        table[rows, :size], table[rows, size : 2 * size] = c, -s
        table[rows, LANES : LANES + size], table[rows, LANES + size : LANES + 2 * size] = -s, -c
    high, low = np_split(table)
    return np.concatenate([high, high, low], axis=0)


def z_inverse(level):
    size = ZS[level]
    angle = 2 * np.pi * np.arange(size)[:, None] * np.arange(size)[None, :] / size
    raised = np_ring_hat(np.arange(NZ)[None, :] * 0.5**level - np.arange(size)[:, None], size)
    c, s = np.cos(angle) @ raised / size, np.sin(angle) @ raised / size
    table = np.concatenate([np.concatenate([c, s], axis=1), np.concatenate([-s, c], axis=1)], axis=0)
    rows = 2 * LANES if level == 0 else LANES
    table = np.concatenate([table, np.zeros((rows - table.shape[0], 2 * LANES))], axis=0)
    high, low = np_split(table)
    return np.concatenate([high, high, low], axis=0)


def y_forward(level):
    size = PERIOD[level]
    angle = 2 * np.pi * np.arange(size)[:, None] * np.arange(size)[None, :] / size
    c, s = np.cos(angle), np.sin(angle)
    high, low = np_split(np.block([[c, s], [-s, c]]))
    return np.concatenate([high, high, low], axis=1)


def y_inverse(level):
    size = PERIOD[level]
    angle = 2 * np.pi * np.arange(ROWS[level])[:, None] * np.arange(size)[None, :] / size
    keep = (np.arange(ROWS[level]) <= BY[level])[:, None]
    c, s = np.cos(angle) * keep / size, np.sin(angle) * keep / size
    table = np.block([[c, -s], [s, c]]) if level == 0 else np.block([[c, -s]])
    if table.shape[0] < 16:
        table = np.concatenate([table, np.zeros((16 - table.shape[0], 2 * size))], axis=0)
    high, low = np_split(table)
    return np.concatenate([high, high, low], axis=1)


def taps_z(level):
    size = ZS[level]
    angle = 2 * np.pi * (np.arange(KERNEL) - HALF)[:, None] * np.arange(size)[None, :] / size
    table = np.zeros((LANES, 2 * LANES))
    for copy in range(1 if level == 0 else 2):
        table[:KERNEL, copy * size : (copy + 1) * size] = np.cos(angle)
        table[:KERNEL, LANES + copy * size : LANES + (copy + 1) * size] = np.sin(angle)
    return table.astype(np.float32)


def taps_y(level):
    size = PERIOD[level]
    angle = 2 * np.pi * np.arange(size)[:, None] * (np.arange(16) - HALF)[None, :] / size
    keep = (np.arange(16) < KERNEL)[None, :]
    c, s = np.cos(angle) * keep, np.sin(angle) * keep
    return np.block([[c, -s], [s, c]]).astype(np.float32)


def tables():
    xy = transfer_xy()
    z = transfer_z()
    bf16 = ml_dtypes.bfloat16
    out = [xy.T.astype(bf16), xy.astype(bf16), np.concatenate([z, z], axis=0).astype(bf16)]
    for level in range(LEVELS):
        out += [z_forward(level), z_inverse(level), y_forward(level), y_inverse(level), taps_z(level), taps_y(level)]
    return out


def split(value):
    high = value.astype(jnp.bfloat16)
    return high, (value - high.astype(jnp.float32)).astype(jnp.bfloat16)


def matmul(a, b):
    return jnp.dot(a, b, preferred_element_type=jnp.float32)


def matmul_nt(a, b):
    return lax.dot_general(a, b, (((1,), (1,)), ((), ())), preferred_element_type=jnp.float32)


def exact(a, b):
    return jnp.dot(a, b, preferred_element_type=jnp.float32, precision=lax.Precision.HIGHEST)


def rows_iota(rows, columns):
    return lax.broadcasted_iota(jnp.int32, (rows, columns), 0)


def bases(cell):
    return cell // (CY * NZ), (cell // NZ) % CY, cell % NZ


def two_rows(row, base, above, f):
    return jnp.where(row == base, 1.0 - f, jnp.where(row == above, f, 0.0))


def spread(count_ref, cell_ref, frac_ref, charge_ref, grid_ref):
    slots = cell_ref.shape[-1]
    grid_ref[...] = jnp.zeros_like(grid_ref)

    def step(index, carry):
        start = pl.multiple_of(index * CHUNK, CHUNK)
        part = pl.ds(start, CHUNK)
        base_x, base_y, base_z = bases(cell_ref[0, :, part])
        f = [frac_ref[k, 0, :, part] for k in range(3)]
        slot = start + lax.broadcasted_iota(jnp.int32, (1, CHUNK), 1)
        charge = jnp.where(slot < count_ref[0, 0], charge_ref[0, :, part], 0.0)
        row = rows_iota(CY, CHUNK)
        weight_x = two_rows(row, base_x, base_x + 1, f[0]) * charge
        weight_y = two_rows(row, base_y, base_y + 1, f[1])
        edge_y = jnp.where(base_y == CY - 1, f[1], 0.0)
        strip = row - jnp.where(row < 12, 0, 4)
        strip = jnp.where((row >= 12) & (row < 16), -1, strip)
        strip_x = two_rows(strip, base_x, base_x + 1, f[0]) * (charge * edge_y)
        top = jnp.concatenate([weight_x[x : x + 1] * weight_y for x in range(CX + 1)] + [strip_x], axis=0)
        row_z = rows_iota(NZ, CHUNK)
        z_side = two_rows(row_z, base_z, lax.rem(base_z + 1, NZ), f[2])
        top_high, top_low = split(top)
        z_high, z_low = split(z_side)
        both = matmul_nt(top_high, jnp.concatenate([z_high, z_low], axis=0))
        term = both[:, :LANES] + both[:, LANES:] + matmul_nt(top_low, z_high)
        grid_ref[...] += term.reshape(grid_ref.shape)
        return carry

    lax.fori_loop(0, slots // CHUNK, step, 0)


def lane_iota():
    return lax.broadcasted_iota(jnp.int32, (1, 1, LANES), 2)


def restrict(grid_ref, down_ref, down_z_ref, middle_ref, low_ref):
    high, low = split(grid_ref[...].reshape(GRID_ROWS, LANES))
    both = matmul(down_ref[...], jnp.concatenate([high, low], axis=1))
    high, low = split(both[:, :LANES] + both[:, LANES:])
    value = matmul(jnp.concatenate([high, low], axis=1), down_z_ref[...])
    middle = value[: LOW_ROWS[0]].reshape(BX[1] + 1, ROWS[1], LANES)
    coarse = value[LOW_ROWS[0] :].reshape(BX[2] + 1, ROWS[2], LANES)
    twice = jnp.concatenate([coarse, coarse], axis=1)
    first = BX[1] - BX[2]
    mine = lane_iota() < FIRST_LANE[2]
    middle_ref[:first] = middle[:first]
    middle_ref[first:] = jnp.where(mine, middle[first:], twice)
    low_ref[...] = jnp.where(mine, middle[: BX[2] + 1], twice)


def build_taps(level, kernel_ref, padded_ref, z_ref, y_ref, real_ref, imag_ref):
    padded_ref[...] = jnp.zeros_like(padded_ref)
    padded_ref[:, :KERNEL, :KERNEL] = kernel_ref[...]
    along_z = exact(padded_ref[...].reshape(KERNEL * 16, LANES), z_ref[...])
    size = PERIOD[level]
    for shift in range(0, KERNEL, 2):
        pieces = []
        for one in range(shift, min(shift + 2, KERNEL)):
            rows = along_z[one * 16 : (one + 1) * 16]
            pieces.append(jnp.concatenate([rows[:, :LANES], rows[:, LANES:]], axis=0))
        both = exact(y_ref[...], jnp.concatenate(pieces, axis=1))
        for k in range(len(pieces)):
            real_ref[shift + k] = both[:size, k * LANES : (k + 1) * LANES]
            imag_ref[shift + k] = both[size:, k * LANES : (k + 1) * LANES]


def three(value, axis):
    high, low = split(value)
    return jnp.concatenate([high, low, high], axis=axis)


def convolve(level, window_ref, real_ref, imag_ref, tables, along_z_ref, spectrum_ref):
    forward_z, inverse_z, forward_y, inverse_y = tables
    size, pair = PERIOD[level], PAIR[level]
    used = BX[level] + 1 + 2 * HALF
    flat = window_ref[:used].reshape(used * size, LANES)
    along_z_ref[: used * size] = matmul(three(flat, 1), forward_z[...])

    def part(layer, which):
        if layer >= used:
            return jnp.zeros((size, LANES), jnp.float32)
        return along_z_ref[layer * size : (layer + 1) * size, which * LANES : (which + 1) * LANES]

    count = SPECTRA[level]
    for first in range(0, count, 2):
        pieces = []
        for layer in range(first, min(first + 2, count)):
            real = part(layer, 0) - part(layer + pair, 1)
            imag = part(layer, 1) + part(layer + pair, 0)
            pieces.append(three(jnp.concatenate([real, imag], axis=0), 0))
        both = matmul(forward_y[...], jnp.concatenate(pieces, axis=1))
        for k in range(len(pieces)):
            spectrum_ref[first + k] = both[:, k * LANES : (k + 1) * LANES]
    products = []
    for out in range(pair):
        reals, imags = [], []
        for tile in range(0, size, 8):
            real = jnp.zeros((8, LANES), jnp.float32)
            imag = jnp.zeros((8, LANES), jnp.float32)
            for shift in range(KERNEL):
                a = spectrum_ref[out + shift, tile : tile + 8]
                b = spectrum_ref[out + shift, size + tile : size + tile + 8]
                c = real_ref[shift, tile : tile + 8]
                s = imag_ref[shift, tile : tile + 8]
                real = real + a * c - b * s
                imag = imag + a * s + b * c
            reals.append(real)
            imags.append(imag)
        products.append(three(jnp.concatenate(reals + imags, axis=0), 0))
    rows = ROWS[level]
    lines = []
    for first in range(0, pair, 2):
        both = matmul(inverse_y[...], jnp.concatenate(products[first : first + 2], axis=1))
        for k in range(len(products[first : first + 2])):
            line = both[:rows, k * LANES : (k + 1) * LANES]
            if level == 0:
                line = jnp.concatenate([line, both[rows:, k * LANES : (k + 1) * LANES]], axis=1)
            lines.append(line)
    value = matmul(three(jnp.concatenate(lines, axis=0), 1), inverse_z[...])
    layers = [value[out * rows : (out + 1) * rows, :LANES] for out in range(pair)]
    layers += [value[out * rows : (out + 1) * rows, LANES:] for out in range(pair)]
    return layers[: BX[level] + 1]


GRID, MIDDLE, LOW = range(3)


def side(step, size):
    return {-1: (0, REACH), 0: (0, size + 1), 1: (size - HALF, REACH)}[step]


def plan_messages():
    low, fine = [], []
    for dx, layer in ((-2, 0), (2, BX[1])):
        for dy in (-1, 0, 1):
            low.append((dx, dy, LOW if dx < 0 else MIDDLE, (layer, 1), (0, 8), "far"))
    around = [(dx, dy) for dx in (-1, 1) for dy in (0, -1, 1)] + [(0, -1), (0, 1)]
    for dx, dy in around:
        rows = {-1: (0, 8), 0: (0, 16), 1: (8, 8)}[dy]
        low.append((dx, dy, LOW if dx < 0 else MIDDLE, (0, REACH) if dx < 0 else side(dx, BX[1]), rows, "near"))
    for dx, dy in around:
        rows = {-1: (0, 8), 0: (0, CY), 1: (CY - 8, 8)}[dy]
        fine.append((dx, dy, GRID, side(dx, BX[0]), rows, "face"))
        if dy >= 0:
            strip = {-1: (0, 8), 0: (0, CY), 1: (CY - 8, 8)}[dx]
            fine.append((dx, dy, GRID, (CX + 1, 1), strip, "strip"))
    return fine, low


FINE_PLAN, LOW_PLAN = plan_messages()
PLAN = FINE_PLAN + LOW_PLAN


def add_rows(window_ref, layer, first, piece):
    rows = slice(first, first + piece.shape[-2])
    layers = slice(layer, layer + piece.shape[0])
    window_ref[layers, rows, :] = window_ref[layers, rows, :] + piece


def add_level_rows(window_ref, level, layer, dy, piece):
    size = BY[level]
    if dy == 0:
        add_rows(window_ref, layer, 0, piece[:, : size + 1])
    elif dy < 0:
        add_rows(window_ref, layer, size, piece[:, :REACH])
    else:
        base = piece.shape[-2] - 8 if piece.shape[-2] > 8 else (size // 8) * 8
        first = size - HALF - base
        add_rows(window_ref, layer, PERIOD[level] - HALF, piece[:, first : first + HALF])
        add_rows(window_ref, layer, 0, piece[:, first + HALF : first + HALF + 1])


def add_low(windows, message, landed):
    dx, dy, _, (first, count), rows, kind = message
    if kind == "far":
        layer = HALF + (0 if dx < 0 else BX[2]) - dx * BX[2]
        add_level_rows(windows[2], 2, layer, dy, landed[...])
        return
    add_level_rows(windows[1], 1, HALF + first - dx * BX[1], dy, landed[...])
    ride = BX[1] - BX[2] if dx == 0 else 0
    add_level_rows(windows[2], 2, HALF - dx * BX[2], dy, landed[ride : ride + BX[2] + 1, :8, :])


def add_fine(window_ref, message, landed):
    dx, dy, _, (first, count), rows, kind = message
    if kind == "strip":
        low, size = side(dx, BX[0])
        target = CY if dy == 0 else 0
        offset = strip_row(low) - rows[0]
        for k in range(size):
            place = strip_row(low + k) - rows[0]
            layer = HALF + low + k - dx * BX[0]
            window_ref[layer, target : target + 1, :] = (
                window_ref[layer, target : target + 1, :] + landed[0, place : place + 1, :]
            )
        return
    layers = slice(HALF + first - dx * BX[0], HALF + first - dx * BX[0] + count)
    row = lax.broadcasted_iota(jnp.int32, (1, 8, LANES), 1)
    if dy == 0:
        window_ref[layers, :CY, :] = window_ref[layers, :CY, :] + landed[...]
    elif dy < 0:
        at = slice(CY, CY + 8)
        window_ref[layers, at, :] = window_ref[layers, at, :] + jnp.where(row < REACH, landed[...], 0.0)
    else:
        at = slice(PERIOD[0] - 8, PERIOD[0])
        window_ref[layers, at, :] = window_ref[layers, at, :] + jnp.where(row >= 8 - HALF, landed[...], 0.0)


def grid_kernel(sizes, n_tables, *refs):
    count_ref, cell_ref, frac_ref, charge_ref = refs[:4]
    kernels = refs[4:7]
    table_sources = refs[7 : 7 + n_tables]
    out_ref = refs[7 + n_tables]
    scratch = list(refs[8 + n_tables :])

    def take(count):
        taken = scratch[:count]
        del scratch[:count]
        return taken

    grid_ref, middle_ref, low_ref, padded_ref = take(4)
    table_refs = take(n_tables)
    windows, reals, imags, along_z, spectra = take(3), take(3), take(3), take(3), take(3)
    landed = take(len(PLAN))
    send_sem, recv_sem, table_sem = take(3)

    me = (lax.axis_index("gx"), lax.axis_index("gy"))

    def device(dx, dy):
        return (lax.rem(me[0] + dx + sizes[0], sizes[0]), lax.rem(me[1] + dy + sizes[1], sizes[1]))

    barrier = pltpu.get_barrier_semaphore()
    around = sorted({message[:2] for message in PLAN})
    for dx, dy in around:
        pl.semaphore_signal(barrier, inc=1, device_id=device(dx, dy), device_id_type=MESH)
    loads = [
        pltpu.make_async_copy(source, target, table_sem.at[index])
        for index, (source, target) in enumerate(zip(table_sources, table_refs))
    ]
    for load in loads:
        load.start()

    spread(count_ref, cell_ref, frac_ref, charge_ref, grid_ref)
    pl.semaphore_wait(barrier, len(around))

    sources = (grid_ref, middle_ref, low_ref)
    copies = []
    for index, (dx, dy, source, (first, size), (low, rows), _) in enumerate(PLAN):
        copies.append(
            pltpu.make_async_remote_copy(
                src_ref=sources[source].at[pl.ds(first, size), pl.ds(low, rows)],
                dst_ref=landed[index],
                send_sem=send_sem.at[index],
                recv_sem=recv_sem.at[index],
                device_id=device(dx, dy),
                device_id_type=MESH,
            )
        )
    n_fine = len(FINE_PLAN)
    for copy in copies[:n_fine]:
        copy.start()
    for load in loads:
        load.wait()
    down_ref, up_ref, down_z_ref = table_refs[:3]
    restrict(grid_ref, down_ref, down_z_ref, middle_ref, low_ref)
    for copy in copies[n_fine:]:
        copy.start()

    level_tables = [table_refs[3 + 6 * level : 9 + 6 * level] for level in range(LEVELS)]
    for level in (2, 1, 0):
        build_taps(level, kernels[level], padded_ref, *level_tables[level][4:], reals[level], imags[level])

    for level in range(LEVELS):
        windows[level][...] = jnp.zeros_like(windows[level])
    windows[0][HALF : HALF + CX + 1, :CY, :] = grid_ref[: CX + 1]
    for x in range(CX + 1):
        windows[0][HALF + x, CY : CY + 1, :] = grid_ref[CX + 1, strip_row(x) : strip_row(x) + 1, :]
    windows[1][HALF : HALF + BX[1] + 1, : ROWS[1], :] = middle_ref[...]
    windows[2][HALF : HALF + BX[2] + 1, : ROWS[2], :] = low_ref[:, : ROWS[2], :]

    for index, message in enumerate(LOW_PLAN):
        copies[n_fine + index].wait()
        add_low(windows, message, landed[n_fine + index])
    below = []
    for level in (1, 2):
        below += convolve(
            level, windows[level], reals[level], imags[level], level_tables[level][:4], along_z[level], spectra[level]
        )
    high, low = split(jnp.concatenate(below, axis=0))
    both = matmul(up_ref[...], jnp.concatenate([high, low], axis=1))
    out_ref[...] = (both[:, :LANES] + both[:, LANES:]).reshape(out_ref.shape)
    for index, message in enumerate(FINE_PLAN):
        copies[index].wait()
        add_fine(windows[0], message, landed[index])
    layers = convolve(0, windows[0], reals[0], imags[0], level_tables[0][:4], along_z[0], spectra[0])
    for x in range(CX + 1):
        out_ref[x] = out_ref[x] + layers[x][:CY]
        at = slice(strip_row(x), strip_row(x) + 1)
        out_ref[CX + 1, at, :] = out_ref[CX + 1, at, :] + layers[x][CY : CY + 1]


def force_kernel(count_ref, cell_ref, frac_ref, charge_ref, grid_ref, potential_ref, forces_ref):
    slots = cell_ref.shape[-1]
    potential_ref[...] = grid_ref[:CX]
    forces_ref[...] = jnp.zeros_like(forces_ref)
    count = count_ref[0, 0]

    def gather(rows, index):
        return jnp.take_along_axis(rows, index, axis=1)

    def pick(values, base):
        width = CX // 2
        while width >= 1:
            bit = (base & width) != 0
            values = [jnp.where(bit, values[width + k], values[k]) for k in range(width + 1)]
            width //= 2
        return values

    def step(index, carry):
        part = pl.ds(pl.multiple_of(index * LANES, LANES), LANES)
        base_x, base_y, base_z = bases(cell_ref[0, :, part])
        f = [jnp.broadcast_to(frac_ref[k, 0, :, part], (8, LANES)) for k in range(3)]
        slot = index * LANES + lax.broadcasted_iota(jnp.int32, (1, LANES), 1)
        charge = jnp.where(slot < count, charge_ref[0, :, part], 0.0)
        base_x = jnp.broadcast_to(base_x, (8, LANES))
        base_y = jnp.broadcast_to(base_y, (8, LANES))
        z_at = jnp.broadcast_to(base_z, (8, LANES))
        z_next = (z_at + 1) & (NZ - 1)
        row = rows_iota(8, LANES)
        across, along, slope = [jnp.zeros((8, LANES), jnp.float32) for _ in range(3)]

        def corners(lower, upper):
            low, high = [], []
            for at_z, target in ((z_at, low), (z_next, high)):
                target.append(lower(at_z))
                target.append(upper(at_z))
            rise = [high[k] - low[k] for k in range(2)]
            level = [low[k] + f[2] * rise[k] for k in range(2)]
            step_x = level[1] - level[0]
            return step_x, level[0] + f[0] * step_x, rise[0] + f[0] * (rise[1] - rise[0])

        for tile in range(CY // 8):
            found = []
            for at_z in (z_at, z_next):
                values = [gather(grid_ref[x, tile * 8 : tile * 8 + 8, :], at_z) for x in range(CX + 1)]
                found.append(pick(values, base_x))
            step_x, level, rise = corners(
                lambda at_z: found[0][0] if at_z is z_at else found[1][0],
                lambda at_z: found[0][1] if at_z is z_at else found[1][1],
            )
            lower, upper = row + tile * 8 == base_y, row + tile * 8 == base_y + 1
            weight = jnp.where(lower, 1.0 - f[1], jnp.where(upper, f[1], 0.0))
            sign = jnp.where(lower, -1.0, jnp.where(upper, 1.0, 0.0))
            across = across + weight * step_x
            along = along + sign * level
            slope = slope + weight * rise
        lower_x, upper_x = [], []
        for at_z in (z_at, z_next):
            low_sum = jnp.zeros((8, LANES), jnp.float32)
            high_sum = jnp.zeros((8, LANES), jnp.float32)
            for tile in range(3):
                value = gather(grid_ref[CX + 1, tile * 8 : tile * 8 + 8, :], at_z)
                layer = row + (tile * 8 if tile < 2 else 12)
                if tile == 1:
                    layer = jnp.where(layer < 12, layer, -5)
                low_sum = jnp.where(layer == base_x, value, low_sum)
                high_sum = jnp.where(layer == base_x + 1, value, high_sum)
            lower_x.append(low_sum)
            upper_x.append(high_sum)
        edge = base_y == CY - 1
        weight = jnp.where(edge, f[1], 0.0)
        level_low = lower_x[0] + f[2] * (lower_x[1] - lower_x[0])
        level_high = upper_x[0] + f[2] * (upper_x[1] - upper_x[0])
        across = across + weight * (level_high - level_low)
        mixed = (1.0 - f[0]) * level_low + f[0] * level_high
        along = along + jnp.where(edge, mixed, 0.0)
        rise = (1.0 - f[0]) * (lower_x[1] - lower_x[0]) + f[0] * (upper_x[1] - upper_x[0])
        slope = slope + weight * rise
        for k, value in enumerate((across, along, slope)):
            forces_ref[k, 0, :, part] = -charge * jnp.sum(value, axis=0, keepdims=True)
        return carry

    lax.fori_loop(0, jnp.minimum(pl.cdiv(count, LANES), slots // LANES), step, 0)


VMEM = pl.BlockSpec(memory_space=pltpu.VMEM)
SMEM = pl.BlockSpec(memory_space=pltpu.SMEM)
ANY = pl.BlockSpec(memory_space=pl.ANY)


def solution(mesh):
    sizes = (mesh.shape["gx"], mesh.shape["gy"])
    constants = tables()

    def per_device(atom_cell, atom_frac, atom_charge, atom_count, fine_kernel, middle_kernel, coarse_kernel):
        slots = atom_cell.shape[-1]
        f32 = jnp.float32
        grid = (CX + 2, CY, LANES)
        scratch = [
            pltpu.VMEM(grid, f32),
            pltpu.VMEM((BX[1] + 1, ROWS[1], LANES), f32),
            pltpu.VMEM((BX[2] + 1, ROWS[1], LANES), f32),
            pltpu.VMEM((KERNEL, 16, LANES), f32),
        ]
        scratch += [pltpu.VMEM(table.shape, jnp.dtype(table.dtype)) for table in constants]
        scratch += [pltpu.VMEM((WINDOW[k], PERIOD[k], LANES), f32) for k in range(LEVELS)]
        scratch += [pltpu.VMEM((KERNEL, PERIOD[k], LANES), f32) for k in range(LEVELS)] * 2
        scratch += [pltpu.VMEM((WINDOW[k] * PERIOD[k], 2 * LANES), f32) for k in range(LEVELS)]
        scratch += [pltpu.VMEM((SPECTRA[k], 2 * PERIOD[k], LANES), f32) for k in range(LEVELS)]
        scratch += [pltpu.VMEM((message[3][1], message[4][1], LANES), f32) for message in PLAN]
        scratch += [pltpu.SemaphoreType.DMA((len(PLAN),))] * 2 + [pltpu.SemaphoreType.DMA((len(constants),))]
        extended = pl.pallas_call(
            lambda *refs: grid_kernel(sizes, len(constants), *refs),
            out_shape=jax.ShapeDtypeStruct(grid, f32),
            in_specs=[SMEM] + [VMEM] * 6 + [ANY] * len(constants),
            out_specs=VMEM,
            scratch_shapes=scratch,
            compiler_params=pltpu.CompilerParams(collective_id=0, has_side_effects=True),
            name="grid",
        )(
            atom_count,
            atom_cell,
            atom_frac,
            atom_charge,
            fine_kernel,
            middle_kernel,
            coarse_kernel,
            *[jnp.asarray(table) for table in constants],
        )
        potential, forces = pl.pallas_call(
            force_kernel,
            out_shape=(jax.ShapeDtypeStruct((CX, CY, NZ), f32), jax.ShapeDtypeStruct((3, 1, 1, slots), f32)),
            in_specs=[SMEM, VMEM, VMEM, VMEM, VMEM],
            out_specs=(VMEM, VMEM),
            name="forces",
        )(atom_count, atom_cell, atom_frac, atom_charge, extended)
        return potential, forces

    return jax.shard_map(
        per_device,
        mesh=mesh,
        in_specs=(
            P("gx", "gy", None),
            P(None, "gx", "gy", None),
            P("gx", "gy", None),
            P("gx", "gy"),
            P(),
            P(),
            P(),
        ),
        out_specs=(P("gx", "gy", None), P(None, "gx", "gy", None)),
        check_vma=False,
    )
```

```python
import jax
import jax.numpy as jnp
import ml_dtypes
import numpy as np
from jax import lax
from jax.experimental import pallas as pl
from jax.experimental.pallas import tpu as pltpu
from jax.sharding import PartitionSpec as P

CX = 16
CY = 24
NZ = 128
KERNEL = 9
HALF = KERNEL // 2
REACH = HALF + 1
LANES = 128
CHUNK = 512
FORCE_CHUNK = 256
FORCE_UNROLL = 8
LEVELS = 3
MESH = pl.DeviceIdType.MESH

BX = tuple(CX >> k for k in range(LEVELS))
BY = tuple(CY >> k for k in range(LEVELS))
ZS = tuple(NZ >> k for k in range(LEVELS))
PAIR = tuple((size + 2) // 2 for size in BX)
PERIOD = tuple(-(-(size + 1 + 2 * HALF) // 8) * 8 for size in BY)
WINDOW = tuple(2 * size + 2 * HALF for size in PAIR)
SPECTRA = tuple(size + 2 * HALF for size in PAIR)
ROWS = (32, 16, 8)
FIRST_LANE = (0, 0, ZS[1])
GRID_ROWS = (CX + 2) * CY
LOW_ROWS = ((BX[1] + 1) * ROWS[1], (BX[2] + 1) * ROWS[2])


def strip_row(x):
    return x if x < 12 else x + 4


def np_hat(distance):
    return np.maximum(1.0 - np.abs(distance), 0.0)


def np_ring_hat(distance, period):
    distance = np.abs(distance)
    return np.maximum(1.0 - np.minimum(distance, period - distance), 0.0)


def np_split(value):
    high = value.astype(np.float32).astype(ml_dtypes.bfloat16)
    low = (value - high.astype(np.float64)).astype(ml_dtypes.bfloat16)
    return high, low


def fine_places():
    xs, ys = np.full(GRID_ROWS, -1e6), np.full(GRID_ROWS, -1e6)
    for x in range(CX + 1):
        for y in range(CY):
            xs[x * CY + y], ys[x * CY + y] = x, y
        xs[(CX + 1) * CY + strip_row(x)], ys[(CX + 1) * CY + strip_row(x)] = x, CY
    return xs, ys


def transfer_xy():
    xs, ys = fine_places()
    parts = []
    for level in (1, 2):
        scale = 0.5**level
        layers = np.repeat(np.arange(BX[level] + 1), ROWS[level])
        rows = np.tile(np.arange(ROWS[level]), BX[level] + 1)
        weight = np_hat(xs[:, None] * scale - layers[None, :]) * np_hat(ys[:, None] * scale - rows[None, :])
        parts.append(weight * (rows <= BY[level])[None, :])
    return np.concatenate(parts, axis=1)


def transfer_z():
    weight = np.zeros((NZ, LANES))
    for level in (1, 2):
        z, low = np.arange(NZ)[:, None], np.arange(ZS[level])[None, :]
        weight[:, FIRST_LANE[level] : FIRST_LANE[level] + ZS[level]] = np_ring_hat(z * 0.5**level - low, ZS[level])
    return weight


def z_forward(level):
    size = ZS[level]
    angle = 2 * np.pi * np.arange(size)[:, None] * np.arange(size)[None, :] / size
    c, s = np.cos(angle), np.sin(angle)
    table = np.zeros((LANES, 2 * LANES))
    first = FIRST_LANE[level]
    if level == 0:
        table[:, :LANES], table[:, LANES:] = c, -s
    else:
        rows = slice(first, first + size)
        table[rows, :size], table[rows, size : 2 * size] = c, -s
        table[rows, LANES : LANES + size], table[rows, LANES + size : LANES + 2 * size] = -s, -c
    high, low = np_split(table)
    return np.concatenate([high, high, low], axis=0)


def z_inverse(level):
    size = ZS[level]
    angle = 2 * np.pi * np.arange(size)[:, None] * np.arange(size)[None, :] / size
    raised = np_ring_hat(np.arange(NZ)[None, :] * 0.5**level - np.arange(size)[:, None], size)
    c, s = np.cos(angle) @ raised / size, np.sin(angle) @ raised / size
    table = np.concatenate([np.concatenate([c, s], axis=1), np.concatenate([-s, c], axis=1)], axis=0)
    rows = 2 * LANES if level == 0 else LANES
    table = np.concatenate([table, np.zeros((rows - table.shape[0], 2 * LANES))], axis=0)
    high, low = np_split(table)
    return np.concatenate([high, high, low], axis=0)


def y_forward(level):
    size = PERIOD[level]
    angle = 2 * np.pi * np.arange(size)[:, None] * np.arange(size)[None, :] / size
    c, s = np.cos(angle), np.sin(angle)
    high, low = np_split(np.block([[c, s], [-s, c]]))
    return np.concatenate([high, high, low], axis=1)


def y_inverse(level):
    size = PERIOD[level]
    angle = 2 * np.pi * np.arange(ROWS[level])[:, None] * np.arange(size)[None, :] / size
    keep = (np.arange(ROWS[level]) <= BY[level])[:, None]
    c, s = np.cos(angle) * keep / size, np.sin(angle) * keep / size
    table = np.block([[c, -s], [s, c]]) if level == 0 else np.block([[c, -s]])
    if table.shape[0] < 16:
        table = np.concatenate([table, np.zeros((16 - table.shape[0], 2 * size))], axis=0)
    high, low = np_split(table)
    return np.concatenate([high, high, low], axis=1)


def taps_z(level):
    size = ZS[level]
    angle = 2 * np.pi * (np.arange(KERNEL) - HALF)[:, None] * np.arange(size)[None, :] / size
    table = np.zeros((LANES, 2 * LANES))
    for copy in range(1 if level == 0 else 2):
        table[:KERNEL, copy * size : (copy + 1) * size] = np.cos(angle)
        table[:KERNEL, LANES + copy * size : LANES + (copy + 1) * size] = np.sin(angle)
    return table.astype(np.float32)


def taps_y(level):
    size = PERIOD[level]
    angle = 2 * np.pi * np.arange(size)[:, None] * (np.arange(16) - HALF)[None, :] / size
    keep = (np.arange(16) < KERNEL)[None, :]
    c, s = np.cos(angle) * keep, np.sin(angle) * keep
    return np.block([[c, -s], [s, c]]).astype(np.float32)


def tables():
    xy = transfer_xy()
    z = transfer_z()
    bf16 = ml_dtypes.bfloat16
    out = [xy.T.astype(bf16), xy.astype(bf16), np.concatenate([z, z], axis=0).astype(bf16)]
    for level in range(LEVELS):
        out += [z_forward(level), z_inverse(level), y_forward(level), y_inverse(level), taps_z(level), taps_y(level)]
    return out


def split(value):
    high = value.astype(jnp.bfloat16)
    return high, (value - high.astype(jnp.float32)).astype(jnp.bfloat16)


def matmul(a, b):
    return jnp.dot(a, b, preferred_element_type=jnp.float32)


def matmul_nt(a, b):
    return lax.dot_general(a, b, (((1,), (1,)), ((), ())), preferred_element_type=jnp.float32)


def exact(a, b):
    return jnp.dot(a, b, preferred_element_type=jnp.float32, precision=lax.Precision.HIGHEST)


def rows_iota(rows, columns):
    return lax.broadcasted_iota(jnp.int32, (rows, columns), 0)


def bases(cell):
    return cell // (CY * NZ), (cell // NZ) % CY, cell % NZ


def two_rows(row, base, above, f):
    return jnp.where(row == base, 1.0 - f, jnp.where(row == above, f, 0.0))


def spread(count_ref, cell_ref, frac_ref, charge_ref, grid_ref):
    slots = cell_ref.shape[-1]
    grid_ref[...] = jnp.zeros_like(grid_ref)

    def step(index, carry):
        start = pl.multiple_of(index * CHUNK, CHUNK)
        part = pl.ds(start, CHUNK)
        base_x, base_y, base_z = bases(cell_ref[0, :, part])
        f = [frac_ref[k, 0, :, part] for k in range(3)]
        slot = start + lax.broadcasted_iota(jnp.int32, (1, CHUNK), 1)
        charge = jnp.where(slot < count_ref[0, 0], charge_ref[0, :, part], 0.0)
        row = rows_iota(CY, CHUNK)
        weight_x = two_rows(row, base_x, base_x + 1, f[0]) * charge
        weight_y = two_rows(row, base_y, base_y + 1, f[1])
        edge_y = jnp.where(base_y == CY - 1, f[1], 0.0)
        strip = row - jnp.where(row < 12, 0, 4)
        strip = jnp.where((row >= 12) & (row < 16), -1, strip)
        strip_x = two_rows(strip, base_x, base_x + 1, f[0]) * (charge * edge_y)
        top = jnp.concatenate([weight_x[x : x + 1] * weight_y for x in range(CX + 1)] + [strip_x], axis=0)
        row_z = rows_iota(NZ, CHUNK)
        z_side = two_rows(row_z, base_z, lax.rem(base_z + 1, NZ), f[2])
        top_high, top_low = split(top)
        z_high, z_low = split(z_side)
        both = matmul_nt(top_high, jnp.concatenate([z_high, z_low], axis=0))
        term = both[:, :LANES] + both[:, LANES:] + matmul_nt(top_low, z_high)
        grid_ref[...] += term.reshape(grid_ref.shape)
        return carry

    lax.fori_loop(0, slots // CHUNK, step, 0)


def lane_iota():
    return lax.broadcasted_iota(jnp.int32, (1, 1, LANES), 2)


def restrict(grid_ref, down_ref, down_z_ref, middle_ref, low_ref):
    high, low = split(grid_ref[...].reshape(GRID_ROWS, LANES))
    both = matmul(down_ref[...], jnp.concatenate([high, low], axis=1))
    high, low = split(both[:, :LANES] + both[:, LANES:])
    value = matmul(jnp.concatenate([high, low], axis=1), down_z_ref[...])
    middle = value[: LOW_ROWS[0]].reshape(BX[1] + 1, ROWS[1], LANES)
    coarse = value[LOW_ROWS[0] :].reshape(BX[2] + 1, ROWS[2], LANES)
    twice = jnp.concatenate([coarse, coarse], axis=1)
    first = BX[1] - BX[2]
    mine = lane_iota() < FIRST_LANE[2]
    middle_ref[:first] = middle[:first]
    middle_ref[first:] = jnp.where(mine, middle[first:], twice)
    low_ref[...] = jnp.where(mine, middle[: BX[2] + 1], twice)


def build_taps(level, kernel_ref, padded_ref, z_ref, y_ref, real_ref, imag_ref):
    padded_ref[...] = jnp.zeros_like(padded_ref)
    padded_ref[:, :KERNEL, :KERNEL] = kernel_ref[...]
    along_z = exact(padded_ref[...].reshape(KERNEL * 16, LANES), z_ref[...])
    size = PERIOD[level]
    for shift in range(0, KERNEL, 2):
        pieces = []
        for one in range(shift, min(shift + 2, KERNEL)):
            rows = along_z[one * 16 : (one + 1) * 16]
            pieces.append(jnp.concatenate([rows[:, :LANES], rows[:, LANES:]], axis=0))
        both = exact(y_ref[...], jnp.concatenate(pieces, axis=1))
        for k in range(len(pieces)):
            real_ref[shift + k] = both[:size, k * LANES : (k + 1) * LANES]
            imag_ref[shift + k] = both[size:, k * LANES : (k + 1) * LANES]


def three(value, axis):
    high, low = split(value)
    return jnp.concatenate([high, low, high], axis=axis)


def convolve(level, window_ref, real_ref, imag_ref, tables, along_z_ref, spectrum_ref):
    forward_z, inverse_z, forward_y, inverse_y = tables
    size, pair = PERIOD[level], PAIR[level]
    used = BX[level] + 1 + 2 * HALF
    flat = window_ref[:used].reshape(used * size, LANES)
    along_z_ref[: used * size] = matmul(three(flat, 1), forward_z[...])

    def part(layer, which):
        if layer >= used:
            return jnp.zeros((size, LANES), jnp.float32)
        return along_z_ref[layer * size : (layer + 1) * size, which * LANES : (which + 1) * LANES]

    count = SPECTRA[level]
    for first in range(0, count, 2):
        pieces = []
        for layer in range(first, min(first + 2, count)):
            real = part(layer, 0) - part(layer + pair, 1)
            imag = part(layer, 1) + part(layer + pair, 0)
            pieces.append(three(jnp.concatenate([real, imag], axis=0), 0))
        both = matmul(forward_y[...], jnp.concatenate(pieces, axis=1))
        for k in range(len(pieces)):
            spectrum_ref[first + k] = both[:, k * LANES : (k + 1) * LANES]
    products = []
    for out in range(pair):
        reals, imags = [], []
        for tile in range(0, size, 8):
            real = jnp.zeros((8, LANES), jnp.float32)
            imag = jnp.zeros((8, LANES), jnp.float32)
            for shift in range(KERNEL):
                a = spectrum_ref[out + shift, tile : tile + 8]
                b = spectrum_ref[out + shift, size + tile : size + tile + 8]
                c = real_ref[shift, tile : tile + 8]
                s = imag_ref[shift, tile : tile + 8]
                real = real + a * c - b * s
                imag = imag + a * s + b * c
            reals.append(real)
            imags.append(imag)
        products.append(three(jnp.concatenate(reals + imags, axis=0), 0))
    rows = ROWS[level]
    lines = []
    for first in range(0, pair, 2):
        both = matmul(inverse_y[...], jnp.concatenate(products[first : first + 2], axis=1))
        for k in range(len(products[first : first + 2])):
            line = both[:rows, k * LANES : (k + 1) * LANES]
            if level == 0:
                line = jnp.concatenate([line, both[rows:, k * LANES : (k + 1) * LANES]], axis=1)
            lines.append(line)
    value = matmul(three(jnp.concatenate(lines, axis=0), 1), inverse_z[...])
    layers = [value[out * rows : (out + 1) * rows, :LANES] for out in range(pair)]
    layers += [value[out * rows : (out + 1) * rows, LANES:] for out in range(pair)]
    return layers[: BX[level] + 1]


GRID, MIDDLE, LOW = range(3)


def side(step, size):
    return {-1: (0, REACH), 0: (0, size + 1), 1: (size - HALF, REACH)}[step]


def plan_messages():
    low, fine = [], []
    for dx, layer in ((-2, 0), (2, BX[1])):
        for dy in (-1, 0, 1):
            low.append((dx, dy, LOW if dx < 0 else MIDDLE, (layer, 1), (0, 8), "far"))
    around = [(dx, dy) for dx in (-1, 1) for dy in (0, -1, 1)] + [(0, -1), (0, 1)]
    for dx, dy in around:
        rows = {-1: (0, 8), 0: (0, 16), 1: (8, 8)}[dy]
        low.append((dx, dy, LOW if dx < 0 else MIDDLE, (0, REACH) if dx < 0 else side(dx, BX[1]), rows, "near"))
    for dx, dy in around:
        rows = {-1: (0, 8), 0: (0, CY), 1: (CY - 8, 8)}[dy]
        fine.append((dx, dy, GRID, side(dx, BX[0]), rows, "face"))
        if dy >= 0:
            strip = {-1: (0, 8), 0: (0, CY), 1: (CY - 8, 8)}[dx]
            fine.append((dx, dy, GRID, (CX + 1, 1), strip, "strip"))
    return fine, low


FINE_PLAN, LOW_PLAN = plan_messages()
PLAN = FINE_PLAN + LOW_PLAN


def add_rows(window_ref, layer, first, piece):
    rows = slice(first, first + piece.shape[-2])
    layers = slice(layer, layer + piece.shape[0])
    window_ref[layers, rows, :] = window_ref[layers, rows, :] + piece


def add_level_rows(window_ref, level, layer, dy, piece):
    size = BY[level]
    if dy == 0:
        add_rows(window_ref, layer, 0, piece[:, : size + 1])
    elif dy < 0:
        add_rows(window_ref, layer, size, piece[:, :REACH])
    else:
        base = piece.shape[-2] - 8 if piece.shape[-2] > 8 else (size // 8) * 8
        first = size - HALF - base
        add_rows(window_ref, layer, PERIOD[level] - HALF, piece[:, first : first + HALF])
        add_rows(window_ref, layer, 0, piece[:, first + HALF : first + HALF + 1])


def add_low(windows, message, landed):
    dx, dy, _, (first, count), rows, kind = message
    if kind == "far":
        layer = HALF + (0 if dx < 0 else BX[2]) - dx * BX[2]
        add_level_rows(windows[2], 2, layer, dy, landed[...])
        return
    add_level_rows(windows[1], 1, HALF + first - dx * BX[1], dy, landed[...])
    ride = BX[1] - BX[2] if dx == 0 else 0
    add_level_rows(windows[2], 2, HALF - dx * BX[2], dy, landed[ride : ride + BX[2] + 1, :8, :])


def add_fine(window_ref, message, landed):
    dx, dy, _, (first, count), rows, kind = message
    if kind == "strip":
        low, size = side(dx, BX[0])
        target = CY if dy == 0 else 0
        offset = strip_row(low) - rows[0]
        for k in range(size):
            place = strip_row(low + k) - rows[0]
            layer = HALF + low + k - dx * BX[0]
            window_ref[layer, target : target + 1, :] = (
                window_ref[layer, target : target + 1, :] + landed[0, place : place + 1, :]
            )
        return
    layers = slice(HALF + first - dx * BX[0], HALF + first - dx * BX[0] + count)
    row = lax.broadcasted_iota(jnp.int32, (1, 8, LANES), 1)
    if dy == 0:
        window_ref[layers, :CY, :] = window_ref[layers, :CY, :] + landed[...]
    elif dy < 0:
        at = slice(CY, CY + 8)
        window_ref[layers, at, :] = window_ref[layers, at, :] + jnp.where(row < REACH, landed[...], 0.0)
    else:
        at = slice(PERIOD[0] - 8, PERIOD[0])
        window_ref[layers, at, :] = window_ref[layers, at, :] + jnp.where(row >= 8 - HALF, landed[...], 0.0)


def grid_kernel(sizes, n_tables, *refs):
    count_ref, cell_ref, frac_ref, charge_ref = refs[:4]
    kernels = refs[4:7]
    table_sources = refs[7 : 7 + n_tables]
    out_ref = refs[7 + n_tables]
    scratch = list(refs[8 + n_tables :])

    def take(count):
        taken = scratch[:count]
        del scratch[:count]
        return taken

    grid_ref, middle_ref, low_ref, padded_ref = take(4)
    table_refs = take(n_tables)
    windows, reals, imags, along_z, spectra = take(3), take(3), take(3), take(3), take(3)
    landed = take(len(PLAN))
    send_sem, recv_sem, table_sem = take(3)

    me = (lax.axis_index("gx"), lax.axis_index("gy"))

    def device(dx, dy):
        return (lax.rem(me[0] + dx + sizes[0], sizes[0]), lax.rem(me[1] + dy + sizes[1], sizes[1]))

    barrier = pltpu.get_barrier_semaphore()
    around = sorted({message[:2] for message in PLAN})
    for dx, dy in around:
        pl.semaphore_signal(barrier, inc=1, device_id=device(dx, dy), device_id_type=MESH)
    loads = [
        pltpu.make_async_copy(source, target, table_sem.at[index])
        for index, (source, target) in enumerate(zip(table_sources, table_refs))
    ]
    for load in loads:
        load.start()

    spread(count_ref, cell_ref, frac_ref, charge_ref, grid_ref)
    pl.semaphore_wait(barrier, len(around))

    sources = (grid_ref, middle_ref, low_ref)
    copies = []
    for index, (dx, dy, source, (first, size), (low, rows), _) in enumerate(PLAN):
        copies.append(
            pltpu.make_async_remote_copy(
                src_ref=sources[source].at[pl.ds(first, size), pl.ds(low, rows)],
                dst_ref=landed[index],
                send_sem=send_sem.at[index],
                recv_sem=recv_sem.at[index],
                device_id=device(dx, dy),
                device_id_type=MESH,
            )
        )
    n_fine = len(FINE_PLAN)
    for copy in copies[:n_fine]:
        copy.start()
    for load in loads:
        load.wait()
    down_ref, up_ref, down_z_ref = table_refs[:3]
    restrict(grid_ref, down_ref, down_z_ref, middle_ref, low_ref)
    for copy in copies[n_fine:]:
        copy.start()

    level_tables = [table_refs[3 + 6 * level : 9 + 6 * level] for level in range(LEVELS)]
    for level in (2, 1, 0):
        build_taps(level, kernels[level], padded_ref, *level_tables[level][4:], reals[level], imags[level])

    for level in range(LEVELS):
        windows[level][...] = jnp.zeros_like(windows[level])
    windows[0][HALF : HALF + CX + 1, :CY, :] = grid_ref[: CX + 1]
    for x in range(CX + 1):
        windows[0][HALF + x, CY : CY + 1, :] = grid_ref[CX + 1, strip_row(x) : strip_row(x) + 1, :]
    windows[1][HALF : HALF + BX[1] + 1, : ROWS[1], :] = middle_ref[...]
    windows[2][HALF : HALF + BX[2] + 1, : ROWS[2], :] = low_ref[:, : ROWS[2], :]

    for index, message in enumerate(LOW_PLAN):
        copies[n_fine + index].wait()
        add_low(windows, message, landed[n_fine + index])
    below = []
    for level in (1, 2):
        below += convolve(
            level, windows[level], reals[level], imags[level], level_tables[level][:4], along_z[level], spectra[level]
        )
    high, low = split(jnp.concatenate(below, axis=0))
    both = matmul(up_ref[...], jnp.concatenate([high, low], axis=1))
    out_ref[...] = (both[:, :LANES] + both[:, LANES:]).reshape(out_ref.shape)
    for index, message in enumerate(FINE_PLAN):
        copies[index].wait()
        add_fine(windows[0], message, landed[index])
    layers = convolve(0, windows[0], reals[0], imags[0], level_tables[0][:4], along_z[0], spectra[0])
    for x in range(CX + 1):
        out_ref[x] = out_ref[x] + layers[x][:CY]
        at = slice(strip_row(x), strip_row(x) + 1)
        out_ref[CX + 1, at, :] = out_ref[CX + 1, at, :] + layers[x][CY : CY + 1]


def force_kernel(count_ref, cell_ref, frac_ref, charge_ref, grid_ref, potential_ref, forces_ref, left_ref):
    slots = cell_ref.shape[-1]
    potential_ref[...] = grid_ref[:CX]
    forces_ref[...] = jnp.zeros_like(forces_ref)
    count = count_ref[0, 0]
    left_ref[...] = jnp.concatenate(split(grid_ref[...].reshape(GRID_ROWS, LANES)), axis=1)

    def pick(values, base):
        width = CX // 2
        while width >= 1:
            bit = (base & width) != 0
            values = [jnp.where(bit, values[width + k], values[k]) for k in range(width + 1)]
            width //= 2
        return values

    def chunk(index):
        part = pl.ds(pl.multiple_of(index * FORCE_CHUNK, FORCE_CHUNK), FORCE_CHUNK)
        base_x, base_y, base_z = bases(cell_ref[0, :, part])
        row_z = rows_iota(NZ, FORCE_CHUNK)
        found = []
        for at_z in (base_z, (base_z + 1) & (NZ - 1)):
            chosen = jnp.where(row_z == at_z, 1.0, 0.0).astype(jnp.bfloat16)
            found.append(matmul(left_ref[...], jnp.concatenate([chosen, chosen], axis=0)))
        shape = (8, FORCE_CHUNK)
        f = [jnp.broadcast_to(frac_ref[k, 0, :, part], shape) for k in range(3)]
        slot = index * FORCE_CHUNK + lax.broadcasted_iota(jnp.int32, (1, FORCE_CHUNK), 1)
        charge = jnp.where(slot < count, charge_ref[0, :, part], 0.0)
        base_x = jnp.broadcast_to(base_x, shape)
        base_y = jnp.broadcast_to(base_y, shape)
        row = rows_iota(*shape)
        across, along, slope = [jnp.zeros(shape, jnp.float32) for _ in range(3)]
        for tile in range(CY // 8):
            ends = []
            for values in found:
                rows = [values[x * CY + tile * 8 : x * CY + tile * 8 + 8] for x in range(CX + 1)]
                ends.append(pick(rows, base_x))
            rise = [ends[1][k] - ends[0][k] for k in range(2)]
            level = [ends[0][k] + f[2] * rise[k] for k in range(2)]
            step_x = level[1] - level[0]
            lower, upper = row + tile * 8 == base_y, row + tile * 8 == base_y + 1
            weight = jnp.where(lower, 1.0 - f[1], jnp.where(upper, f[1], 0.0))
            sign = jnp.where(lower, -1.0, jnp.where(upper, 1.0, 0.0))
            across = across + weight * step_x
            along = along + sign * (level[0] + f[0] * step_x)
            slope = slope + weight * (rise[0] + f[0] * (rise[1] - rise[0]))
        ends = []
        for values in found:
            low, high = [jnp.zeros(shape, jnp.float32) for _ in range(2)]
            for tile in range(CY // 8):
                value = values[(CX + 1) * CY + tile * 8 : (CX + 1) * CY + tile * 8 + 8]
                layer = row + (tile * 8 if tile < 2 else 12)
                if tile == 1:
                    layer = jnp.where(layer < 12, layer, -5)
                low = jnp.where(layer == base_x, value, low)
                high = jnp.where(layer == base_x + 1, value, high)
            ends.append((low, high))
        edge = base_y == CY - 1
        weight = jnp.where(edge, f[1], 0.0)
        rise = [ends[1][k] - ends[0][k] for k in range(2)]
        level = [ends[0][k] + f[2] * rise[k] for k in range(2)]
        across = across + weight * (level[1] - level[0])
        along = along + jnp.where(edge, level[0] + f[0] * (0.0 - level[0]) + f[0] * level[1], 0.0)
        slope = slope + weight * (rise[0] + f[0] * (0.0 - rise[0]) + f[0] * rise[1])
        for k, value in enumerate((across, along, slope)):
            forces_ref[k, 0, :, part] = -charge * jnp.sum(value, axis=0, keepdims=True)

    def step(index, carry):
        for k in range(FORCE_UNROLL):
            chunk(index * FORCE_UNROLL + k)
        return carry

    width = FORCE_CHUNK * FORCE_UNROLL
    lax.fori_loop(0, jnp.minimum(pl.cdiv(count, width), slots // width), step, 0)


VMEM = pl.BlockSpec(memory_space=pltpu.VMEM)
SMEM = pl.BlockSpec(memory_space=pltpu.SMEM)
ANY = pl.BlockSpec(memory_space=pl.ANY)


def solution(mesh):
    sizes = (mesh.shape["gx"], mesh.shape["gy"])
    constants = tables()

    def per_device(atom_cell, atom_frac, atom_charge, atom_count, fine_kernel, middle_kernel, coarse_kernel):
        slots = atom_cell.shape[-1]
        f32 = jnp.float32
        grid = (CX + 2, CY, LANES)
        scratch = [
            pltpu.VMEM(grid, f32),
            pltpu.VMEM((BX[1] + 1, ROWS[1], LANES), f32),
            pltpu.VMEM((BX[2] + 1, ROWS[1], LANES), f32),
            pltpu.VMEM((KERNEL, 16, LANES), f32),
        ]
        scratch += [pltpu.VMEM(table.shape, jnp.dtype(table.dtype)) for table in constants]
        scratch += [pltpu.VMEM((WINDOW[k], PERIOD[k], LANES), f32) for k in range(LEVELS)]
        scratch += [pltpu.VMEM((KERNEL, PERIOD[k], LANES), f32) for k in range(LEVELS)] * 2
        scratch += [pltpu.VMEM((WINDOW[k] * PERIOD[k], 2 * LANES), f32) for k in range(LEVELS)]
        scratch += [pltpu.VMEM((SPECTRA[k], 2 * PERIOD[k], LANES), f32) for k in range(LEVELS)]
        scratch += [pltpu.VMEM((message[3][1], message[4][1], LANES), f32) for message in PLAN]
        scratch += [pltpu.SemaphoreType.DMA((len(PLAN),))] * 2 + [pltpu.SemaphoreType.DMA((len(constants),))]
        extended = pl.pallas_call(
            lambda *refs: grid_kernel(sizes, len(constants), *refs),
            out_shape=jax.ShapeDtypeStruct(grid, f32),
            in_specs=[SMEM] + [VMEM] * 6 + [ANY] * len(constants),
            out_specs=VMEM,
            scratch_shapes=scratch,
            compiler_params=pltpu.CompilerParams(collective_id=0, has_side_effects=True),
            name="grid",
        )(
            atom_count,
            atom_cell,
            atom_frac,
            atom_charge,
            fine_kernel,
            middle_kernel,
            coarse_kernel,
            *[jnp.asarray(table) for table in constants],
        )
        potential, forces = pl.pallas_call(
            force_kernel,
            out_shape=(jax.ShapeDtypeStruct((CX, CY, NZ), f32), jax.ShapeDtypeStruct((3, 1, 1, slots), f32)),
            in_specs=[SMEM, VMEM, VMEM, VMEM, VMEM],
            out_specs=(VMEM, VMEM),
            scratch_shapes=[pltpu.VMEM((GRID_ROWS, 2 * LANES), jnp.bfloat16)],
            name="forces",
        )(atom_count, atom_cell, atom_frac, atom_charge, extended)
        return potential, forces

    return jax.shard_map(
        per_device,
        mesh=mesh,
        in_specs=(
            P("gx", "gy", None),
            P(None, "gx", "gy", None),
            P("gx", "gy", None),
            P("gx", "gy"),
            P(),
            P(),
            P(),
        ),
        out_specs=(P("gx", "gy", None), P(None, "gx", "gy", None)),
        check_vma=False,
    )
```

```python
import jax
import jax.numpy as jnp
import ml_dtypes
import numpy as np
from jax import lax
from jax.experimental import pallas as pl
from jax.experimental.pallas import tpu as pltpu
from jax.sharding import PartitionSpec as P

CX = 16
CY = 24
NZ = 128
KERNEL = 9
HALF = KERNEL // 2
REACH = HALF + 1
LANES = 128
LAYERS = CX + 1
TOP_ROWS = -(-LAYERS * (CY + 1) // 16) * 16
FORCE_CHUNK = 256
SPREAD_PART = 512
FORCE_UNROLL = 8
LEVELS = 3
MESH = pl.DeviceIdType.MESH

BX = tuple(CX >> k for k in range(LEVELS))
BY = tuple(CY >> k for k in range(LEVELS))
ZS = tuple(NZ >> k for k in range(LEVELS))
PAIR = tuple((size + 2) // 2 for size in BX)
PERIOD = tuple(-(-(size + 1 + 2 * HALF) // 8) * 8 for size in BY)
WINDOW = tuple(2 * size + 2 * HALF for size in PAIR)
SPECTRA = tuple(size + 2 * HALF for size in PAIR)
ROWS = (32, 16, 8)
FIRST_LANE = (0, 0, ZS[1])
GRID_ROWS = (CX + 2) * CY
LOW_ROWS = ((BX[1] + 1) * ROWS[1], (BX[2] + 1) * ROWS[2])


def strip_row(x):
    return x if x < 12 else x + 4


def np_hat(distance):
    return np.maximum(1.0 - np.abs(distance), 0.0)


def np_ring_hat(distance, period):
    distance = np.abs(distance)
    return np.maximum(1.0 - np.minimum(distance, period - distance), 0.0)


def np_split(value):
    high = value.astype(np.float32).astype(ml_dtypes.bfloat16)
    low = (value - high.astype(np.float64)).astype(ml_dtypes.bfloat16)
    return high, low


def fine_places():
    xs, ys = np.full(GRID_ROWS, -1e6), np.full(GRID_ROWS, -1e6)
    for x in range(CX + 1):
        for y in range(CY):
            xs[x * CY + y], ys[x * CY + y] = x, y
        xs[(CX + 1) * CY + strip_row(x)], ys[(CX + 1) * CY + strip_row(x)] = x, CY
    return xs, ys


def transfer_xy():
    xs, ys = fine_places()
    parts = []
    for level in (1, 2):
        scale = 0.5**level
        layers = np.repeat(np.arange(BX[level] + 1), ROWS[level])
        rows = np.tile(np.arange(ROWS[level]), BX[level] + 1)
        weight = np_hat(xs[:, None] * scale - layers[None, :]) * np_hat(ys[:, None] * scale - rows[None, :])
        parts.append(weight * (rows <= BY[level])[None, :])
    return np.concatenate(parts, axis=1)


def transfer_z():
    weight = np.zeros((NZ, LANES))
    for level in (1, 2):
        z, low = np.arange(NZ)[:, None], np.arange(ZS[level])[None, :]
        weight[:, FIRST_LANE[level] : FIRST_LANE[level] + ZS[level]] = np_ring_hat(z * 0.5**level - low, ZS[level])
    return weight


def z_forward(level):
    size = ZS[level]
    angle = 2 * np.pi * np.arange(size)[:, None] * np.arange(size)[None, :] / size
    c, s = np.cos(angle), np.sin(angle)
    table = np.zeros((LANES, 2 * LANES))
    first = FIRST_LANE[level]
    if level == 0:
        table[:, :LANES], table[:, LANES:] = c, -s
    else:
        rows = slice(first, first + size)
        table[rows, :size], table[rows, size : 2 * size] = c, -s
        table[rows, LANES : LANES + size], table[rows, LANES + size : LANES + 2 * size] = -s, -c
    high, low = np_split(table)
    return np.concatenate([high, high, low], axis=0)


def z_inverse(level):
    size = ZS[level]
    angle = 2 * np.pi * np.arange(size)[:, None] * np.arange(size)[None, :] / size
    raised = np_ring_hat(np.arange(NZ)[None, :] * 0.5**level - np.arange(size)[:, None], size)
    c, s = np.cos(angle) @ raised / size, np.sin(angle) @ raised / size
    table = np.concatenate([np.concatenate([c, s], axis=1), np.concatenate([-s, c], axis=1)], axis=0)
    rows = 2 * LANES if level == 0 else LANES
    table = np.concatenate([table, np.zeros((rows - table.shape[0], 2 * LANES))], axis=0)
    high, low = np_split(table)
    return np.concatenate([high, high, low], axis=0)


def y_forward(level):
    size = PERIOD[level]
    angle = 2 * np.pi * np.arange(size)[:, None] * np.arange(size)[None, :] / size
    c, s = np.cos(angle), np.sin(angle)
    high, low = np_split(np.block([[c, s], [-s, c]]))
    return np.concatenate([high, high, low], axis=1)


def y_inverse(level):
    size = PERIOD[level]
    angle = 2 * np.pi * np.arange(ROWS[level])[:, None] * np.arange(size)[None, :] / size
    keep = (np.arange(ROWS[level]) <= BY[level])[:, None]
    c, s = np.cos(angle) * keep / size, np.sin(angle) * keep / size
    table = np.block([[c, -s], [s, c]]) if level == 0 else np.block([[c, -s]])
    if table.shape[0] < 16:
        table = np.concatenate([table, np.zeros((16 - table.shape[0], 2 * size))], axis=0)
    high, low = np_split(table)
    return np.concatenate([high, high, low], axis=1)


def stack_split(table, axis):
    high, low = np_split(table)
    return np.concatenate([high, high, low], axis=axis)


def taps_z(level):
    size = ZS[level]
    angle = 2 * np.pi * (np.arange(KERNEL) - HALF)[:, None] * np.arange(size)[None, :] / size
    table = np.zeros((LANES, 2 * LANES))
    for copy in range(1 if level == 0 else 2):
        table[:KERNEL, copy * size : (copy + 1) * size] = np.cos(angle)
        table[:KERNEL, LANES + copy * size : LANES + (copy + 1) * size] = np.sin(angle)
    return stack_split(table, 0)


def taps_y(level):
    size = PERIOD[level]
    angle = 2 * np.pi * np.arange(size)[:, None] * (np.arange(16) - HALF)[None, :] / size
    keep = (np.arange(16) < KERNEL)[None, :]
    c, s = np.cos(angle) * keep, np.sin(angle) * keep
    return stack_split(np.block([[c, -s], [s, c]]), 1)


def tables():
    xy = transfer_xy()
    z = transfer_z()
    bf16 = ml_dtypes.bfloat16
    out = [xy.T.astype(bf16), xy.astype(bf16), np.concatenate([z, z], axis=0).astype(bf16)]
    for level in range(LEVELS):
        out += [z_forward(level), z_inverse(level), y_forward(level), y_inverse(level), taps_z(level), taps_y(level)]
    return out


def split(value):
    high = value.astype(jnp.bfloat16)
    return high, (value - high.astype(jnp.float32)).astype(jnp.bfloat16)


def matmul(a, b):
    return jnp.dot(a, b, preferred_element_type=jnp.float32)


def matmul_nt(a, b):
    return lax.dot_general(a, b, (((1,), (1,)), ((), ())), preferred_element_type=jnp.float32)


def rows_iota(rows, columns):
    return lax.broadcasted_iota(jnp.int32, (rows, columns), 0)


def bases(cell):
    return cell // (CY * NZ), (cell // NZ) % CY, cell % NZ


def wide(value, dtype):
    return jnp.broadcast_to(value, (16, value.shape[1])).astype(dtype)


def row_patterns(columns):
    row = rows_iota(16, columns)
    patterns = []
    for tile in range(TOP_ROWS // 16):
        xs, ys = [], []
        for part in range(2):
            first = tile * 16 + part * 8
            if first < LAYERS * CY:
                xs.append(first // CY)
                ys.append(row + (first % CY - 8 * part))
            else:
                at = row + (first - LAYERS * CY - 8 * part)
                xs.append(jnp.where(at < LAYERS, at, -9))
                ys.append(jnp.full_like(row, CY))
        if all(isinstance(x, int) for x in xs) and xs[0] == xs[1]:
            x = jnp.full((16, columns), xs[0], jnp.int16)
        else:
            x = jnp.where(row < 8, xs[0], xs[1]).astype(jnp.int16)
        patterns.append((x, jnp.where(row < 8, ys[0], ys[1]).astype(jnp.int16)))
    return patterns


def spread_sides(count_ref, cell_ref, frac_ref, charge_ref, start, patterns, row_z):
    bf16, i16 = jnp.bfloat16, jnp.int16
    part = slice(start, start + SPREAD_PART)
    base_x, base_y, base_z = bases(cell_ref[0, :, part])
    f = [frac_ref[k, 0, :, part] for k in range(3)]
    slot = start + lax.broadcasted_iota(jnp.int32, (1, SPREAD_PART), 1)
    charge = jnp.where(slot < count_ref[0, 0], charge_ref[0, :, part], 0.0)
    nothing = jnp.zeros((16, SPREAD_PART), bf16)
    x_at, x_next = wide(base_x, i16), wide(base_x + 1, i16)
    y_at, y_next = wide(base_y, i16), wide(base_y + 1, i16)
    corner = {}
    for a, along_x in enumerate((charge * (1.0 - f[0]), charge * f[0])):
        for b, along_y in enumerate((1.0 - f[1], f[1])):
            high, low = split(along_x * along_y)
            corner[a, b] = (wide(high, bf16), wide(low, bf16))
    highs, lows = [], []
    known = {}
    for tile, (xs, ys) in enumerate(patterns):
        key = tile % 3 if (tile + 1) * 16 <= LAYERS * CY else tile
        if key not in known:
            here, above = ys == y_at, ys == y_next
            known[key] = [
                [jnp.where(here, corner[a, 0][k], jnp.where(above, corner[a, 1][k], nothing)) for k in range(2)]
                for a in range(2)
            ]
        here, above = xs == x_at, xs == x_next
        for k, target in enumerate((highs, lows)):
            target.append(jnp.where(here, known[key][0][k], jnp.where(above, known[key][1][k], nothing)))
    weights = [[wide(piece, bf16) for piece in split(value)] for value in (1.0 - f[2], f[2])]
    sides = ([], [])
    z_at, z_next = wide(base_z, i16), wide((base_z + 1) & (NZ - 1), i16)
    for rows in row_z:
        here, above = rows == z_at, rows == z_next
        for k in range(2):
            sides[k].append(jnp.where(here, weights[0][k], jnp.where(above, weights[1][k], nothing)))
    return [jnp.concatenate(pieces, axis=0) for pieces in (highs, lows, *sides)]


def spread(count_ref, cell_ref, frac_ref, charge_ref, grid_ref):
    slots = cell_ref.shape[-1]
    patterns = row_patterns(SPREAD_PART)
    row_z = [(rows_iota(16, SPREAD_PART) + first).astype(jnp.int16) for first in range(0, NZ, 16)]
    parts = [
        spread_sides(count_ref, cell_ref, frac_ref, charge_ref, start, patterns, row_z)
        for start in range(0, slots, SPREAD_PART)
    ]
    top_high, top_low, z_high, z_low = [jnp.concatenate(pieces, axis=1) for pieces in zip(*parts)]
    both = matmul_nt(top_high, jnp.concatenate([z_high, z_low], axis=0))
    value = both[:, :LANES] + both[:, LANES:] + matmul_nt(top_low, z_high)
    layers = LAYERS * CY
    grid_ref[:LAYERS] = value[:layers].reshape(LAYERS, CY, LANES)
    grid_ref[LAYERS] = jnp.zeros((CY, LANES), jnp.float32)
    for x in range(LAYERS):
        grid_ref[LAYERS, strip_row(x) : strip_row(x) + 1, :] = value[layers + x : layers + x + 1]


def lane_iota():
    return lax.broadcasted_iota(jnp.int32, (1, 1, LANES), 2)


def restrict(grid_ref, down_ref, down_z_ref, middle_ref, low_ref):
    high, low = split(grid_ref[...].reshape(GRID_ROWS, LANES))
    both = matmul(down_ref[...], jnp.concatenate([high, low], axis=1))
    high, low = split(both[:, :LANES] + both[:, LANES:])
    value = matmul(jnp.concatenate([high, low], axis=1), down_z_ref[...])
    middle = value[: LOW_ROWS[0]].reshape(BX[1] + 1, ROWS[1], LANES)
    coarse = value[LOW_ROWS[0] :].reshape(BX[2] + 1, ROWS[2], LANES)
    twice = jnp.concatenate([coarse, coarse], axis=1)
    first = BX[1] - BX[2]
    mine = lane_iota() < FIRST_LANE[2]
    middle_ref[:first] = middle[:first]
    middle_ref[first:] = jnp.where(mine, middle[first:], twice)
    low_ref[...] = jnp.where(mine, middle[: BX[2] + 1], twice)


def build_taps(level, kernel_ref, padded_ref, z_ref, y_ref, real_ref, imag_ref):
    padded_ref[...] = jnp.zeros_like(padded_ref)
    padded_ref[:, :KERNEL, :KERNEL] = kernel_ref[...]
    along_z = matmul(three(padded_ref[...].reshape(KERNEL * 16, LANES), 1), z_ref[...])
    size = PERIOD[level]
    for shift in range(0, KERNEL, 2):
        pieces = []
        for one in range(shift, min(shift + 2, KERNEL)):
            rows = along_z[one * 16 : (one + 1) * 16]
            pieces.append(three(jnp.concatenate([rows[:, :LANES], rows[:, LANES:]], axis=0), 0))
        both = matmul(y_ref[...], jnp.concatenate(pieces, axis=1))
        for k in range(len(pieces)):
            real_ref[shift + k] = both[:size, k * LANES : (k + 1) * LANES]
            imag_ref[shift + k] = both[size:, k * LANES : (k + 1) * LANES]


def three(value, axis):
    high, low = split(value)
    return jnp.concatenate([high, low, high], axis=axis)


def convolve(level, window_ref, real_ref, imag_ref, tables, along_z_ref, spectrum_ref):
    forward_z, inverse_z, forward_y, inverse_y = tables
    size, pair = PERIOD[level], PAIR[level]
    used = BX[level] + 1 + 2 * HALF
    flat = window_ref[:used].reshape(used * size, LANES)
    half = (used // 2 + 1) * size
    for rows in (slice(0, half), slice(half, used * size)):
        along_z_ref[rows] = matmul(three(flat[rows], 1), forward_z[...])

    def part(layer, which):
        if layer >= used:
            return jnp.zeros((size, LANES), jnp.float32)
        return along_z_ref[layer * size : (layer + 1) * size, which * LANES : (which + 1) * LANES]

    count = SPECTRA[level]
    for first in range(0, count, 2):
        pieces = []
        for layer in range(first, min(first + 2, count)):
            real = part(layer, 0) - part(layer + pair, 1)
            imag = part(layer, 1) + part(layer + pair, 0)
            pieces.append(three(jnp.concatenate([real, imag], axis=0), 0))
        both = matmul(forward_y[...], jnp.concatenate(pieces, axis=1))
        for k in range(len(pieces)):
            spectrum_ref[first + k] = both[:, k * LANES : (k + 1) * LANES]
    products = []
    for out in range(pair):
        reals, imags = [], []
        for tile in range(0, size, 8):
            real = jnp.zeros((8, LANES), jnp.float32)
            imag = jnp.zeros((8, LANES), jnp.float32)
            for shift in range(KERNEL):
                a = spectrum_ref[out + shift, tile : tile + 8]
                b = spectrum_ref[out + shift, size + tile : size + tile + 8]
                c = real_ref[shift, tile : tile + 8]
                s = imag_ref[shift, tile : tile + 8]
                real = real + a * c - b * s
                imag = imag + a * s + b * c
            reals.append(real)
            imags.append(imag)
        products.append(three(jnp.concatenate(reals + imags, axis=0), 0))
    rows = ROWS[level]
    lines = []
    for first in range(0, pair, 2):
        both = matmul(inverse_y[...], jnp.concatenate(products[first : first + 2], axis=1))
        for k in range(len(products[first : first + 2])):
            line = both[:rows, k * LANES : (k + 1) * LANES]
            if level == 0:
                line = jnp.concatenate([line, both[rows:, k * LANES : (k + 1) * LANES]], axis=1)
            lines.append(line)
    half = pair // 2 + 1
    values = []
    for group in (lines[:half], lines[half:]):
        value = matmul(three(jnp.concatenate(group, axis=0), 1), inverse_z[...])
        values += [value[k * rows : (k + 1) * rows] for k in range(len(group))]
    layers = [value[:, :LANES] for value in values] + [value[:, LANES:] for value in values]
    return layers[: BX[level] + 1]


GRID, MIDDLE, LOW, LANDED = range(4)


def side(step, size):
    return {-1: (0, REACH), 0: (0, size + 1), 1: (size - HALF, REACH)}[step]


class Message:
    def __init__(self, kind, dx, dy, source, layers, rows, relayed=None):
        self.kind, self.dx, self.dy = kind, dx, dy
        self.source, self.layers, self.rows, self.relayed = source, layers, rows, relayed
        self.hop = (dx, dy) if relayed is None else (0, dy)
        self.local = (layers, rows)
        if relayed is not None:
            self.local = ((0, layers[1]), (rows[0] - relayed.rows[0], rows[1]))


def plan_messages():
    near, far, face, strip = {}, {}, {}, {}
    top, bottom = (CY - 8, 8), (0, 8)
    for dx, layer in ((-2, 0), (2, BX[1])):
        far[dx, 0] = Message("far", dx, 0, LOW if dx < 0 else MIDDLE, (layer, 1), (0, 8))
    for dx in (-1, 1):
        near[dx, 0] = Message("near", dx, 0, LOW if dx < 0 else MIDDLE, side(dx, BX[1]), (0, ROWS[1]))
        strip[dx, 0] = Message("strip", dx, 0, GRID, (CX + 1, 1), bottom if dx < 0 else top)
        for name, rows in (("top", top), ("bottom", bottom), ("centre", (8, CY - 16))):
            face[dx, name] = Message("face", dx, 0, GRID, side(dx, BX[0]), rows)
    for dy in (-1, 1):
        rows = bottom if dy < 0 else (ROWS[1] - 8, 8)
        near[0, dy] = Message("near", 0, dy, MIDDLE, side(0, BX[1]), rows)
        face[0, dy] = Message("face", 0, dy, GRID, side(0, BX[0]), bottom if dy < 0 else top)
        for dx in (-2, 2):
            far[dx, dy] = Message("far", dx, dy, LANDED, far[dx, 0].layers, (0, 8), far[dx, 0])
        for dx in (-1, 1):
            near[dx, dy] = Message("near", dx, dy, LANDED, near[dx, 0].layers, rows, near[dx, 0])
            first = face[dx, "bottom" if dy < 0 else "top"]
            face[dx, dy] = Message("face", dx, dy, LANDED, first.layers, first.rows, first)
    strip[0, 1] = Message("strip", 0, 1, GRID, (CX + 1, 1), (0, CY))
    for dx in (-1, 1):
        strip[dx, 1] = Message("strip", dx, 1, LANDED, (CX + 1, 1), strip[dx, 0].rows, strip[dx, 0])
    sides = (-1, 1)
    first = [near[dx, 0] for dx in sides]
    first += [face[dx, name] for name in ("top", "bottom") for dx in sides] + [strip[dx, 0] for dx in sides]
    first += [near[0, dy] for dy in sides] + [far[dx, 0] for dx in (-2, 2)]
    first += [face[0, dy] for dy in sides] + [strip[0, 1]] + [face[dx, "centre"] for dx in sides]
    second = [near[dx, dy] for dx in sides for dy in sides] + [far[dx, dy] for dx in (-2, 2) for dy in sides]
    second += [face[dx, dy] for dy in (1, -1) for dx in sides] + [strip[dx, 1] for dx in sides]
    return first, second


FIRST, SECOND = plan_messages()
PLAN = FIRST + SECOND


def add_rows(window_ref, layer, first, piece):
    rows = slice(first, first + piece.shape[-2])
    layers = slice(layer, layer + piece.shape[0])
    window_ref[layers, rows, :] = window_ref[layers, rows, :] + piece


def add_level_rows(window_ref, level, layer, dy, piece):
    size = BY[level]
    if dy == 0:
        add_rows(window_ref, layer, 0, piece[:, : size + 1])
    elif dy < 0:
        add_rows(window_ref, layer, size, piece[:, :REACH])
    else:
        base = piece.shape[-2] - 8 if piece.shape[-2] > 8 else (size // 8) * 8
        first = size - HALF - base
        add_rows(window_ref, layer, PERIOD[level] - HALF, piece[:, first : first + HALF])
        add_rows(window_ref, layer, 0, piece[:, first + HALF : first + HALF + 1])


def add_low(windows, message, landed):
    dx, dy, first = message.dx, message.dy, message.layers[0]
    if message.kind == "far":
        layer = HALF + (0 if dx < 0 else BX[2]) - dx * BX[2]
        add_level_rows(windows[2], 2, layer, dy, landed[...])
        return
    add_level_rows(windows[1], 1, HALF + first - dx * BX[1], dy, landed[...])
    ride = BX[1] - BX[2] if dx == 0 else 0
    add_level_rows(windows[2], 2, HALF - dx * BX[2], dy, landed[ride : ride + BX[2] + 1, :8, :])


def add_fine(window_ref, message, landed):
    dx, dy, rows = message.dx, message.dy, message.rows
    if message.kind == "strip":
        low, size = side(dx, BX[0])
        target = CY if dy == 0 else 0
        for k in range(size):
            place = strip_row(low + k) - rows[0]
            layer = HALF + low + k - dx * BX[0]
            window_ref[layer, target : target + 1, :] = (
                window_ref[layer, target : target + 1, :] + landed[0, place : place + 1, :]
            )
        return
    first, count = message.layers
    layers = slice(HALF + first - dx * BX[0], HALF + first - dx * BX[0] + count)
    row = lax.broadcasted_iota(jnp.int32, (1, 8, LANES), 1)
    value = landed[...]
    at = slice(rows[0], rows[0] + rows[1])
    if dy < 0:
        at, value = slice(CY, CY + 8), jnp.where(row < REACH, value, 0.0)
    elif dy > 0:
        at, value = slice(PERIOD[0] - 8, PERIOD[0]), jnp.where(row >= 8 - HALF, value, 0.0)
    window_ref[layers, at, :] = window_ref[layers, at, :] + value


def grid_kernel(sizes, n_tables, *refs):
    count_ref, cell_ref, frac_ref, charge_ref = refs[:4]
    kernels = refs[4:7]
    table_sources = refs[7 : 7 + n_tables]
    out_ref = refs[7 + n_tables]
    scratch = list(refs[8 + n_tables :])

    def take(count):
        taken = scratch[:count]
        del scratch[:count]
        return taken

    grid_ref, middle_ref, low_ref, padded_ref = take(4)
    table_refs = take(n_tables)
    windows, reals, imags, along_z, spectra = take(3), take(3), take(3), take(3), take(3)
    landed = take(len(PLAN))
    send_sem, recv_sem, table_sem = take(3)

    me = (lax.axis_index("gx"), lax.axis_index("gy"))

    def device(dx, dy):
        return (lax.rem(me[0] + dx + sizes[0], sizes[0]), lax.rem(me[1] + dy + sizes[1], sizes[1]))

    barrier = pltpu.get_barrier_semaphore()
    around = sorted({message.hop for message in PLAN})
    for dx, dy in around:
        pl.semaphore_signal(barrier, inc=1, device_id=device(dx, dy), device_id_type=MESH)
    loads = [
        pltpu.make_async_copy(source, target, table_sem.at[index])
        for index, (source, target) in enumerate(zip(table_sources, table_refs))
    ]
    for load in loads:
        load.start()

    spread(count_ref, cell_ref, frac_ref, charge_ref, grid_ref)
    for load in loads[:3]:
        load.wait()
    down_ref, up_ref, down_z_ref = table_refs[:3]
    restrict(grid_ref, down_ref, down_z_ref, middle_ref, low_ref)
    pl.semaphore_wait(barrier, len(around))

    sources = (grid_ref, middle_ref, low_ref)
    copies = {}
    for index, message in enumerate(PLAN):
        relayed = message.relayed
        source = sources[message.source] if relayed is None else landed[PLAN.index(relayed)]
        (first, size), (low, rows) = message.local
        copies[message] = pltpu.make_async_remote_copy(
            src_ref=source.at[pl.ds(first, size), pl.ds(low, rows)],
            dst_ref=landed[index],
            send_sem=send_sem.at[index],
            recv_sem=recv_sem.at[index],
            device_id=device(*message.hop),
            device_id_type=MESH,
        )
    arrived = set()

    def arrive(message):
        if message not in arrived:
            arrived.add(message)
            copies[message].wait_recv()

    for message in FIRST:
        copies[message].start()
    for load in loads[3:]:
        load.wait()

    level_tables = [table_refs[3 + 6 * level : 9 + 6 * level] for level in range(LEVELS)]
    for level in (2, 1, 0):
        build_taps(level, kernels[level], padded_ref, *level_tables[level][4:], reals[level], imags[level])

    for level in range(LEVELS):
        windows[level][...] = jnp.zeros_like(windows[level])
    windows[0][HALF : HALF + CX + 1, :CY, :] = grid_ref[: CX + 1]
    for x in range(CX + 1):
        windows[0][HALF + x, CY : CY + 1, :] = grid_ref[CX + 1, strip_row(x) : strip_row(x) + 1, :]
    windows[1][HALF : HALF + BX[1] + 1, : ROWS[1], :] = middle_ref[...]
    windows[2][HALF : HALF + BX[2] + 1, : ROWS[2], :] = low_ref[:, : ROWS[2], :]

    for message in FIRST:
        copies[message].wait_send()
    for message in SECOND:
        arrive(message.relayed)
        copies[message].start()
    for message in PLAN:
        if message.kind in ("near", "far"):
            arrive(message)
            add_low(windows, message, landed[PLAN.index(message)])
    below = []
    for level in (1, 2):
        below += convolve(
            level, windows[level], reals[level], imags[level], level_tables[level][:4], along_z[level], spectra[level]
        )
    high, low = split(jnp.concatenate(below, axis=0))
    both = matmul(up_ref[...], jnp.concatenate([high, low], axis=1))
    out_ref[...] = (both[:, :LANES] + both[:, LANES:]).reshape(out_ref.shape)
    for message in PLAN:
        if message.kind in ("face", "strip"):
            arrive(message)
            add_fine(windows[0], message, landed[PLAN.index(message)])
    layers = convolve(0, windows[0], reals[0], imags[0], level_tables[0][:4], along_z[0], spectra[0])
    for x in range(CX + 1):
        out_ref[x] = out_ref[x] + layers[x][:CY]
        at = slice(strip_row(x), strip_row(x) + 1)
        out_ref[CX + 1, at, :] = out_ref[CX + 1, at, :] + layers[x][CY : CY + 1]
    for message in SECOND:
        copies[message].wait_send()


def force_kernel(count_ref, cell_ref, frac_ref, charge_ref, grid_ref, potential_ref, forces_ref, left_ref):
    slots = cell_ref.shape[-1]
    potential_ref[...] = grid_ref[:CX]
    forces_ref[...] = jnp.zeros_like(forces_ref)
    count = count_ref[0, 0]
    left_ref[...] = jnp.concatenate(split(grid_ref[...].reshape(GRID_ROWS, LANES)), axis=1)

    def pick(values, base):
        width = CX // 2
        while width >= 1:
            bit = (base & width) != 0
            values = [jnp.where(bit, values[width + k], values[k]) for k in range(width + 1)]
            width //= 2
        return values

    def chunk(index):
        part = pl.ds(pl.multiple_of(index * FORCE_CHUNK, FORCE_CHUNK), FORCE_CHUNK)
        base_x, base_y, base_z = bases(cell_ref[0, :, part])
        row_z = rows_iota(NZ, FORCE_CHUNK)
        found = []
        for at_z in (base_z, (base_z + 1) & (NZ - 1)):
            chosen = jnp.where(row_z == at_z, 1.0, 0.0).astype(jnp.bfloat16)
            found.append(matmul(left_ref[...], jnp.concatenate([chosen, chosen], axis=0)))
        shape = (8, FORCE_CHUNK)
        f = [jnp.broadcast_to(frac_ref[k, 0, :, part], shape) for k in range(3)]
        slot = index * FORCE_CHUNK + lax.broadcasted_iota(jnp.int32, (1, FORCE_CHUNK), 1)
        charge = jnp.where(slot < count, charge_ref[0, :, part], 0.0)
        base_x = jnp.broadcast_to(base_x, shape)
        base_y = jnp.broadcast_to(base_y, shape)
        row = rows_iota(*shape)
        across, along, slope = [jnp.zeros(shape, jnp.float32) for _ in range(3)]
        for tile in range(CY // 8):
            ends = []
            for values in found:
                rows = [values[x * CY + tile * 8 : x * CY + tile * 8 + 8] for x in range(CX + 1)]
                ends.append(pick(rows, base_x))
            rise = [ends[1][k] - ends[0][k] for k in range(2)]
            level = [ends[0][k] + f[2] * rise[k] for k in range(2)]
            step_x = level[1] - level[0]
            lower, upper = row + tile * 8 == base_y, row + tile * 8 == base_y + 1
            weight = jnp.where(lower, 1.0 - f[1], jnp.where(upper, f[1], 0.0))
            sign = jnp.where(lower, -1.0, jnp.where(upper, 1.0, 0.0))
            across = across + weight * step_x
            along = along + sign * (level[0] + f[0] * step_x)
            slope = slope + weight * (rise[0] + f[0] * (rise[1] - rise[0]))
        ends = []
        for values in found:
            low, high = [jnp.zeros(shape, jnp.float32) for _ in range(2)]
            for tile in range(CY // 8):
                value = values[(CX + 1) * CY + tile * 8 : (CX + 1) * CY + tile * 8 + 8]
                layer = row + (tile * 8 if tile < 2 else 12)
                if tile == 1:
                    layer = jnp.where(layer < 12, layer, -5)
                low = jnp.where(layer == base_x, value, low)
                high = jnp.where(layer == base_x + 1, value, high)
            ends.append((low, high))
        edge = base_y == CY - 1
        weight = jnp.where(edge, f[1], 0.0)
        rise = [ends[1][k] - ends[0][k] for k in range(2)]
        level = [ends[0][k] + f[2] * rise[k] for k in range(2)]
        across = across + weight * (level[1] - level[0])
        along = along + jnp.where(edge, level[0] + f[0] * (0.0 - level[0]) + f[0] * level[1], 0.0)
        slope = slope + weight * (rise[0] + f[0] * (0.0 - rise[0]) + f[0] * rise[1])
        for k, value in enumerate((across, along, slope)):
            forces_ref[k, 0, :, part] = -charge * jnp.sum(value, axis=0, keepdims=True)

    def step(index, carry):
        for k in range(FORCE_UNROLL):
            chunk(index * FORCE_UNROLL + k)
        return carry

    width = FORCE_CHUNK * FORCE_UNROLL
    lax.fori_loop(0, jnp.minimum(pl.cdiv(count, width), slots // width), step, 0)


VMEM = pl.BlockSpec(memory_space=pltpu.VMEM)
SMEM = pl.BlockSpec(memory_space=pltpu.SMEM)
ANY = pl.BlockSpec(memory_space=pl.ANY)


def solution(mesh):
    sizes = (mesh.shape["gx"], mesh.shape["gy"])
    constants = tables()

    def per_device(atom_cell, atom_frac, atom_charge, atom_count, fine_kernel, middle_kernel, coarse_kernel):
        slots = atom_cell.shape[-1]
        f32 = jnp.float32
        grid = (CX + 2, CY, LANES)
        scratch = [
            pltpu.VMEM(grid, f32),
            pltpu.VMEM((BX[1] + 1, ROWS[1], LANES), f32),
            pltpu.VMEM((BX[2] + 1, ROWS[1], LANES), f32),
            pltpu.VMEM((KERNEL, 16, LANES), f32),
        ]
        scratch += [pltpu.VMEM(table.shape, jnp.dtype(table.dtype)) for table in constants]
        scratch += [pltpu.VMEM((WINDOW[k], PERIOD[k], LANES), f32) for k in range(LEVELS)]
        scratch += [pltpu.VMEM((KERNEL, PERIOD[k], LANES), f32) for k in range(LEVELS)] * 2
        scratch += [pltpu.VMEM((WINDOW[k] * PERIOD[k], 2 * LANES), f32) for k in range(LEVELS)]
        scratch += [pltpu.VMEM((SPECTRA[k], 2 * PERIOD[k], LANES), f32) for k in range(LEVELS)]
        scratch += [pltpu.VMEM((message.layers[1], message.rows[1], LANES), f32) for message in PLAN]
        scratch += [pltpu.SemaphoreType.DMA((len(PLAN),))] * 2 + [pltpu.SemaphoreType.DMA((len(constants),))]
        extended = pl.pallas_call(
            lambda *refs: grid_kernel(sizes, len(constants), *refs),
            out_shape=jax.ShapeDtypeStruct(grid, f32),
            in_specs=[SMEM] + [VMEM] * 6 + [ANY] * len(constants),
            out_specs=VMEM,
            scratch_shapes=scratch,
            compiler_params=pltpu.CompilerParams(collective_id=0, has_side_effects=True),
            name="grid",
        )(
            atom_count,
            atom_cell,
            atom_frac,
            atom_charge,
            fine_kernel,
            middle_kernel,
            coarse_kernel,
            *[jnp.asarray(table) for table in constants],
        )
        potential, forces = pl.pallas_call(
            force_kernel,
            out_shape=(jax.ShapeDtypeStruct((CX, CY, NZ), f32), jax.ShapeDtypeStruct((3, 1, 1, slots), f32)),
            in_specs=[SMEM, VMEM, VMEM, VMEM, VMEM],
            out_specs=(VMEM, VMEM),
            scratch_shapes=[pltpu.VMEM((GRID_ROWS, 2 * LANES), jnp.bfloat16)],
            name="forces",
        )(atom_count, atom_cell, atom_frac, atom_charge, extended)
        return potential, forces

    return jax.shard_map(
        per_device,
        mesh=mesh,
        in_specs=(
            P("gx", "gy", None),
            P(None, "gx", "gy", None),
            P("gx", "gy", None),
            P("gx", "gy"),
            P(),
            P(),
            P(),
        ),
        out_specs=(P("gx", "gy", None), P(None, "gx", "gy", None)),
        check_vma=False,
    )
```

```python
import jax
import jax.numpy as jnp
import ml_dtypes
import numpy as np
from jax import lax
from jax.experimental import pallas as pl
from jax.experimental.pallas import tpu as pltpu
from jax.sharding import PartitionSpec as P

CX = 16
CY = 24
NZ = 128
KERNEL = 9
HALF = KERNEL // 2
REACH = HALF + 1
LANES = 128
LAYERS = CX + 1
TOP_ROWS = -(-LAYERS * (CY + 1) // 16) * 16
FORCE_CHUNK = 256
SPREAD_PART = 512
FORCE_UNROLL = 8
LEVELS = 3
MESH = pl.DeviceIdType.MESH

BX = tuple(CX >> k for k in range(LEVELS))
BY = tuple(CY >> k for k in range(LEVELS))
ZS = tuple(NZ >> k for k in range(LEVELS))
PAIR = tuple((size + 2) // 2 for size in BX)
PERIOD = tuple(-(-(size + 1 + 2 * HALF) // 8) * 8 for size in BY)
WINDOW = tuple(2 * size + 2 * HALF for size in PAIR)
SPECTRA = tuple(size + 2 * HALF for size in PAIR)
ROWS = (32, 16, 8)
FIRST_LANE = (0, 0, ZS[1])
GRID_ROWS = (CX + 2) * CY
LOW_ROWS = ((BX[1] + 1) * ROWS[1], (BX[2] + 1) * ROWS[2])


def strip_row(x):
    return x if x < 12 else x + 4


def np_hat(distance):
    return np.maximum(1.0 - np.abs(distance), 0.0)


def np_ring_hat(distance, period):
    distance = np.abs(distance)
    return np.maximum(1.0 - np.minimum(distance, period - distance), 0.0)


def np_split(value):
    high = value.astype(np.float32).astype(ml_dtypes.bfloat16)
    low = (value - high.astype(np.float64)).astype(ml_dtypes.bfloat16)
    return high, low


def fine_places():
    xs, ys = np.full(GRID_ROWS, -1e6), np.full(GRID_ROWS, -1e6)
    for x in range(CX + 1):
        for y in range(CY):
            xs[x * CY + y], ys[x * CY + y] = x, y
        xs[(CX + 1) * CY + strip_row(x)], ys[(CX + 1) * CY + strip_row(x)] = x, CY
    return xs, ys


def transfer_xy():
    xs, ys = fine_places()
    parts = []
    for level in (1, 2):
        scale = 0.5**level
        layers = np.repeat(np.arange(BX[level] + 1), ROWS[level])
        rows = np.tile(np.arange(ROWS[level]), BX[level] + 1)
        weight = np_hat(xs[:, None] * scale - layers[None, :]) * np_hat(ys[:, None] * scale - rows[None, :])
        parts.append(weight * (rows <= BY[level])[None, :])
    return np.concatenate(parts, axis=1)


def transfer_z():
    weight = np.zeros((NZ, LANES))
    for level in (1, 2):
        z, low = np.arange(NZ)[:, None], np.arange(ZS[level])[None, :]
        weight[:, FIRST_LANE[level] : FIRST_LANE[level] + ZS[level]] = np_ring_hat(z * 0.5**level - low, ZS[level])
    return weight


def z_forward(level):
    size = ZS[level]
    angle = 2 * np.pi * np.arange(size)[:, None] * np.arange(size)[None, :] / size
    c, s = np.cos(angle), np.sin(angle)
    table = np.zeros((LANES, 2 * LANES))
    first = FIRST_LANE[level]
    if level == 0:
        table[:, :LANES], table[:, LANES:] = c, -s
    else:
        rows = slice(first, first + size)
        table[rows, :size], table[rows, size : 2 * size] = c, -s
        table[rows, LANES : LANES + size], table[rows, LANES + size : LANES + 2 * size] = -s, -c
    high, low = np_split(table)
    return np.concatenate([high, high, low], axis=0)


def z_inverse(level):
    size = ZS[level]
    angle = 2 * np.pi * np.arange(size)[:, None] * np.arange(size)[None, :] / size
    raised = np_ring_hat(np.arange(NZ)[None, :] * 0.5**level - np.arange(size)[:, None], size)
    c, s = np.cos(angle) @ raised / size, np.sin(angle) @ raised / size
    table = np.concatenate([np.concatenate([c, s], axis=1), np.concatenate([-s, c], axis=1)], axis=0)
    rows = 2 * LANES if level == 0 else LANES
    table = np.concatenate([table, np.zeros((rows - table.shape[0], 2 * LANES))], axis=0)
    high, low = np_split(table)
    return np.concatenate([high, high, low], axis=0)


def y_forward(level):
    size = PERIOD[level]
    angle = 2 * np.pi * np.arange(size)[:, None] * np.arange(size)[None, :] / size
    c, s = np.cos(angle), np.sin(angle)
    high, low = np_split(np.block([[c, s], [-s, c]]))
    return np.concatenate([high, high, low], axis=1)


def y_inverse(level):
    size = PERIOD[level]
    angle = 2 * np.pi * np.arange(ROWS[level])[:, None] * np.arange(size)[None, :] / size
    keep = (np.arange(ROWS[level]) <= BY[level])[:, None]
    c, s = np.cos(angle) * keep / size, np.sin(angle) * keep / size
    table = np.block([[c, -s], [s, c]]) if level == 0 else np.block([[c, -s]])
    if table.shape[0] < 16:
        table = np.concatenate([table, np.zeros((16 - table.shape[0], 2 * size))], axis=0)
    high, low = np_split(table)
    return np.concatenate([high, high, low], axis=1)


def stack_split(table, axis):
    high, low = np_split(table)
    return np.concatenate([high, high, low], axis=axis)


def taps_z(level):
    size = ZS[level]
    angle = 2 * np.pi * (np.arange(KERNEL) - HALF)[:, None] * np.arange(size)[None, :] / size
    table = np.zeros((LANES, 2 * LANES))
    for copy in range(1 if level == 0 else 2):
        table[:KERNEL, copy * size : (copy + 1) * size] = np.cos(angle)
        table[:KERNEL, LANES + copy * size : LANES + (copy + 1) * size] = np.sin(angle)
    return stack_split(table, 0)


def taps_y(level):
    size = PERIOD[level]
    angle = 2 * np.pi * np.arange(size)[:, None] * (np.arange(16) - HALF)[None, :] / size
    keep = (np.arange(16) < KERNEL)[None, :]
    c, s = np.cos(angle) * keep, np.sin(angle) * keep
    return stack_split(np.block([[c, -s], [s, c]]), 1)


def tables():
    xy = transfer_xy()
    z = transfer_z()
    bf16 = ml_dtypes.bfloat16
    out = [xy.T.astype(bf16), xy.astype(bf16), np.concatenate([z, z], axis=0).astype(bf16)]
    for level in range(LEVELS):
        out += [z_forward(level), z_inverse(level), y_forward(level), y_inverse(level), taps_z(level), taps_y(level)]
    return out


def split(value):
    high = value.astype(jnp.bfloat16)
    return high, (value - high.astype(jnp.float32)).astype(jnp.bfloat16)


def matmul(a, b):
    return jnp.dot(a, b, preferred_element_type=jnp.float32)


def matmul_nt(a, b):
    return lax.dot_general(a, b, (((1,), (1,)), ((), ())), preferred_element_type=jnp.float32)


def rows_iota(rows, columns):
    return lax.broadcasted_iota(jnp.int32, (rows, columns), 0)


def bases(cell):
    return cell // (CY * NZ), (cell // NZ) % CY, cell % NZ


def wide(value, dtype):
    return jnp.broadcast_to(value, (16, value.shape[1])).astype(dtype)


def row_patterns(columns):
    row = rows_iota(16, columns)
    patterns = []
    for tile in range(TOP_ROWS // 16):
        xs, ys = [], []
        for part in range(2):
            first = tile * 16 + part * 8
            if first < LAYERS * CY:
                xs.append(first // CY)
                ys.append(row + (first % CY - 8 * part))
            else:
                at = row + (first - LAYERS * CY - 8 * part)
                xs.append(jnp.where(at < LAYERS, at, -9))
                ys.append(jnp.full_like(row, CY))
        if all(isinstance(x, int) for x in xs) and xs[0] == xs[1]:
            x = jnp.full((16, columns), xs[0], jnp.int16)
        else:
            x = jnp.where(row < 8, xs[0], xs[1]).astype(jnp.int16)
        patterns.append((x, jnp.where(row < 8, ys[0], ys[1]).astype(jnp.int16)))
    return patterns


def spread_sides(count_ref, cell_ref, frac_ref, charge_ref, start, patterns, row_z):
    bf16, i16 = jnp.bfloat16, jnp.int16
    part = slice(start, start + SPREAD_PART)
    base_x, base_y, base_z = bases(cell_ref[0, :, part])
    f = [frac_ref[k, 0, :, part] for k in range(3)]
    slot = start + lax.broadcasted_iota(jnp.int32, (1, SPREAD_PART), 1)
    charge = jnp.where(slot < count_ref[...], charge_ref[0, :, part], 0.0)
    nothing = jnp.zeros((16, SPREAD_PART), bf16)
    x_at, x_next = wide(base_x, i16), wide(base_x + 1, i16)
    y_at, y_next = wide(base_y, i16), wide(base_y + 1, i16)
    corner = {}
    for a, along_x in enumerate((charge * (1.0 - f[0]), charge * f[0])):
        for b, along_y in enumerate((1.0 - f[1], f[1])):
            high, low = split(along_x * along_y)
            corner[a, b] = (wide(high, bf16), wide(low, bf16))
    highs, lows = [], []
    known = {}
    for tile, (xs, ys) in enumerate(patterns):
        key = tile % 3 if (tile + 1) * 16 <= LAYERS * CY else tile
        if key not in known:
            here, above = ys == y_at, ys == y_next
            known[key] = [
                [jnp.where(here, corner[a, 0][k], jnp.where(above, corner[a, 1][k], nothing)) for k in range(2)]
                for a in range(2)
            ]
        here, above = xs == x_at, xs == x_next
        for k, target in enumerate((highs, lows)):
            target.append(jnp.where(here, known[key][0][k], jnp.where(above, known[key][1][k], nothing)))
    weights = [[wide(piece, bf16) for piece in split(value)] for value in (1.0 - f[2], f[2])]
    sides = ([], [])
    z_at, z_next = wide(base_z, i16), wide((base_z + 1) & (NZ - 1), i16)
    for rows in row_z:
        here, above = rows == z_at, rows == z_next
        for k in range(2):
            sides[k].append(jnp.where(here, weights[0][k], jnp.where(above, weights[1][k], nothing)))
    return [jnp.concatenate(pieces, axis=0) for pieces in (highs, lows, *sides)]


def spread(count_ref, cell_ref, frac_ref, charge_ref, grid_ref):
    slots = cell_ref.shape[-1]
    patterns = row_patterns(SPREAD_PART)
    row_z = [(rows_iota(16, SPREAD_PART) + first).astype(jnp.int16) for first in range(0, NZ, 16)]
    parts = [
        spread_sides(count_ref, cell_ref, frac_ref, charge_ref, start, patterns, row_z)
        for start in range(0, slots, SPREAD_PART)
    ]
    top_high, top_low, z_high, z_low = [jnp.concatenate(pieces, axis=1) for pieces in zip(*parts)]
    both = matmul_nt(top_high, jnp.concatenate([z_high, z_low], axis=0))
    value = both[:, :LANES] + both[:, LANES:] + matmul_nt(top_low, z_high)
    layers = LAYERS * CY
    grid_ref[:LAYERS] = value[:layers].reshape(LAYERS, CY, LANES)
    grid_ref[LAYERS] = jnp.zeros((CY, LANES), jnp.float32)
    for x in range(LAYERS):
        grid_ref[LAYERS, strip_row(x) : strip_row(x) + 1, :] = value[layers + x : layers + x + 1]


def lane_iota():
    return lax.broadcasted_iota(jnp.int32, (1, 1, LANES), 2)


def restrict(grid_ref, down_ref, down_z_ref, middle_ref, low_ref):
    high, low = split(grid_ref[...].reshape(GRID_ROWS, LANES))
    both = matmul(down_ref[...], jnp.concatenate([high, low], axis=1))
    high, low = split(both[:, :LANES] + both[:, LANES:])
    value = matmul(jnp.concatenate([high, low], axis=1), down_z_ref[...])
    middle = value[: LOW_ROWS[0]].reshape(BX[1] + 1, ROWS[1], LANES)
    coarse = value[LOW_ROWS[0] :].reshape(BX[2] + 1, ROWS[2], LANES)
    twice = jnp.concatenate([coarse, coarse], axis=1)
    first = BX[1] - BX[2]
    mine = lane_iota() < FIRST_LANE[2]
    middle_ref[:first] = middle[:first]
    middle_ref[first:] = jnp.where(mine, middle[first:], twice)
    low_ref[...] = jnp.where(mine, middle[: BX[2] + 1], twice)


def build_taps(level, kernel_ref, padded_ref, z_ref, y_ref, real_ref, imag_ref):
    padded_ref[...] = jnp.zeros_like(padded_ref)
    padded_ref[:, :KERNEL, :KERNEL] = kernel_ref[...]
    along_z = matmul(three(padded_ref[...].reshape(KERNEL * 16, LANES), 1), z_ref[...])
    size = PERIOD[level]
    for shift in range(0, KERNEL, 2):
        pieces = []
        for one in range(shift, min(shift + 2, KERNEL)):
            rows = along_z[one * 16 : (one + 1) * 16]
            pieces.append(three(jnp.concatenate([rows[:, :LANES], rows[:, LANES:]], axis=0), 0))
        both = matmul(y_ref[...], jnp.concatenate(pieces, axis=1))
        for k in range(len(pieces)):
            real_ref[shift + k] = both[:size, k * LANES : (k + 1) * LANES]
            imag_ref[shift + k] = both[size:, k * LANES : (k + 1) * LANES]


def three(value, axis):
    high, low = split(value)
    return jnp.concatenate([high, low, high], axis=axis)


def convolve(level, window_ref, real_ref, imag_ref, tables, along_z_ref, spectrum_ref):
    forward_z, inverse_z, forward_y, inverse_y = tables
    size, pair = PERIOD[level], PAIR[level]
    used = BX[level] + 1 + 2 * HALF
    flat = window_ref[:used].reshape(used * size, LANES)
    half = (used // 2 + 1) * size
    for rows in (slice(0, half), slice(half, used * size)):
        along_z_ref[rows] = matmul(three(flat[rows], 1), forward_z[...])

    def part(layer, which):
        if layer >= used:
            return jnp.zeros((size, LANES), jnp.float32)
        return along_z_ref[layer * size : (layer + 1) * size, which * LANES : (which + 1) * LANES]

    count = SPECTRA[level]
    for first in range(0, count, 2):
        pieces = []
        for layer in range(first, min(first + 2, count)):
            real = part(layer, 0) - part(layer + pair, 1)
            imag = part(layer, 1) + part(layer + pair, 0)
            pieces.append(three(jnp.concatenate([real, imag], axis=0), 0))
        both = matmul(forward_y[...], jnp.concatenate(pieces, axis=1))
        for k in range(len(pieces)):
            spectrum_ref[first + k] = both[:, k * LANES : (k + 1) * LANES]
    products = []
    for out in range(pair):
        reals, imags = [], []
        for tile in range(0, size, 8):
            real = jnp.zeros((8, LANES), jnp.float32)
            imag = jnp.zeros((8, LANES), jnp.float32)
            for shift in range(KERNEL):
                a = spectrum_ref[out + shift, tile : tile + 8]
                b = spectrum_ref[out + shift, size + tile : size + tile + 8]
                c = real_ref[shift, tile : tile + 8]
                s = imag_ref[shift, tile : tile + 8]
                real = real + a * c - b * s
                imag = imag + a * s + b * c
            reals.append(real)
            imags.append(imag)
        products.append(three(jnp.concatenate(reals + imags, axis=0), 0))
    rows = ROWS[level]
    lines = []
    for first in range(0, pair, 2):
        both = matmul(inverse_y[...], jnp.concatenate(products[first : first + 2], axis=1))
        for k in range(len(products[first : first + 2])):
            line = both[:rows, k * LANES : (k + 1) * LANES]
            if level == 0:
                line = jnp.concatenate([line, both[rows:, k * LANES : (k + 1) * LANES]], axis=1)
            lines.append(line)
    half = pair // 2 + 1
    values = []
    for group in (lines[:half], lines[half:]):
        value = matmul(three(jnp.concatenate(group, axis=0), 1), inverse_z[...])
        values += [value[k * rows : (k + 1) * rows] for k in range(len(group))]
    layers = [value[:, :LANES] for value in values] + [value[:, LANES:] for value in values]
    return layers[: BX[level] + 1]


GRID, MIDDLE, LOW, LANDED = range(4)


def side(step, size):
    return {-1: (0, REACH), 0: (0, size + 1), 1: (size - HALF, REACH)}[step]


class Message:
    def __init__(self, kind, dx, dy, source, layers, rows, relayed=None):
        self.kind, self.dx, self.dy = kind, dx, dy
        self.source, self.layers, self.rows, self.relayed = source, layers, rows, relayed
        self.hop = (dx, dy) if relayed is None else (0, dy)
        self.local = (layers, rows)
        if relayed is not None:
            self.local = ((0, layers[1]), (rows[0] - relayed.rows[0], rows[1]))


def plan_messages():
    near, far, face, strip = {}, {}, {}, {}
    top, bottom = (CY - 8, 8), (0, 8)
    for dx, layer in ((-2, 0), (2, BX[1])):
        far[dx, 0] = Message("far", dx, 0, LOW if dx < 0 else MIDDLE, (layer, 1), (0, 8))
    for dx in (-1, 1):
        near[dx, 0] = Message("near", dx, 0, LOW if dx < 0 else MIDDLE, side(dx, BX[1]), (0, ROWS[1]))
        strip[dx, 0] = Message("strip", dx, 0, GRID, (CX + 1, 1), bottom if dx < 0 else top)
        for name, rows in (("top", top), ("bottom", bottom), ("centre", (8, CY - 16))):
            face[dx, name] = Message("face", dx, 0, GRID, side(dx, BX[0]), rows)
    for dy in (-1, 1):
        rows = bottom if dy < 0 else (ROWS[1] - 8, 8)
        near[0, dy] = Message("near", 0, dy, MIDDLE, side(0, BX[1]), rows)
        face[0, dy] = Message("face", 0, dy, GRID, side(0, BX[0]), bottom if dy < 0 else top)
        for dx in (-2, 2):
            far[dx, dy] = Message("far", dx, dy, LANDED, far[dx, 0].layers, (0, 8), far[dx, 0])
        for dx in (-1, 1):
            near[dx, dy] = Message("near", dx, dy, LANDED, near[dx, 0].layers, rows, near[dx, 0])
            first = face[dx, "bottom" if dy < 0 else "top"]
            face[dx, dy] = Message("face", dx, dy, LANDED, first.layers, first.rows, first)
    strip[0, 1] = Message("strip", 0, 1, GRID, (CX + 1, 1), (0, CY))
    for dx in (-1, 1):
        strip[dx, 1] = Message("strip", dx, 1, LANDED, (CX + 1, 1), strip[dx, 0].rows, strip[dx, 0])
    sides = (-1, 1)
    first = [near[dx, 0] for dx in sides]
    first += [face[dx, name] for name in ("top", "bottom") for dx in sides] + [strip[dx, 0] for dx in sides]
    first += [near[0, dy] for dy in sides] + [far[dx, 0] for dx in (-2, 2)]
    first += [face[0, dy] for dy in sides] + [strip[0, 1]] + [face[dx, "centre"] for dx in sides]
    second = [near[dx, dy] for dx in sides for dy in sides] + [far[dx, dy] for dx in (-2, 2) for dy in sides]
    second += [face[dx, dy] for dy in (1, -1) for dx in sides] + [strip[dx, 1] for dx in sides]
    return first, second


FIRST, SECOND = plan_messages()
PLAN = FIRST + SECOND


def add_rows(window_ref, layer, first, piece):
    rows = slice(first, first + piece.shape[-2])
    layers = slice(layer, layer + piece.shape[0])
    window_ref[layers, rows, :] = window_ref[layers, rows, :] + piece


def add_level_rows(window_ref, level, layer, dy, piece):
    size = BY[level]
    if dy == 0:
        add_rows(window_ref, layer, 0, piece[:, : size + 1])
    elif dy < 0:
        add_rows(window_ref, layer, size, piece[:, :REACH])
    else:
        base = piece.shape[-2] - 8 if piece.shape[-2] > 8 else (size // 8) * 8
        first = size - HALF - base
        add_rows(window_ref, layer, PERIOD[level] - HALF, piece[:, first : first + HALF])
        add_rows(window_ref, layer, 0, piece[:, first + HALF : first + HALF + 1])


def add_low(windows, message, landed):
    dx, dy, first = message.dx, message.dy, message.layers[0]
    if message.kind == "far":
        layer = HALF + (0 if dx < 0 else BX[2]) - dx * BX[2]
        add_level_rows(windows[2], 2, layer, dy, landed[...])
        return
    add_level_rows(windows[1], 1, HALF + first - dx * BX[1], dy, landed[...])
    ride = BX[1] - BX[2] if dx == 0 else 0
    add_level_rows(windows[2], 2, HALF - dx * BX[2], dy, landed[ride : ride + BX[2] + 1, :8, :])


def add_fine(window_ref, message, landed):
    dx, dy, rows = message.dx, message.dy, message.rows
    if message.kind == "strip":
        low, size = side(dx, BX[0])
        target = CY if dy == 0 else 0
        for k in range(size):
            place = strip_row(low + k) - rows[0]
            layer = HALF + low + k - dx * BX[0]
            window_ref[layer, target : target + 1, :] = (
                window_ref[layer, target : target + 1, :] + landed[0, place : place + 1, :]
            )
        return
    first, count = message.layers
    layers = slice(HALF + first - dx * BX[0], HALF + first - dx * BX[0] + count)
    row = lax.broadcasted_iota(jnp.int32, (1, 8, LANES), 1)
    value = landed[...]
    at = slice(rows[0], rows[0] + rows[1])
    if dy < 0:
        at, value = slice(CY, CY + 8), jnp.where(row < REACH, value, 0.0)
    elif dy > 0:
        at, value = slice(PERIOD[0] - 8, PERIOD[0]), jnp.where(row >= 8 - HALF, value, 0.0)
    window_ref[layers, at, :] = window_ref[layers, at, :] + value


def grid_kernel(sizes, n_tables, *refs):
    count_ref, cell_ref, frac_ref, charge_ref = refs[:4]
    kernels = refs[4:7]
    table_sources = refs[7 : 7 + n_tables]
    out_ref = refs[7 + n_tables]
    scratch = list(refs[8 + n_tables :])

    def take(count):
        taken = scratch[:count]
        del scratch[:count]
        return taken

    grid_ref, middle_ref, low_ref, padded_ref = take(4)
    table_refs = take(n_tables)
    windows, reals, imags, along_z, spectra = take(3), take(3), take(3), take(3), take(3)
    landed = take(len(PLAN))
    send_sem, recv_sem, table_sem = take(3)

    me = (lax.axis_index("gx"), lax.axis_index("gy"))

    def device(dx, dy):
        return (lax.rem(me[0] + dx + sizes[0], sizes[0]), lax.rem(me[1] + dy + sizes[1], sizes[1]))

    barrier = pltpu.get_barrier_semaphore()
    around = sorted({message.hop for message in PLAN})
    for dx, dy in around:
        pl.semaphore_signal(barrier, inc=1, device_id=device(dx, dy), device_id_type=MESH)
    loads = [
        pltpu.make_async_copy(source, target, table_sem.at[index])
        for index, (source, target) in enumerate(zip(table_sources, table_refs))
    ]
    for load in loads:
        load.start()

    spread(count_ref, cell_ref, frac_ref, charge_ref, grid_ref)
    for load in loads[:3]:
        load.wait()
    down_ref, up_ref, down_z_ref = table_refs[:3]
    restrict(grid_ref, down_ref, down_z_ref, middle_ref, low_ref)
    pl.semaphore_wait(barrier, len(around))

    sources = (grid_ref, middle_ref, low_ref)
    copies = {}
    for index, message in enumerate(PLAN):
        relayed = message.relayed
        source = sources[message.source] if relayed is None else landed[PLAN.index(relayed)]
        (first, size), (low, rows) = message.local
        copies[message] = pltpu.make_async_remote_copy(
            src_ref=source.at[pl.ds(first, size), pl.ds(low, rows)],
            dst_ref=landed[index],
            send_sem=send_sem.at[index],
            recv_sem=recv_sem.at[index],
            device_id=device(*message.hop),
            device_id_type=MESH,
        )
    arrived = set()

    def arrive(message):
        if message not in arrived:
            arrived.add(message)
            copies[message].wait_recv()

    for message in FIRST:
        copies[message].start()
    for load in loads[3:]:
        load.wait()

    level_tables = [table_refs[3 + 6 * level : 9 + 6 * level] for level in range(LEVELS)]
    for level in (2, 1, 0):
        build_taps(level, kernels[level], padded_ref, *level_tables[level][4:], reals[level], imags[level])

    for level in range(LEVELS):
        windows[level][...] = jnp.zeros_like(windows[level])
    windows[0][HALF : HALF + CX + 1, :CY, :] = grid_ref[: CX + 1]
    for x in range(CX + 1):
        windows[0][HALF + x, CY : CY + 1, :] = grid_ref[CX + 1, strip_row(x) : strip_row(x) + 1, :]
    windows[1][HALF : HALF + BX[1] + 1, : ROWS[1], :] = middle_ref[...]
    windows[2][HALF : HALF + BX[2] + 1, : ROWS[2], :] = low_ref[:, : ROWS[2], :]

    for message in SECOND:
        arrive(message.relayed)
        copies[message].start()
    for message in FIRST:
        copies[message].wait_send()
    for message in PLAN:
        if message.kind in ("near", "far"):
            arrive(message)
            add_low(windows, message, landed[PLAN.index(message)])
    below = []
    for level in (1, 2):
        below += convolve(
            level, windows[level], reals[level], imags[level], level_tables[level][:4], along_z[level], spectra[level]
        )
    high, low = split(jnp.concatenate(below, axis=0))
    both = matmul(up_ref[...], jnp.concatenate([high, low], axis=1))
    out_ref[...] = (both[:, :LANES] + both[:, LANES:]).reshape(out_ref.shape)
    for message in PLAN:
        if message.kind in ("face", "strip"):
            arrive(message)
            add_fine(windows[0], message, landed[PLAN.index(message)])
    layers = convolve(0, windows[0], reals[0], imags[0], level_tables[0][:4], along_z[0], spectra[0])
    for x in range(CX + 1):
        out_ref[x] = out_ref[x] + layers[x][:CY]
        at = slice(strip_row(x), strip_row(x) + 1)
        out_ref[CX + 1, at, :] = out_ref[CX + 1, at, :] + layers[x][CY : CY + 1]
    for message in SECOND:
        copies[message].wait_send()


def force_kernel(count_ref, cell_ref, frac_ref, charge_ref, grid_ref, potential_ref, forces_ref, left_ref):
    slots = cell_ref.shape[-1]
    potential_ref[...] = grid_ref[:CX]
    forces_ref[...] = jnp.zeros_like(forces_ref)
    left_ref[...] = jnp.concatenate(split(grid_ref[...].reshape(GRID_ROWS, LANES)), axis=1)
    count = jnp.max(count_ref[...].astype(jnp.float32)).astype(jnp.int32)

    def pick(values, base):
        width = CX // 2
        while width >= 1:
            bit = (base & width) != 0
            values = [jnp.where(bit, values[width + k], values[k]) for k in range(width + 1)]
            width //= 2
        return values

    def chunk(index):
        part = pl.ds(pl.multiple_of(index * FORCE_CHUNK, FORCE_CHUNK), FORCE_CHUNK)
        base_x, base_y, base_z = bases(cell_ref[0, :, part])
        row_z = rows_iota(NZ, FORCE_CHUNK)
        found = []
        for at_z in (base_z, (base_z + 1) & (NZ - 1)):
            chosen = jnp.where(row_z == at_z, 1.0, 0.0).astype(jnp.bfloat16)
            found.append(matmul(left_ref[...], jnp.concatenate([chosen, chosen], axis=0)))
        shape = (8, FORCE_CHUNK)
        f = [jnp.broadcast_to(frac_ref[k, 0, :, part], shape) for k in range(3)]
        slot = index * FORCE_CHUNK + lax.broadcasted_iota(jnp.int32, (1, FORCE_CHUNK), 1)
        charge = jnp.where(slot < count, charge_ref[0, :, part], 0.0)
        base_x = jnp.broadcast_to(base_x, shape)
        base_y = jnp.broadcast_to(base_y, shape)
        row = rows_iota(*shape)
        across, along, slope = [jnp.zeros(shape, jnp.float32) for _ in range(3)]
        for tile in range(CY // 8):
            ends = []
            for values in found:
                rows = [values[x * CY + tile * 8 : x * CY + tile * 8 + 8] for x in range(CX + 1)]
                ends.append(pick(rows, base_x))
            rise = [ends[1][k] - ends[0][k] for k in range(2)]
            level = [ends[0][k] + f[2] * rise[k] for k in range(2)]
            step_x = level[1] - level[0]
            lower, upper = row + tile * 8 == base_y, row + tile * 8 == base_y + 1
            weight = jnp.where(lower, 1.0 - f[1], jnp.where(upper, f[1], 0.0))
            sign = jnp.where(lower, -1.0, jnp.where(upper, 1.0, 0.0))
            across = across + weight * step_x
            along = along + sign * (level[0] + f[0] * step_x)
            slope = slope + weight * (rise[0] + f[0] * (rise[1] - rise[0]))
        ends = []
        for values in found:
            low, high = [jnp.zeros(shape, jnp.float32) for _ in range(2)]
            for tile in range(CY // 8):
                value = values[(CX + 1) * CY + tile * 8 : (CX + 1) * CY + tile * 8 + 8]
                layer = row + (tile * 8 if tile < 2 else 12)
                if tile == 1:
                    layer = jnp.where(layer < 12, layer, -5)
                low = jnp.where(layer == base_x, value, low)
                high = jnp.where(layer == base_x + 1, value, high)
            ends.append((low, high))
        edge = base_y == CY - 1
        weight = jnp.where(edge, f[1], 0.0)
        rise = [ends[1][k] - ends[0][k] for k in range(2)]
        level = [ends[0][k] + f[2] * rise[k] for k in range(2)]
        across = across + weight * (level[1] - level[0])
        along = along + jnp.where(edge, level[0] + f[0] * (0.0 - level[0]) + f[0] * level[1], 0.0)
        slope = slope + weight * (rise[0] + f[0] * (0.0 - rise[0]) + f[0] * rise[1])
        for k, value in enumerate((across, along, slope)):
            forces_ref[k, 0, :, part] = -charge * jnp.sum(value, axis=0, keepdims=True)

    def step(index, carry):
        for k in range(FORCE_UNROLL):
            chunk(index * FORCE_UNROLL + k)
        return carry

    width = FORCE_CHUNK * FORCE_UNROLL
    lax.fori_loop(0, jnp.minimum(pl.cdiv(count, width), slots // width), step, 0)


VMEM = pl.BlockSpec(memory_space=pltpu.VMEM)
ANY = pl.BlockSpec(memory_space=pl.ANY)


def solution(mesh):
    sizes = (mesh.shape["gx"], mesh.shape["gy"])
    constants = tables()

    def per_device(atom_cell, atom_frac, atom_charge, atom_count, fine_kernel, middle_kernel, coarse_kernel):
        slots = atom_cell.shape[-1]
        f32 = jnp.float32
        grid = (CX + 2, CY, LANES)
        scratch = [
            pltpu.VMEM(grid, f32),
            pltpu.VMEM((BX[1] + 1, ROWS[1], LANES), f32),
            pltpu.VMEM((BX[2] + 1, ROWS[1], LANES), f32),
            pltpu.VMEM((KERNEL, 16, LANES), f32),
        ]
        scratch += [pltpu.VMEM(table.shape, jnp.dtype(table.dtype)) for table in constants]
        scratch += [pltpu.VMEM((WINDOW[k], PERIOD[k], LANES), f32) for k in range(LEVELS)]
        scratch += [pltpu.VMEM((KERNEL, PERIOD[k], LANES), f32) for k in range(LEVELS)] * 2
        scratch += [pltpu.VMEM((WINDOW[k] * PERIOD[k], 2 * LANES), f32) for k in range(LEVELS)]
        scratch += [pltpu.VMEM((SPECTRA[k], 2 * PERIOD[k], LANES), f32) for k in range(LEVELS)]
        scratch += [pltpu.VMEM((message.layers[1], message.rows[1], LANES), f32) for message in PLAN]
        scratch += [pltpu.SemaphoreType.DMA((len(PLAN),))] * 2 + [pltpu.SemaphoreType.DMA((len(constants),))]
        extended = pl.pallas_call(
            lambda *refs: grid_kernel(sizes, len(constants), *refs),
            out_shape=pltpu.VMEM(grid, f32),
            in_specs=[VMEM] * 7 + [ANY] * len(constants),
            out_specs=VMEM,
            scratch_shapes=scratch,
            compiler_params=pltpu.CompilerParams(collective_id=0, has_side_effects=True),
            name="grid",
        )(
            atom_count,
            atom_cell,
            atom_frac,
            atom_charge,
            fine_kernel,
            middle_kernel,
            coarse_kernel,
            *[jnp.asarray(table) for table in constants],
        )
        potential, forces = pl.pallas_call(
            force_kernel,
            out_shape=(jax.ShapeDtypeStruct((CX, CY, NZ), f32), jax.ShapeDtypeStruct((3, 1, 1, slots), f32)),
            in_specs=[VMEM] * 5,
            out_specs=(VMEM, VMEM),
            scratch_shapes=[pltpu.VMEM((GRID_ROWS, 2 * LANES), jnp.bfloat16)],
            name="forces",
        )(atom_count, *[pltpu.with_memory_space_constraint(x, pltpu.VMEM) for x in (atom_cell, atom_frac, atom_charge, extended)])
        return potential, forces

    return jax.shard_map(
        per_device,
        mesh=mesh,
        in_specs=(
            P("gx", "gy", None),
            P(None, "gx", "gy", None),
            P("gx", "gy", None),
            P("gx", "gy"),
            P(),
            P(),
            P(),
        ),
        out_specs=(P("gx", "gy", None), P(None, "gx", "gy", None)),
        check_vma=False,
    )
```

```python
import jax
import jax.numpy as jnp
import ml_dtypes
import numpy as np
from jax import lax
from jax.experimental import pallas as pl
from jax.experimental.pallas import tpu as pltpu
from jax.sharding import PartitionSpec as P

CX = 16
CY = 24
NZ = 128
KERNEL = 9
HALF = KERNEL // 2
REACH = HALF + 1
LANES = 128
LAYERS = CX + 1
TOP_ROWS = -(-LAYERS * (CY + 1) // 16) * 16
FORCE_CHUNK = 256
SPREAD_PART = 512
FORCE_UNROLL = 8
LEVELS = 3
MESH = pl.DeviceIdType.MESH

BX = tuple(CX >> k for k in range(LEVELS))
BY = tuple(CY >> k for k in range(LEVELS))
ZS = tuple(NZ >> k for k in range(LEVELS))
PAIR = tuple((size + 2) // 2 for size in BX)
PERIOD = tuple(-(-(size + 1 + 2 * HALF) // 8) * 8 for size in BY)
WINDOW = (CX + 1, *(size + 1 + 2 * HALF for size in BX[1:]))
SPECTRA = tuple(size + 2 * HALF for size in PAIR)
ROWS = (32, 16, 8)
FIRST_LANE = (0, 0, ZS[1])
GRID_ROWS = (CX + 2) * CY
LOW_ROWS = ((BX[1] + 1) * ROWS[1], (BX[2] + 1) * ROWS[2])


def strip_row(x):
    return x if x < 12 else x + 4


def np_hat(distance):
    return np.maximum(1.0 - np.abs(distance), 0.0)


def np_ring_hat(distance, period):
    distance = np.abs(distance)
    return np.maximum(1.0 - np.minimum(distance, period - distance), 0.0)


def np_split(value):
    high = value.astype(np.float32).astype(ml_dtypes.bfloat16)
    low = (value - high.astype(np.float64)).astype(ml_dtypes.bfloat16)
    return high, low


def fine_places():
    xs, ys = np.full(GRID_ROWS, -1e6), np.full(GRID_ROWS, -1e6)
    for x in range(CX + 1):
        for y in range(CY):
            xs[x * CY + y], ys[x * CY + y] = x, y
        xs[(CX + 1) * CY + strip_row(x)], ys[(CX + 1) * CY + strip_row(x)] = x, CY
    return xs, ys


def transfer_xy():
    xs, ys = fine_places()
    parts = []
    for level in (1, 2):
        scale = 0.5**level
        layers = np.repeat(np.arange(BX[level] + 1), ROWS[level])
        rows = np.tile(np.arange(ROWS[level]), BX[level] + 1)
        weight = np_hat(xs[:, None] * scale - layers[None, :]) * np_hat(ys[:, None] * scale - rows[None, :])
        parts.append(weight * (rows <= BY[level])[None, :])
    return np.concatenate(parts, axis=1)


def transfer_z():
    weight = np.zeros((NZ, LANES))
    for level in (1, 2):
        z, low = np.arange(NZ)[:, None], np.arange(ZS[level])[None, :]
        weight[:, FIRST_LANE[level] : FIRST_LANE[level] + ZS[level]] = np_ring_hat(z * 0.5**level - low, ZS[level])
    return weight


def z_forward(level):
    size = ZS[level]
    angle = 2 * np.pi * np.arange(size)[:, None] * np.arange(size)[None, :] / size
    c, s = np.cos(angle), np.sin(angle)
    table = np.zeros((LANES, 2 * LANES))
    first = FIRST_LANE[level]
    if level == 0:
        table[:, :LANES], table[:, LANES:] = c, -s
    else:
        rows = slice(first, first + size)
        table[rows, :size], table[rows, size : 2 * size] = c, -s
        table[rows, LANES : LANES + size], table[rows, LANES + size : LANES + 2 * size] = -s, -c
    high, low = np_split(table)
    return np.concatenate([high, high, low], axis=0)


def z_inverse(level):
    size = ZS[level]
    angle = 2 * np.pi * np.arange(size)[:, None] * np.arange(size)[None, :] / size
    raised = np_ring_hat(np.arange(NZ)[None, :] * 0.5**level - np.arange(size)[:, None], size)
    c, s = np.cos(angle) @ raised / size, np.sin(angle) @ raised / size
    table = np.concatenate([np.concatenate([c, s], axis=1), np.concatenate([-s, c], axis=1)], axis=0)
    rows = 2 * LANES if level == 0 else LANES
    table = np.concatenate([table, np.zeros((rows - table.shape[0], 2 * LANES))], axis=0)
    high, low = np_split(table)
    return np.concatenate([high, high, low], axis=0)


def y_forward(level):
    size = PERIOD[level]
    angle = 2 * np.pi * np.arange(size)[:, None] * np.arange(size)[None, :] / size
    c, s = np.cos(angle), np.sin(angle)
    high, low = np_split(np.block([[c, s], [-s, c]]))
    return np.concatenate([high, high, low], axis=1)


def y_inverse(level):
    size = PERIOD[level]
    angle = 2 * np.pi * np.arange(ROWS[level])[:, None] * np.arange(size)[None, :] / size
    keep = (np.arange(ROWS[level]) <= BY[level])[:, None]
    c, s = np.cos(angle) * keep / size, np.sin(angle) * keep / size
    table = np.block([[c, -s], [s, c]]) if level == 0 else np.block([[c, -s]])
    if table.shape[0] < 16:
        table = np.concatenate([table, np.zeros((16 - table.shape[0], 2 * size))], axis=0)
    high, low = np_split(table)
    return np.concatenate([high, high, low], axis=1)


def stack_split(table, axis):
    high, low = np_split(table)
    return np.concatenate([high, high, low], axis=axis)


def taps_z(level):
    size = ZS[level]
    angle = 2 * np.pi * (np.arange(KERNEL) - HALF)[:, None] * np.arange(size)[None, :] / size
    table = np.zeros((LANES, 2 * LANES))
    for copy in range(1 if level == 0 else 2):
        table[:KERNEL, copy * size : (copy + 1) * size] = np.cos(angle)
        table[:KERNEL, LANES + copy * size : LANES + (copy + 1) * size] = np.sin(angle)
    return stack_split(table, 0)


def taps_y(level):
    size = PERIOD[level]
    angle = 2 * np.pi * np.arange(size)[:, None] * (np.arange(16) - HALF)[None, :] / size
    keep = (np.arange(16) < KERNEL)[None, :]
    c, s = np.cos(angle) * keep, np.sin(angle) * keep
    return stack_split(np.block([[c, -s], [s, c]]), 1)


def tables():
    xy = transfer_xy()
    z = transfer_z()
    bf16 = ml_dtypes.bfloat16
    out = [xy.T.astype(bf16), xy.astype(bf16), np.concatenate([z, z], axis=0).astype(bf16)]
    for level in range(LEVELS):
        out += [z_forward(level), z_inverse(level), y_forward(level), y_inverse(level), taps_z(level), taps_y(level)]
    return out


def split(value):
    high = value.astype(jnp.bfloat16)
    return high, (value - high.astype(jnp.float32)).astype(jnp.bfloat16)


def matmul(a, b):
    return jnp.dot(a, b, preferred_element_type=jnp.float32)


def matmul_nt(a, b):
    return lax.dot_general(a, b, (((1,), (1,)), ((), ())), preferred_element_type=jnp.float32)


def rows_iota(rows, columns):
    return lax.broadcasted_iota(jnp.int32, (rows, columns), 0)


def bases(cell):
    return cell // (CY * NZ), (cell // NZ) % CY, cell % NZ


def wide(value, dtype):
    return jnp.broadcast_to(value, (16, value.shape[1])).astype(dtype)


def row_patterns(columns):
    row = rows_iota(16, columns)
    patterns = []
    for tile in range(TOP_ROWS // 16):
        xs, ys = [], []
        for part in range(2):
            first = tile * 16 + part * 8
            if first < LAYERS * CY:
                xs.append(first // CY)
                ys.append(row + (first % CY - 8 * part))
            else:
                at = row + (first - LAYERS * CY - 8 * part)
                xs.append(jnp.where(at < LAYERS, at, -9))
                ys.append(jnp.full_like(row, CY))
        if all(isinstance(x, int) for x in xs) and xs[0] == xs[1]:
            x = jnp.full((16, columns), xs[0], jnp.int16)
        else:
            x = jnp.where(row < 8, xs[0], xs[1]).astype(jnp.int16)
        patterns.append((x, jnp.where(row < 8, ys[0], ys[1]).astype(jnp.int16)))
    return patterns


def spread_sides(count_ref, cell_ref, frac_ref, charge_ref, start, patterns, row_z):
    bf16, i16 = jnp.bfloat16, jnp.int16
    part = slice(start, start + SPREAD_PART)
    base_x, base_y, base_z = bases(cell_ref[0, :, part])
    f = [frac_ref[k, 0, :, part] for k in range(3)]
    slot = start + lax.broadcasted_iota(jnp.int32, (1, SPREAD_PART), 1)
    charge = jnp.where(slot < count_ref[...], charge_ref[0, :, part], 0.0)
    nothing = jnp.zeros((16, SPREAD_PART), bf16)
    x_at, x_next = wide(base_x, i16), wide(base_x + 1, i16)
    y_at, y_next = wide(base_y, i16), wide(base_y + 1, i16)
    corner = {}
    for a, along_x in enumerate((charge * (1.0 - f[0]), charge * f[0])):
        for b, along_y in enumerate((1.0 - f[1], f[1])):
            high, low = split(along_x * along_y)
            corner[a, b] = (wide(high, bf16), wide(low, bf16))
    highs, lows = [], []
    known = {}
    for tile, (xs, ys) in enumerate(patterns):
        key = tile % 3 if (tile + 1) * 16 <= LAYERS * CY else tile
        if key not in known:
            here, above = ys == y_at, ys == y_next
            known[key] = [
                [jnp.where(here, corner[a, 0][k], jnp.where(above, corner[a, 1][k], nothing)) for k in range(2)]
                for a in range(2)
            ]
        here, above = xs == x_at, xs == x_next
        for k, target in enumerate((highs, lows)):
            target.append(jnp.where(here, known[key][0][k], jnp.where(above, known[key][1][k], nothing)))
    weights = [[wide(piece, bf16) for piece in split(value)] for value in (1.0 - f[2], f[2])]
    sides = ([], [])
    z_at, z_next = wide(base_z, i16), wide((base_z + 1) & (NZ - 1), i16)
    for rows in row_z:
        here, above = rows == z_at, rows == z_next
        for k in range(2):
            sides[k].append(jnp.where(here, weights[0][k], jnp.where(above, weights[1][k], nothing)))
    return [jnp.concatenate(pieces, axis=0) for pieces in (highs, lows, *sides)]


def spread(count_ref, cell_ref, frac_ref, charge_ref, grid_ref):
    slots = cell_ref.shape[-1]
    patterns = row_patterns(SPREAD_PART)
    row_z = [(rows_iota(16, SPREAD_PART) + first).astype(jnp.int16) for first in range(0, NZ, 16)]
    parts = [
        spread_sides(count_ref, cell_ref, frac_ref, charge_ref, start, patterns, row_z)
        for start in range(0, slots, SPREAD_PART)
    ]
    top_high, top_low, z_high, z_low = [jnp.concatenate(pieces, axis=1) for pieces in zip(*parts)]
    both = matmul_nt(top_high, jnp.concatenate([z_high, z_low], axis=0))
    value = both[:, :LANES] + both[:, LANES:] + matmul_nt(top_low, z_high)
    layers = LAYERS * CY
    grid_ref[:LAYERS] = value[:layers].reshape(LAYERS, CY, LANES)
    grid_ref[LAYERS] = jnp.zeros((CY, LANES), jnp.float32)
    for x in range(LAYERS):
        grid_ref[LAYERS, strip_row(x) : strip_row(x) + 1, :] = value[layers + x : layers + x + 1]


def lane_iota():
    return lax.broadcasted_iota(jnp.int32, (1, 1, LANES), 2)


def restrict(grid_ref, down_ref, down_z_ref, middle_ref, low_ref):
    high, low = split(grid_ref[...].reshape(GRID_ROWS, LANES))
    both = matmul(down_ref[...], jnp.concatenate([high, low], axis=1))
    high, low = split(both[:, :LANES] + both[:, LANES:])
    value = matmul(jnp.concatenate([high, low], axis=1), down_z_ref[...])
    middle = value[: LOW_ROWS[0]].reshape(BX[1] + 1, ROWS[1], LANES)
    coarse = value[LOW_ROWS[0] :].reshape(BX[2] + 1, ROWS[2], LANES)
    twice = jnp.concatenate([coarse, coarse], axis=1)
    first = BX[1] - BX[2]
    mine = lane_iota() < FIRST_LANE[2]
    middle_ref[:first] = middle[:first]
    middle_ref[first:] = jnp.where(mine, middle[first:], twice)
    low_ref[...] = jnp.where(mine, middle[: BX[2] + 1], twice)


def build_taps(level, kernel_ref, padded_ref, z_ref, y_ref, real_ref, imag_ref):
    padded_ref[...] = jnp.zeros_like(padded_ref)
    padded_ref[:, :KERNEL, :KERNEL] = kernel_ref[...]
    along_z = matmul(three(padded_ref[...].reshape(KERNEL * 16, LANES), 1), z_ref[...])
    size = PERIOD[level]
    for shift in range(0, KERNEL, 2):
        pieces = []
        for one in range(shift, min(shift + 2, KERNEL)):
            rows = along_z[one * 16 : (one + 1) * 16]
            pieces.append(three(jnp.concatenate([rows[:, :LANES], rows[:, LANES:]], axis=0), 0))
        both = matmul(y_ref[...], jnp.concatenate(pieces, axis=1))
        for k in range(len(pieces)):
            real_ref[shift + k] = both[:size, k * LANES : (k + 1) * LANES]
            imag_ref[shift + k] = both[size:, k * LANES : (k + 1) * LANES]


def three(value, axis):
    high, low = split(value)
    return jnp.concatenate([high, low, high], axis=axis)


def add_spectra(level, source_ref, slots, taps, tables, along_z_ref, spectrum_ref, sums_ref, fresh):
    forward_z, _, forward_y, _ = tables
    size, pair = PERIOD[level], PAIR[level]
    used = len(slots)
    flat = source_ref[...].reshape(used * size, LANES)
    half = (used // 2 + 1) * size
    for rows in (slice(0, half), slice(half, used * size)):
        along_z_ref[rows] = matmul(three(flat[rows], 1), forward_z[...])

    def part(layer, which):
        slot = slots[layer]
        return along_z_ref[slot * size : (slot + 1) * size, which * LANES : (which + 1) * LANES]

    def combined(layer):
        if layer not in slots:
            return [-part(layer + pair, 1), part(layer + pair, 0)]
        if layer + pair not in slots:
            return [part(layer, 0), part(layer, 1)]
        return [part(layer, 0) - part(layer + pair, 1), part(layer, 1) + part(layer + pair, 0)]

    present = [layer for layer in range(SPECTRA[level]) if layer in slots or layer + pair in slots]
    for first in range(0, len(present), 2):
        group = present[first : first + 2]
        pieces = [three(jnp.concatenate(combined(layer), axis=0), 0) for layer in group]
        both = matmul(forward_y[...], jnp.concatenate(pieces, axis=1))
        for k, layer in enumerate(group):
            spectrum_ref[layer] = both[:, k * LANES : (k + 1) * LANES]
    real_ref, imag_ref = taps
    for out in range(pair):
        for tile in range(0, size, 8):
            rows, rest = slice(tile, tile + 8), slice(size + tile, size + tile + 8)
            real = jnp.zeros((8, LANES), jnp.float32) if fresh else sums_ref[out, rows]
            imag = jnp.zeros((8, LANES), jnp.float32) if fresh else sums_ref[out, rest]
            for shift in range(KERNEL):
                if out + shift in present:
                    a, b = spectrum_ref[out + shift, rows], spectrum_ref[out + shift, rest]
                    c, s = real_ref[shift, rows], imag_ref[shift, rows]
                    real = real + a * c - b * s
                    imag = imag + a * s + b * c
            sums_ref[out, rows] = real
            sums_ref[out, rest] = imag


def from_spectra(level, tables, sums_ref):
    _, inverse_z, _, inverse_y = tables
    pair, rows = PAIR[level], ROWS[level]
    lines = []
    for first in range(0, pair, 2):
        group = range(first, min(first + 2, pair))
        both = matmul(inverse_y[...], jnp.concatenate([three(sums_ref[out], 0) for out in group], axis=1))
        for k in range(len(group)):
            line = both[:rows, k * LANES : (k + 1) * LANES]
            if level == 0:
                line = jnp.concatenate([line, both[rows:, k * LANES : (k + 1) * LANES]], axis=1)
            lines.append(line)
    half = pair // 2 + 1
    values = []
    for group in (lines[:half], lines[half:]):
        value = matmul(three(jnp.concatenate(group, axis=0), 1), inverse_z[...])
        values += [value[k * rows : (k + 1) * rows] for k in range(len(group))]
    layers = [value[:, :LANES] for value in values] + [value[:, LANES:] for value in values]
    return layers[: BX[level] + 1]


GRID, MIDDLE, LOW, LANDED = range(4)


def side(step, size):
    return {-1: (0, REACH), 0: (0, size + 1), 1: (size - HALF, REACH)}[step]


class Message:
    def __init__(self, kind, dx, dy, source, layers, rows, relayed=None):
        self.kind, self.dx, self.dy = kind, dx, dy
        self.source, self.layers, self.rows, self.relayed = source, layers, rows, relayed
        self.hop = (dx, dy) if relayed is None else (0, dy)
        self.local = (layers, rows)
        if relayed is not None:
            self.local = ((0, layers[1]), (rows[0] - relayed.rows[0], rows[1]))


def plan_messages():
    near, far, face, strip = {}, {}, {}, {}
    top, bottom = (CY - 8, 8), (0, 8)
    for dx, layer in ((-2, 0), (2, BX[1])):
        far[dx, 0] = Message("far", dx, 0, LOW if dx < 0 else MIDDLE, (layer, 1), (0, 8))
    for dx in (-1, 1):
        near[dx, 0] = Message("near", dx, 0, LOW if dx < 0 else MIDDLE, side(dx, BX[1]), (0, ROWS[1]))
        strip[dx, 0] = Message("strip", dx, 0, GRID, (CX + 1, 1), bottom if dx < 0 else top)
        for name, rows in (("top", top), ("bottom", bottom), ("centre", (8, CY - 16))):
            face[dx, name] = Message("face", dx, 0, GRID, side(dx, BX[0]), rows)
    for dy in (-1, 1):
        rows = bottom if dy < 0 else (ROWS[1] - 8, 8)
        near[0, dy] = Message("near", 0, dy, MIDDLE, side(0, BX[1]), rows)
        face[0, dy] = Message("face", 0, dy, GRID, side(0, BX[0]), bottom if dy < 0 else top)
        for dx in (-2, 2):
            far[dx, dy] = Message("far", dx, dy, LANDED, far[dx, 0].layers, (0, 8), far[dx, 0])
        for dx in (-1, 1):
            near[dx, dy] = Message("near", dx, dy, LANDED, near[dx, 0].layers, rows, near[dx, 0])
            first = face[dx, "bottom" if dy < 0 else "top"]
            face[dx, dy] = Message("face", dx, dy, LANDED, first.layers, first.rows, first)
    strip[0, 1] = Message("strip", 0, 1, GRID, (CX + 1, 1), (0, CY))
    for dx in (-1, 1):
        strip[dx, 1] = Message("strip", dx, 1, LANDED, (CX + 1, 1), strip[dx, 0].rows, strip[dx, 0])
    sides = (-1, 1)
    first = [near[dx, 0] for dx in sides]
    first += [face[dx, name] for name in ("top", "bottom") for dx in sides] + [strip[dx, 0] for dx in sides]
    first += [near[0, dy] for dy in sides] + [far[dx, 0] for dx in (-2, 2)]
    first += [face[0, dy] for dy in sides] + [strip[0, 1]] + [face[dx, "centre"] for dx in sides]
    second = [near[dx, dy] for dx in sides for dy in sides] + [far[dx, dy] for dx in (-2, 2) for dy in sides]
    second += [face[dx, dy] for dy in (1, -1) for dx in sides] + [strip[dx, 1] for dx in sides]
    return first, second


FIRST, SECOND = plan_messages()
PLAN = FIRST + SECOND


def add_rows(window_ref, layer, first, piece):
    rows = slice(first, first + piece.shape[-2])
    layers = slice(layer, layer + piece.shape[0])
    window_ref[layers, rows, :] = window_ref[layers, rows, :] + piece


def add_level_rows(window_ref, level, layer, dy, piece):
    size = BY[level]
    if dy == 0:
        add_rows(window_ref, layer, 0, piece[:, : size + 1])
    elif dy < 0:
        add_rows(window_ref, layer, size, piece[:, :REACH])
    else:
        base = piece.shape[-2] - 8 if piece.shape[-2] > 8 else (size // 8) * 8
        first = size - HALF - base
        add_rows(window_ref, layer, PERIOD[level] - HALF, piece[:, first : first + HALF])
        add_rows(window_ref, layer, 0, piece[:, first + HALF : first + HALF + 1])


def add_low(windows, message, landed):
    dx, dy, first = message.dx, message.dy, message.layers[0]
    if message.kind == "far":
        layer = HALF + (0 if dx < 0 else BX[2]) - dx * BX[2]
        add_level_rows(windows[2], 2, layer, dy, landed[...])
        return
    add_level_rows(windows[1], 1, HALF + first - dx * BX[1], dy, landed[...])
    ride = BX[1] - BX[2] if dx == 0 else 0
    add_level_rows(windows[2], 2, HALF - dx * BX[2], dy, landed[ride : ride + BX[2] + 1, :8, :])


def add_fine(window_ref, message, landed):
    dx, dy, rows = message.dx, message.dy, message.rows
    offset = {-1: REACH, 0: 0, 1: HALF - BX[0]}[dx]
    if message.kind == "strip":
        low, size = side(dx, BX[0])
        target = CY if dy == 0 else 0
        for k in range(size):
            place = strip_row(low + k) - rows[0]
            layer = offset + low + k
            window_ref[layer, target : target + 1, :] = (
                window_ref[layer, target : target + 1, :] + landed[0, place : place + 1, :]
            )
        return
    first, count = message.layers
    layers = slice(offset + first, offset + first + count)
    row = lax.broadcasted_iota(jnp.int32, (1, 8, LANES), 1)
    value = landed[...]
    at = slice(rows[0], rows[0] + rows[1])
    if dy < 0:
        at, value = slice(CY, CY + 8), jnp.where(row < REACH, value, 0.0)
    elif dy > 0:
        at, value = slice(PERIOD[0] - 8, PERIOD[0]), jnp.where(row >= 8 - HALF, value, 0.0)
    window_ref[layers, at, :] = window_ref[layers, at, :] + value


def grid_kernel(sizes, n_tables, *refs):
    count_ref, cell_ref, frac_ref, charge_ref = refs[:4]
    kernels = refs[4:7]
    table_sources = refs[7 : 7 + n_tables]
    out_ref = refs[7 + n_tables]
    scratch = list(refs[8 + n_tables :])

    def take(count):
        taken = scratch[:count]
        del scratch[:count]
        return taken

    grid_ref, middle_ref, low_ref, padded_ref = take(4)
    table_refs = take(n_tables)
    windows, reals, imags, along_z, spectra, sums = take(3), take(3), take(3), take(3), take(3), take(3)
    (edges_ref,) = take(1)
    landed = take(len(PLAN))
    send_sem, recv_sem, table_sem = take(3)

    me = (lax.axis_index("gx"), lax.axis_index("gy"))

    def device(dx, dy):
        return (lax.rem(me[0] + dx + sizes[0], sizes[0]), lax.rem(me[1] + dy + sizes[1], sizes[1]))

    barrier = pltpu.get_barrier_semaphore()
    around = sorted({message.hop for message in PLAN})
    for dx, dy in around:
        pl.semaphore_signal(barrier, inc=1, device_id=device(dx, dy), device_id_type=MESH)
    loads = [
        pltpu.make_async_copy(source, target, table_sem.at[index])
        for index, (source, target) in enumerate(zip(table_sources, table_refs))
    ]
    for load in loads:
        load.start()

    spread(count_ref, cell_ref, frac_ref, charge_ref, grid_ref)
    for load in loads[:3]:
        load.wait()
    down_ref, up_ref, down_z_ref = table_refs[:3]
    restrict(grid_ref, down_ref, down_z_ref, middle_ref, low_ref)
    pl.semaphore_wait(barrier, len(around))

    sources = (grid_ref, middle_ref, low_ref)
    copies = {}
    for index, message in enumerate(PLAN):
        relayed = message.relayed
        source = sources[message.source] if relayed is None else landed[PLAN.index(relayed)]
        (first, size), (low, rows) = message.local
        copies[message] = pltpu.make_async_remote_copy(
            src_ref=source.at[pl.ds(first, size), pl.ds(low, rows)],
            dst_ref=landed[index],
            send_sem=send_sem.at[index],
            recv_sem=recv_sem.at[index],
            device_id=device(*message.hop),
            device_id_type=MESH,
        )
    arrived = set()

    def arrive(message):
        if message not in arrived:
            arrived.add(message)
            copies[message].wait_recv()

    for message in FIRST:
        copies[message].start()
    for load in loads[3:]:
        load.wait()

    level_tables = [table_refs[3 + 6 * level : 9 + 6 * level] for level in range(LEVELS)]
    for level in (2, 1, 0):
        build_taps(level, kernels[level], padded_ref, *level_tables[level][4:], reals[level], imags[level])

    for level in range(LEVELS):
        windows[level][...] = jnp.zeros_like(windows[level])
    edges_ref[...] = jnp.zeros_like(edges_ref)
    windows[0][:, :CY, :] = grid_ref[: CX + 1]
    for x in range(CX + 1):
        windows[0][x, CY : CY + 1, :] = grid_ref[CX + 1, strip_row(x) : strip_row(x) + 1, :]
    windows[1][HALF : HALF + BX[1] + 1, : ROWS[1], :] = middle_ref[...]
    windows[2][HALF : HALF + BX[2] + 1, : ROWS[2], :] = low_ref[:, : ROWS[2], :]

    for message in SECOND:
        if message.kind in ('near', 'far'):
            arrive(message.relayed)
            copies[message].start()
    def run(level, source_ref, layers, fresh):
        slots = {layer: slot for slot, layer in enumerate(layers)}
        taps = (reals[level], imags[level])
        tables = level_tables[level][:4]
        add_spectra(level, source_ref, slots, taps, tables, along_z[level], spectra[level], sums[level], fresh)

    fine = [message for message in PLAN if message.kind in ("face", "strip")]
    for message in fine:
        if message.dx == 0:
            arrive(message)
            add_fine(windows[0], message, landed[PLAN.index(message)])
    run(0, windows[0], range(HALF, HALF + CX + 1), True)
    for message in SECOND:
        if message.kind not in ('near', 'far'):
            arrive(message.relayed)
            copies[message].start()
    for message in PLAN:
        if message.kind in ("near", "far"):
            arrive(message)
            add_low(windows, message, landed[PLAN.index(message)])
    below = []
    for level in (1, 2):
        run(level, windows[level], range(BX[level] + 1 + 2 * HALF), True)
        below += from_spectra(level, level_tables[level][:4], sums[level])
    high, low = split(jnp.concatenate(below, axis=0))
    both = matmul(up_ref[...], jnp.concatenate([high, low], axis=1))
    out_ref[...] = (both[:, :LANES] + both[:, LANES:]).reshape(out_ref.shape)
    for message in PLAN:
        copies[message].wait_send()
    for message in fine:
        if message.dx != 0:
            arrive(message)
            add_fine(edges_ref, message, landed[PLAN.index(message)])
    last = CX + 1 + 2 * HALF
    run(0, edges_ref, [*range(REACH), *range(last - REACH, last)], False)
    layers = from_spectra(0, level_tables[0][:4], sums[0])
    for x in range(CX + 1):
        out_ref[x] = out_ref[x] + layers[x][:CY]
        at = slice(strip_row(x), strip_row(x) + 1)
        out_ref[CX + 1, at, :] = out_ref[CX + 1, at, :] + layers[x][CY : CY + 1]


def force_kernel(count_ref, cell_ref, frac_ref, charge_ref, grid_ref, potential_ref, forces_ref, left_ref):
    slots = cell_ref.shape[-1]
    potential_ref[...] = grid_ref[:CX]
    forces_ref[...] = jnp.zeros_like(forces_ref)
    left_ref[...] = jnp.concatenate(split(grid_ref[...].reshape(GRID_ROWS, LANES)), axis=1)
    count = jnp.max(count_ref[...].astype(jnp.float32)).astype(jnp.int32)

    def pick(values, base):
        width = CX // 2
        while width >= 1:
            bit = (base & width) != 0
            values = [jnp.where(bit, values[width + k], values[k]) for k in range(width + 1)]
            width //= 2
        return values

    def chunk(index):
        part = pl.ds(pl.multiple_of(index * FORCE_CHUNK, FORCE_CHUNK), FORCE_CHUNK)
        base_x, base_y, base_z = bases(cell_ref[0, :, part])
        row = rows_iota(16, FORCE_CHUNK)
        one, nothing = [jnp.full((16, FORCE_CHUNK), value, jnp.bfloat16) for value in (1.0, 0.0)]
        found = []
        for at_z in (base_z, (base_z + 1) & (NZ - 1)):
            target = wide(at_z, jnp.int16)
            chosen = [jnp.where((row + z).astype(jnp.int16) == target, one, nothing) for z in range(0, NZ, 16)]
            found.append(matmul(left_ref[...], jnp.concatenate(chosen * 2, axis=0)))
        shape = (8, FORCE_CHUNK)
        f = [jnp.broadcast_to(frac_ref[k, 0, :, part], shape) for k in range(3)]
        slot = index * FORCE_CHUNK + lax.broadcasted_iota(jnp.int32, (1, FORCE_CHUNK), 1)
        charge = jnp.where(slot < count, charge_ref[0, :, part], 0.0)
        base_x = jnp.broadcast_to(base_x, shape)
        base_y = jnp.broadcast_to(base_y, shape)
        row = rows_iota(*shape)
        across, along, slope = [jnp.zeros(shape, jnp.float32) for _ in range(3)]
        for tile in range(CY // 8):
            ends = []
            for values in found:
                rows = [values[x * CY + tile * 8 : x * CY + tile * 8 + 8] for x in range(CX + 1)]
                ends.append(pick(rows, base_x))
            rise = [ends[1][k] - ends[0][k] for k in range(2)]
            level = [ends[0][k] + f[2] * rise[k] for k in range(2)]
            step_x = level[1] - level[0]
            lower, upper = row + tile * 8 == base_y, row + tile * 8 == base_y + 1
            weight = jnp.where(lower, 1.0 - f[1], jnp.where(upper, f[1], 0.0))
            sign = jnp.where(lower, -1.0, jnp.where(upper, 1.0, 0.0))
            across = across + weight * step_x
            along = along + sign * (level[0] + f[0] * step_x)
            slope = slope + weight * (rise[0] + f[0] * (rise[1] - rise[0]))
        ends = []
        for values in found:
            low, high = [jnp.zeros(shape, jnp.float32) for _ in range(2)]
            for tile in range(CY // 8):
                value = values[(CX + 1) * CY + tile * 8 : (CX + 1) * CY + tile * 8 + 8]
                layer = row + (tile * 8 if tile < 2 else 12)
                if tile == 1:
                    layer = jnp.where(layer < 12, layer, -5)
                low = jnp.where(layer == base_x, value, low)
                high = jnp.where(layer == base_x + 1, value, high)
            ends.append((low, high))
        edge = base_y == CY - 1
        weight = jnp.where(edge, f[1], 0.0)
        rise = [ends[1][k] - ends[0][k] for k in range(2)]
        level = [ends[0][k] + f[2] * rise[k] for k in range(2)]
        across = across + weight * (level[1] - level[0])
        along = along + jnp.where(edge, level[0] + f[0] * (0.0 - level[0]) + f[0] * level[1], 0.0)
        slope = slope + weight * (rise[0] + f[0] * (0.0 - rise[0]) + f[0] * rise[1])
        for k, value in enumerate((across, along, slope)):
            forces_ref[k, 0, :, part] = -charge * jnp.sum(value, axis=0, keepdims=True)

    def step(index, carry):
        for k in range(FORCE_UNROLL):
            chunk(index * FORCE_UNROLL + k)
        return carry

    width = FORCE_CHUNK * FORCE_UNROLL
    lax.fori_loop(0, jnp.minimum(pl.cdiv(count, width), slots // width), step, 0)


VMEM = pl.BlockSpec(memory_space=pltpu.VMEM)
ANY = pl.BlockSpec(memory_space=pl.ANY)


def solution(mesh):
    sizes = (mesh.shape["gx"], mesh.shape["gy"])
    constants = tables()

    def per_device(atom_cell, atom_frac, atom_charge, atom_count, fine_kernel, middle_kernel, coarse_kernel):
        slots = atom_cell.shape[-1]
        f32 = jnp.float32
        grid = (CX + 2, CY, LANES)
        scratch = [
            pltpu.VMEM(grid, f32),
            pltpu.VMEM((BX[1] + 1, ROWS[1], LANES), f32),
            pltpu.VMEM((BX[2] + 1, ROWS[1], LANES), f32),
            pltpu.VMEM((KERNEL, 16, LANES), f32),
        ]
        scratch += [pltpu.VMEM(table.shape, jnp.dtype(table.dtype)) for table in constants]
        scratch += [pltpu.VMEM((WINDOW[k], PERIOD[k], LANES), f32) for k in range(LEVELS)]
        scratch += [pltpu.VMEM((KERNEL, PERIOD[k], LANES), f32) for k in range(LEVELS)] * 2
        scratch += [pltpu.VMEM((WINDOW[k] * PERIOD[k], 2 * LANES), f32) for k in range(LEVELS)]
        scratch += [pltpu.VMEM((SPECTRA[k], 2 * PERIOD[k], LANES), f32) for k in range(LEVELS)]
        scratch += [pltpu.VMEM((PAIR[k], 2 * PERIOD[k], LANES), f32) for k in range(LEVELS)]
        scratch += [pltpu.VMEM((2 * REACH, PERIOD[0], LANES), f32)]
        scratch += [pltpu.VMEM((message.layers[1], message.rows[1], LANES), f32) for message in PLAN]
        scratch += [pltpu.SemaphoreType.DMA((len(PLAN),))] * 2 + [pltpu.SemaphoreType.DMA((len(constants),))]
        extended = pl.pallas_call(
            lambda *refs: grid_kernel(sizes, len(constants), *refs),
            out_shape=pltpu.VMEM(grid, f32),
            in_specs=[VMEM] * 7 + [ANY] * len(constants),
            out_specs=VMEM,
            scratch_shapes=scratch,
            compiler_params=pltpu.CompilerParams(collective_id=0, has_side_effects=True),
            name="grid",
        )(
            atom_count,
            atom_cell,
            atom_frac,
            atom_charge,
            fine_kernel,
            middle_kernel,
            coarse_kernel,
            *[jnp.asarray(table) for table in constants],
        )
        potential, forces = pl.pallas_call(
            force_kernel,
            out_shape=(jax.ShapeDtypeStruct((CX, CY, NZ), f32), jax.ShapeDtypeStruct((3, 1, 1, slots), f32)),
            in_specs=[VMEM] * 5,
            out_specs=(VMEM, VMEM),
            scratch_shapes=[pltpu.VMEM((GRID_ROWS, 2 * LANES), jnp.bfloat16)],
            name="forces",
        )(atom_count, *[pltpu.with_memory_space_constraint(x, pltpu.VMEM) for x in (atom_cell, atom_frac, atom_charge, extended)])
        return potential, forces

    return jax.shard_map(
        per_device,
        mesh=mesh,
        in_specs=(
            P("gx", "gy", None),
            P(None, "gx", "gy", None),
            P("gx", "gy", None),
            P("gx", "gy"),
            P(),
            P(),
            P(),
        ),
        out_specs=(P("gx", "gy", None), P(None, "gx", "gy", None)),
        check_vma=False,
    )
```

```python
import jax
import jax.numpy as jnp
import ml_dtypes
import numpy as np
from jax import lax
from jax.experimental import pallas as pl
from jax.experimental.pallas import tpu as pltpu
from jax.sharding import PartitionSpec as P

CX = 16
CY = 24
NZ = 128
KERNEL = 9
HALF = KERNEL // 2
REACH = HALF + 1
LANES = 128
LAYERS = CX + 1
TOP_ROWS = -(-LAYERS * (CY + 1) // 16) * 16
FORCE_CHUNK = 256
SPREAD_PART = 512
FORCE_UNROLL = 8
LEVELS = 3
MESH = pl.DeviceIdType.MESH

BX = tuple(CX >> k for k in range(LEVELS))
BY = tuple(CY >> k for k in range(LEVELS))
ZS = tuple(NZ >> k for k in range(LEVELS))
PAIR = tuple((size + 2) // 2 for size in BX)
PERIOD = tuple(-(-(size + 1 + 2 * HALF) // 8) * 8 for size in BY)
WINDOW = (CX + 1, *(size + 1 + 2 * HALF for size in BX[1:]))
SPECTRA = tuple(size + 2 * HALF for size in PAIR)
ROWS = (32, 16, 8)
FIRST_LANE = (0, 0, ZS[1])
GRID_ROWS = (CX + 2) * CY
LOW_ROWS = ((BX[1] + 1) * ROWS[1], (BX[2] + 1) * ROWS[2])


def strip_row(x):
    return x if x < 12 else x + 4


def np_hat(distance):
    return np.maximum(1.0 - np.abs(distance), 0.0)


def np_ring_hat(distance, period):
    distance = np.abs(distance)
    return np.maximum(1.0 - np.minimum(distance, period - distance), 0.0)


def np_split(value):
    high = value.astype(np.float32).astype(ml_dtypes.bfloat16)
    low = (value - high.astype(np.float64)).astype(ml_dtypes.bfloat16)
    return high, low


def fine_places():
    xs, ys = np.full(GRID_ROWS, -1e6), np.full(GRID_ROWS, -1e6)
    for x in range(CX + 1):
        for y in range(CY):
            xs[x * CY + y], ys[x * CY + y] = x, y
        xs[(CX + 1) * CY + strip_row(x)], ys[(CX + 1) * CY + strip_row(x)] = x, CY
    return xs, ys


def transfer_xy():
    xs, ys = fine_places()
    parts = []
    for level in (1, 2):
        scale = 0.5**level
        layers = np.repeat(np.arange(BX[level] + 1), ROWS[level])
        rows = np.tile(np.arange(ROWS[level]), BX[level] + 1)
        weight = np_hat(xs[:, None] * scale - layers[None, :]) * np_hat(ys[:, None] * scale - rows[None, :])
        parts.append(weight * (rows <= BY[level])[None, :])
    return np.concatenate(parts, axis=1)


def transfer_z():
    weight = np.zeros((NZ, LANES))
    for level in (1, 2):
        z, low = np.arange(NZ)[:, None], np.arange(ZS[level])[None, :]
        weight[:, FIRST_LANE[level] : FIRST_LANE[level] + ZS[level]] = np_ring_hat(z * 0.5**level - low, ZS[level])
    return weight


def z_forward(level):
    size = ZS[level]
    angle = 2 * np.pi * np.arange(size)[:, None] * np.arange(size)[None, :] / size
    c, s = np.cos(angle), np.sin(angle)
    table = np.zeros((LANES, 2 * LANES))
    first = FIRST_LANE[level]
    if level == 0:
        table[:, :LANES], table[:, LANES:] = c, -s
    else:
        rows = slice(first, first + size)
        table[rows, :size], table[rows, size : 2 * size] = c, -s
        table[rows, LANES : LANES + size], table[rows, LANES + size : LANES + 2 * size] = -s, -c
    high, low = np_split(table)
    return np.concatenate([high, high, low], axis=0)


def z_inverse(level):
    size = ZS[level]
    angle = 2 * np.pi * np.arange(size)[:, None] * np.arange(size)[None, :] / size
    raised = np_ring_hat(np.arange(NZ)[None, :] * 0.5**level - np.arange(size)[:, None], size)
    c, s = np.cos(angle) @ raised / size, np.sin(angle) @ raised / size
    table = np.concatenate([np.concatenate([c, s], axis=1), np.concatenate([-s, c], axis=1)], axis=0)
    rows = 2 * LANES if level == 0 else LANES
    table = np.concatenate([table, np.zeros((rows - table.shape[0], 2 * LANES))], axis=0)
    high, low = np_split(table)
    return np.concatenate([high, high, low], axis=0)


def y_forward(level):
    size = PERIOD[level]
    angle = 2 * np.pi * np.arange(size)[:, None] * np.arange(size)[None, :] / size
    c, s = np.cos(angle), np.sin(angle)
    high, low = np_split(np.block([[c, s], [-s, c]]))
    return np.concatenate([high, high, low], axis=1)


def y_inverse(level):
    size = PERIOD[level]
    angle = 2 * np.pi * np.arange(ROWS[level])[:, None] * np.arange(size)[None, :] / size
    keep = (np.arange(ROWS[level]) <= BY[level])[:, None]
    c, s = np.cos(angle) * keep / size, np.sin(angle) * keep / size
    table = np.block([[c, -s], [s, c]]) if level == 0 else np.block([[c, -s]])
    if table.shape[0] < 16:
        table = np.concatenate([table, np.zeros((16 - table.shape[0], 2 * size))], axis=0)
    high, low = np_split(table)
    return np.concatenate([high, high, low], axis=1)


def stack_split(table, axis):
    high, low = np_split(table)
    return np.concatenate([high, high, low], axis=axis)


def taps_z(level):
    size = ZS[level]
    angle = 2 * np.pi * (np.arange(KERNEL) - HALF)[:, None] * np.arange(size)[None, :] / size
    table = np.zeros((LANES, 2 * LANES))
    for copy in range(1 if level == 0 else 2):
        table[:KERNEL, copy * size : (copy + 1) * size] = np.cos(angle)
        table[:KERNEL, LANES + copy * size : LANES + (copy + 1) * size] = np.sin(angle)
    return stack_split(table, 0)


def taps_y(level):
    size = PERIOD[level]
    angle = 2 * np.pi * np.arange(size)[:, None] * (np.arange(16) - HALF)[None, :] / size
    keep = (np.arange(16) < KERNEL)[None, :]
    c, s = np.cos(angle) * keep, np.sin(angle) * keep
    return stack_split(np.block([[c, -s], [s, c]]), 1)


def tables():
    xy = transfer_xy()
    z = transfer_z()
    bf16 = ml_dtypes.bfloat16
    stacked = [xy.astype(bf16)]
    for level in range(LEVELS):
        stacked += [z_forward(level), z_inverse(level), y_forward(level), y_inverse(level), taps_z(level), taps_y(level)]
    places, first = [], 0
    for table in stacked:
        places.append((slice(first, first + table.shape[0]), slice(0, table.shape[1])))
        first += table.shape[0]
    whole = np.zeros((first, 2 * LANES), bf16)
    for place, table in zip(places, stacked):
        whole[place] = table
    return [xy.T.astype(bf16), np.concatenate([z, z], axis=0).astype(bf16), whole], places


class Part:
    def __init__(self, ref, place):
        self.ref, self.place = ref, place

    def __getitem__(self, _):
        return self.ref[self.place]


def split(value):
    high = value.astype(jnp.bfloat16)
    return high, (value - high.astype(jnp.float32)).astype(jnp.bfloat16)


def matmul(a, b):
    return jnp.dot(a, b, preferred_element_type=jnp.float32)


def matmul_nt(a, b):
    return lax.dot_general(a, b, (((1,), (1,)), ((), ())), preferred_element_type=jnp.float32)


def rows_iota(rows, columns):
    return lax.broadcasted_iota(jnp.int32, (rows, columns), 0)


def bases(cell):
    return cell // (CY * NZ), (cell // NZ) % CY, cell % NZ


def wide(value, dtype):
    return jnp.broadcast_to(value, (16, value.shape[1])).astype(dtype)


def row_patterns(columns):
    row = rows_iota(16, columns)
    patterns = []
    for tile in range(TOP_ROWS // 16):
        xs, ys = [], []
        for part in range(2):
            first = tile * 16 + part * 8
            if first < LAYERS * CY:
                xs.append(first // CY)
                ys.append(row + (first % CY - 8 * part))
            else:
                at = row + (first - LAYERS * CY - 8 * part)
                xs.append(jnp.where(at < LAYERS, at, -9))
                ys.append(jnp.full_like(row, CY))
        if all(isinstance(x, int) for x in xs) and xs[0] == xs[1]:
            x = jnp.full((16, columns), xs[0], jnp.int16)
        else:
            x = jnp.where(row < 8, xs[0], xs[1]).astype(jnp.int16)
        patterns.append((x, jnp.where(row < 8, ys[0], ys[1]).astype(jnp.int16)))
    return patterns


def spread_sides(count_ref, cell_ref, frac_ref, charge_ref, start, patterns, row_z):
    bf16, i16 = jnp.bfloat16, jnp.int16
    part = slice(start, start + SPREAD_PART)
    base_x, base_y, base_z = bases(cell_ref[0, :, part])
    f = [frac_ref[k, 0, :, part] for k in range(3)]
    slot = start + lax.broadcasted_iota(jnp.int32, (1, SPREAD_PART), 1)
    charge = jnp.where(slot < count_ref[...], charge_ref[0, :, part], 0.0)
    nothing = jnp.zeros((16, SPREAD_PART), bf16)
    x_at, x_next = wide(base_x, i16), wide(base_x + 1, i16)
    y_at, y_next = wide(base_y, i16), wide(base_y + 1, i16)
    corner = {}
    for a, along_x in enumerate((charge * (1.0 - f[0]), charge * f[0])):
        for b, along_y in enumerate((1.0 - f[1], f[1])):
            high, low = split(along_x * along_y)
            corner[a, b] = (wide(high, bf16), wide(low, bf16))
    highs, lows = [], []
    known = {}
    for tile, (xs, ys) in enumerate(patterns):
        key = tile % 3 if (tile + 1) * 16 <= LAYERS * CY else tile
        if key not in known:
            here, above = ys == y_at, ys == y_next
            known[key] = [
                [jnp.where(here, corner[a, 0][k], jnp.where(above, corner[a, 1][k], nothing)) for k in range(2)]
                for a in range(2)
            ]
        here, above = xs == x_at, xs == x_next
        for k, target in enumerate((highs, lows)):
            target.append(jnp.where(here, known[key][0][k], jnp.where(above, known[key][1][k], nothing)))
    weights = [[wide(piece, bf16) for piece in split(value)] for value in (1.0 - f[2], f[2])]
    sides = ([], [])
    z_at, z_next = wide(base_z, i16), wide((base_z + 1) & (NZ - 1), i16)
    for rows in row_z:
        here, above = rows == z_at, rows == z_next
        for k in range(2):
            sides[k].append(jnp.where(here, weights[0][k], jnp.where(above, weights[1][k], nothing)))
    return [jnp.concatenate(pieces, axis=0) for pieces in (highs, lows, *sides)]


def spread(count_ref, cell_ref, frac_ref, charge_ref, grid_ref):
    slots = cell_ref.shape[-1]
    patterns = row_patterns(SPREAD_PART)
    row_z = [(rows_iota(16, SPREAD_PART) + first).astype(jnp.int16) for first in range(0, NZ, 16)]
    parts = [
        spread_sides(count_ref, cell_ref, frac_ref, charge_ref, start, patterns, row_z)
        for start in range(0, slots, SPREAD_PART)
    ]
    top_high, top_low, z_high, z_low = [jnp.concatenate(pieces, axis=1) for pieces in zip(*parts)]
    both = matmul_nt(top_high, jnp.concatenate([z_high, z_low], axis=0))
    value = both[:, :LANES] + both[:, LANES:] + matmul_nt(top_low, z_high)
    layers = LAYERS * CY
    grid_ref[:LAYERS] = value[:layers].reshape(LAYERS, CY, LANES)
    grid_ref[LAYERS] = jnp.zeros((CY, LANES), jnp.float32)
    for x in range(LAYERS):
        grid_ref[LAYERS, strip_row(x) : strip_row(x) + 1, :] = value[layers + x : layers + x + 1]


def lane_iota():
    return lax.broadcasted_iota(jnp.int32, (1, 1, LANES), 2)


def restrict(grid_ref, down_ref, down_z_ref, middle_ref, low_ref):
    high, low = split(grid_ref[...].reshape(GRID_ROWS, LANES))
    both = matmul(down_ref[...], jnp.concatenate([high, low], axis=1))
    high, low = split(both[:, :LANES] + both[:, LANES:])
    value = matmul(jnp.concatenate([high, low], axis=1), down_z_ref[...])
    middle = value[: LOW_ROWS[0]].reshape(BX[1] + 1, ROWS[1], LANES)
    coarse = value[LOW_ROWS[0] :].reshape(BX[2] + 1, ROWS[2], LANES)
    twice = jnp.concatenate([coarse, coarse], axis=1)
    first = BX[1] - BX[2]
    mine = lane_iota() < FIRST_LANE[2]
    middle_ref[:first] = middle[:first]
    middle_ref[first:] = jnp.where(mine, middle[first:], twice)
    low_ref[...] = jnp.where(mine, middle[: BX[2] + 1], twice)


def build_taps(level, kernel_ref, padded_ref, z_ref, y_ref, real_ref, imag_ref):
    padded_ref[...] = jnp.zeros_like(padded_ref)
    padded_ref[:, :KERNEL, :KERNEL] = kernel_ref[...]
    along_z = matmul(three(padded_ref[...].reshape(KERNEL * 16, LANES), 1), z_ref[...])
    size = PERIOD[level]
    for shift in range(0, KERNEL, 2):
        pieces = []
        for one in range(shift, min(shift + 2, KERNEL)):
            rows = along_z[one * 16 : (one + 1) * 16]
            pieces.append(three(jnp.concatenate([rows[:, :LANES], rows[:, LANES:]], axis=0), 0))
        both = matmul(y_ref[...], jnp.concatenate(pieces, axis=1))
        for k in range(len(pieces)):
            real_ref[shift + k] = both[:size, k * LANES : (k + 1) * LANES]
            imag_ref[shift + k] = both[size:, k * LANES : (k + 1) * LANES]


def three(value, axis):
    high, low = split(value)
    return jnp.concatenate([high, low, high], axis=axis)


def add_spectra(level, source_ref, slots, taps, tables, along_z_ref, spectrum_ref, sums_ref, fresh):
    forward_z, _, forward_y, _ = tables
    size, pair = PERIOD[level], PAIR[level]
    used = len(slots)
    flat = source_ref[...].reshape(used * size, LANES)
    half = (used // 2 + 1) * size
    for rows in (slice(0, half), slice(half, used * size)):
        along_z_ref[rows] = matmul(three(flat[rows], 1), forward_z[...])

    def part(layer, which):
        slot = slots[layer]
        return along_z_ref[slot * size : (slot + 1) * size, which * LANES : (which + 1) * LANES]

    def combined(layer):
        if layer not in slots:
            return [-part(layer + pair, 1), part(layer + pair, 0)]
        if layer + pair not in slots:
            return [part(layer, 0), part(layer, 1)]
        return [part(layer, 0) - part(layer + pair, 1), part(layer, 1) + part(layer + pair, 0)]

    present = [layer for layer in range(SPECTRA[level]) if layer in slots or layer + pair in slots]
    for first in range(0, len(present), 2):
        group = present[first : first + 2]
        pieces = [three(jnp.concatenate(combined(layer), axis=0), 0) for layer in group]
        both = matmul(forward_y[...], jnp.concatenate(pieces, axis=1))
        for k, layer in enumerate(group):
            spectrum_ref[layer] = both[:, k * LANES : (k + 1) * LANES]
    real_ref, imag_ref = taps
    for out in range(pair):
        for tile in range(0, size, 8):
            rows, rest = slice(tile, tile + 8), slice(size + tile, size + tile + 8)
            real = jnp.zeros((8, LANES), jnp.float32) if fresh else sums_ref[out, rows]
            imag = jnp.zeros((8, LANES), jnp.float32) if fresh else sums_ref[out, rest]
            for shift in range(KERNEL):
                if out + shift in present:
                    a, b = spectrum_ref[out + shift, rows], spectrum_ref[out + shift, rest]
                    c, s = real_ref[shift, rows], imag_ref[shift, rows]
                    real = real + a * c - b * s
                    imag = imag + a * s + b * c
            sums_ref[out, rows] = real
            sums_ref[out, rest] = imag


def from_spectra(level, tables, sums_ref):
    _, inverse_z, _, inverse_y = tables
    pair, rows = PAIR[level], ROWS[level]
    lines = []
    for first in range(0, pair, 2):
        group = range(first, min(first + 2, pair))
        both = matmul(inverse_y[...], jnp.concatenate([three(sums_ref[out], 0) for out in group], axis=1))
        for k in range(len(group)):
            line = both[:rows, k * LANES : (k + 1) * LANES]
            if level == 0:
                line = jnp.concatenate([line, both[rows:, k * LANES : (k + 1) * LANES]], axis=1)
            lines.append(line)
    half = pair // 2 + 1
    values = []
    for group in (lines[:half], lines[half:]):
        value = matmul(three(jnp.concatenate(group, axis=0), 1), inverse_z[...])
        values += [value[k * rows : (k + 1) * rows] for k in range(len(group))]
    layers = [value[:, :LANES] for value in values] + [value[:, LANES:] for value in values]
    return layers[: BX[level] + 1]


GRID, MIDDLE, LOW, LANDED = range(4)


def side(step, size):
    return {-1: (0, REACH), 0: (0, size + 1), 1: (size - HALF, REACH)}[step]


class Message:
    def __init__(self, kind, dx, dy, source, layers, rows, relayed=None):
        self.kind, self.dx, self.dy = kind, dx, dy
        self.source, self.layers, self.rows, self.relayed = source, layers, rows, relayed
        self.hop = (dx, dy) if relayed is None else (0, dy)
        self.local = (layers, rows)
        if relayed is not None:
            self.local = ((0, layers[1]), (rows[0] - relayed.rows[0], rows[1]))


def plan_messages():
    near, far, face, strip = {}, {}, {}, {}
    top, bottom = (CY - 8, 8), (0, 8)
    for dx, layer in ((-2, 0), (2, BX[1])):
        far[dx, 0] = Message("far", dx, 0, LOW if dx < 0 else MIDDLE, (layer, 1), (0, 8))
    for dx in (-1, 1):
        near[dx, 0] = Message("near", dx, 0, LOW if dx < 0 else MIDDLE, side(dx, BX[1]), (0, ROWS[1]))
        strip[dx, 0] = Message("strip", dx, 0, GRID, (CX + 1, 1), bottom if dx < 0 else top)
        for name, rows in (("top", top), ("bottom", bottom), ("centre", (8, CY - 16))):
            face[dx, name] = Message("face", dx, 0, GRID, side(dx, BX[0]), rows)
    for dy in (-1, 1):
        rows = bottom if dy < 0 else (ROWS[1] - 8, 8)
        near[0, dy] = Message("near", 0, dy, MIDDLE, side(0, BX[1]), rows)
        face[0, dy] = Message("face", 0, dy, GRID, side(0, BX[0]), bottom if dy < 0 else top)
        for dx in (-2, 2):
            far[dx, dy] = Message("far", dx, dy, LANDED, far[dx, 0].layers, (0, 8), far[dx, 0])
        for dx in (-1, 1):
            near[dx, dy] = Message("near", dx, dy, LANDED, near[dx, 0].layers, rows, near[dx, 0])
            first = face[dx, "bottom" if dy < 0 else "top"]
            face[dx, dy] = Message("face", dx, dy, LANDED, first.layers, first.rows, first)
    strip[0, 1] = Message("strip", 0, 1, GRID, (CX + 1, 1), (0, CY))
    for dx in (-1, 1):
        strip[dx, 1] = Message("strip", dx, 1, LANDED, (CX + 1, 1), strip[dx, 0].rows, strip[dx, 0])
    sides = (-1, 1)
    first = [near[dx, 0] for dx in sides]
    first += [face[dx, name] for name in ("top", "bottom") for dx in sides] + [strip[dx, 0] for dx in sides]
    first += [near[0, dy] for dy in sides] + [far[dx, 0] for dx in (-2, 2)]
    first += [face[0, dy] for dy in sides] + [strip[0, 1]] + [face[dx, "centre"] for dx in sides]
    second = [near[dx, dy] for dx in sides for dy in sides] + [far[dx, dy] for dx in (-2, 2) for dy in sides]
    second += [face[dx, dy] for dy in (1, -1) for dx in sides] + [strip[dx, 1] for dx in sides]
    return first, second


FIRST, SECOND = plan_messages()
PLAN = FIRST + SECOND


def add_rows(window_ref, layer, first, piece):
    rows = slice(first, first + piece.shape[-2])
    layers = slice(layer, layer + piece.shape[0])
    window_ref[layers, rows, :] = window_ref[layers, rows, :] + piece


def add_level_rows(window_ref, level, layer, dy, piece):
    size = BY[level]
    if dy == 0:
        add_rows(window_ref, layer, 0, piece[:, : size + 1])
    elif dy < 0:
        add_rows(window_ref, layer, size, piece[:, :REACH])
    else:
        base = piece.shape[-2] - 8 if piece.shape[-2] > 8 else (size // 8) * 8
        first = size - HALF - base
        add_rows(window_ref, layer, PERIOD[level] - HALF, piece[:, first : first + HALF])
        add_rows(window_ref, layer, 0, piece[:, first + HALF : first + HALF + 1])


def add_low(windows, message, landed):
    dx, dy, first = message.dx, message.dy, message.layers[0]
    if message.kind == "far":
        layer = HALF + (0 if dx < 0 else BX[2]) - dx * BX[2]
        add_level_rows(windows[2], 2, layer, dy, landed[...])
        return
    add_level_rows(windows[1], 1, HALF + first - dx * BX[1], dy, landed[...])
    ride = BX[1] - BX[2] if dx == 0 else 0
    add_level_rows(windows[2], 2, HALF - dx * BX[2], dy, landed[ride : ride + BX[2] + 1, :8, :])


def add_fine(window_ref, message, landed):
    dx, dy, rows = message.dx, message.dy, message.rows
    offset = {-1: REACH, 0: 0, 1: HALF - BX[0]}[dx]
    if message.kind == "strip":
        low, size = side(dx, BX[0])
        target = CY if dy == 0 else 0
        for k in range(size):
            place = strip_row(low + k) - rows[0]
            layer = offset + low + k
            window_ref[layer, target : target + 1, :] = (
                window_ref[layer, target : target + 1, :] + landed[0, place : place + 1, :]
            )
        return
    first, count = message.layers
    layers = slice(offset + first, offset + first + count)
    row = lax.broadcasted_iota(jnp.int32, (1, 8, LANES), 1)
    value = landed[...]
    at = slice(rows[0], rows[0] + rows[1])
    if dy < 0:
        at, value = slice(CY, CY + 8), jnp.where(row < REACH, value, 0.0)
    elif dy > 0:
        at, value = slice(PERIOD[0] - 8, PERIOD[0]), jnp.where(row >= 8 - HALF, value, 0.0)
    window_ref[layers, at, :] = window_ref[layers, at, :] + value


def grid_kernel(sizes, n_tables, places, *refs):
    count_ref, cell_ref, frac_ref, charge_ref = refs[:4]
    kernels = refs[4:7]
    table_sources = refs[7 : 7 + n_tables]
    out_ref = refs[7 + n_tables]
    scratch = list(refs[8 + n_tables :])

    def take(count):
        taken = scratch[:count]
        del scratch[:count]
        return taken

    grid_ref, middle_ref, low_ref, padded_ref = take(4)
    table_refs = take(n_tables)
    windows, reals, imags, along_z, spectra, sums = take(3), take(3), take(3), take(3), take(3), take(3)
    (edges_ref,) = take(1)
    landed = take(len(PLAN))
    send_sem, recv_sem, table_sem = take(3)

    me = (lax.axis_index("gx"), lax.axis_index("gy"))

    def device(dx, dy):
        return (lax.rem(me[0] + dx + sizes[0], sizes[0]), lax.rem(me[1] + dy + sizes[1], sizes[1]))

    barrier = pltpu.get_barrier_semaphore()
    around = sorted({message.hop for message in PLAN})
    for dx, dy in around:
        pl.semaphore_signal(barrier, inc=1, device_id=device(dx, dy), device_id_type=MESH)
    loads = [
        pltpu.make_async_copy(source, target, table_sem.at[index])
        for index, (source, target) in enumerate(zip(table_sources, table_refs))
    ]
    for load in loads:
        load.start()

    spread(count_ref, cell_ref, frac_ref, charge_ref, grid_ref)
    for load in loads[:2]:
        load.wait()
    down_ref, down_z_ref, stacked_ref = table_refs
    restrict(grid_ref, down_ref, down_z_ref, middle_ref, low_ref)
    pl.semaphore_wait(barrier, len(around))

    sources = (grid_ref, middle_ref, low_ref)
    copies = {}
    for index, message in enumerate(PLAN):
        relayed = message.relayed
        source = sources[message.source] if relayed is None else landed[PLAN.index(relayed)]
        (first, size), (low, rows) = message.local
        copies[message] = pltpu.make_async_remote_copy(
            src_ref=source.at[pl.ds(first, size), pl.ds(low, rows)],
            dst_ref=landed[index],
            send_sem=send_sem.at[index],
            recv_sem=recv_sem.at[index],
            device_id=device(*message.hop),
            device_id_type=MESH,
        )
    arrived = set()

    def arrive(message):
        if message not in arrived:
            arrived.add(message)
            copies[message].wait_recv()

    for message in FIRST:
        copies[message].start()
    loads[2].wait()
    up_ref, *parts = [Part(stacked_ref, place) for place in places]

    level_tables = [parts[6 * level : 6 * level + 6] for level in range(LEVELS)]
    for level in (2, 1, 0):
        build_taps(level, kernels[level], padded_ref, *level_tables[level][4:], reals[level], imags[level])

    for level in range(LEVELS):
        windows[level][...] = jnp.zeros_like(windows[level])
    edges_ref[...] = jnp.zeros_like(edges_ref)
    windows[0][:, :CY, :] = grid_ref[: CX + 1]
    for x in range(CX + 1):
        windows[0][x, CY : CY + 1, :] = grid_ref[CX + 1, strip_row(x) : strip_row(x) + 1, :]
    windows[1][HALF : HALF + BX[1] + 1, : ROWS[1], :] = middle_ref[...]
    windows[2][HALF : HALF + BX[2] + 1, : ROWS[2], :] = low_ref[:, : ROWS[2], :]

    for message in SECOND:
        if message.kind in ('near', 'far'):
            arrive(message.relayed)
            copies[message].start()
    def run(level, source_ref, layers, fresh):
        slots = {layer: slot for slot, layer in enumerate(layers)}
        taps = (reals[level], imags[level])
        tables = level_tables[level][:4]
        add_spectra(level, source_ref, slots, taps, tables, along_z[level], spectra[level], sums[level], fresh)

    fine = [message for message in PLAN if message.kind in ("face", "strip")]
    for message in fine:
        if message.dx == 0:
            arrive(message)
            add_fine(windows[0], message, landed[PLAN.index(message)])
    run(0, windows[0], range(HALF, HALF + CX + 1), True)
    for message in SECOND:
        if message.kind not in ('near', 'far'):
            arrive(message.relayed)
            copies[message].start()
    for message in PLAN:
        if message.kind in ("near", "far"):
            arrive(message)
            add_low(windows, message, landed[PLAN.index(message)])
    below = []
    for level in (1, 2):
        run(level, windows[level], range(BX[level] + 1 + 2 * HALF), True)
        below += from_spectra(level, level_tables[level][:4], sums[level])
    high, low = split(jnp.concatenate(below, axis=0))
    both = matmul(up_ref[...], jnp.concatenate([high, low], axis=1))
    out_ref[...] = (both[:, :LANES] + both[:, LANES:]).reshape(out_ref.shape)
    for message in PLAN:
        copies[message].wait_send()
    for message in fine:
        if message.dx != 0:
            arrive(message)
            add_fine(edges_ref, message, landed[PLAN.index(message)])
    last = CX + 1 + 2 * HALF
    run(0, edges_ref, [*range(REACH), *range(last - REACH, last)], False)
    layers = from_spectra(0, level_tables[0][:4], sums[0])
    for x in range(CX + 1):
        out_ref[x] = out_ref[x] + layers[x][:CY]
        at = slice(strip_row(x), strip_row(x) + 1)
        out_ref[CX + 1, at, :] = out_ref[CX + 1, at, :] + layers[x][CY : CY + 1]


def force_kernel(count_ref, cell_ref, frac_ref, charge_ref, grid_ref, potential_ref, forces_ref, left_ref):
    slots = cell_ref.shape[-1]
    potential_ref[...] = grid_ref[:CX]
    forces_ref[...] = jnp.zeros_like(forces_ref)
    left_ref[...] = jnp.concatenate(split(grid_ref[...].reshape(GRID_ROWS, LANES)), axis=1)
    count = jnp.max(count_ref[...].astype(jnp.float32)).astype(jnp.int32)

    def pick(values, base):
        width = CX // 2
        while width >= 1:
            bit = (base & width) != 0
            values = [jnp.where(bit, values[width + k], values[k]) for k in range(width + 1)]
            width //= 2
        return values

    def chunk(index):
        part = pl.ds(pl.multiple_of(index * FORCE_CHUNK, FORCE_CHUNK), FORCE_CHUNK)
        base_x, base_y, base_z = bases(cell_ref[0, :, part])
        row = rows_iota(16, FORCE_CHUNK)
        one, nothing = [jnp.full((16, FORCE_CHUNK), value, jnp.bfloat16) for value in (1.0, 0.0)]
        found = []
        for at_z in (base_z, (base_z + 1) & (NZ - 1)):
            target = wide(at_z, jnp.int16)
            chosen = [jnp.where((row + z).astype(jnp.int16) == target, one, nothing) for z in range(0, NZ, 16)]
            found.append(matmul(left_ref[...], jnp.concatenate(chosen * 2, axis=0)))
        shape = (8, FORCE_CHUNK)
        f = [jnp.broadcast_to(frac_ref[k, 0, :, part], shape) for k in range(3)]
        slot = index * FORCE_CHUNK + lax.broadcasted_iota(jnp.int32, (1, FORCE_CHUNK), 1)
        charge = jnp.where(slot < count, charge_ref[0, :, part], 0.0)
        base_x = jnp.broadcast_to(base_x, shape)
        base_y = jnp.broadcast_to(base_y, shape)
        row = rows_iota(*shape)
        across, along, slope = [jnp.zeros(shape, jnp.float32) for _ in range(3)]
        for tile in range(CY // 8):
            ends = []
            for values in found:
                rows = [values[x * CY + tile * 8 : x * CY + tile * 8 + 8] for x in range(CX + 1)]
                ends.append(pick(rows, base_x))
            rise = [ends[1][k] - ends[0][k] for k in range(2)]
            level = [ends[0][k] + f[2] * rise[k] for k in range(2)]
            step_x = level[1] - level[0]
            lower, upper = row + tile * 8 == base_y, row + tile * 8 == base_y + 1
            weight = jnp.where(lower, 1.0 - f[1], jnp.where(upper, f[1], 0.0))
            sign = jnp.where(lower, -1.0, jnp.where(upper, 1.0, 0.0))
            across = across + weight * step_x
            along = along + sign * (level[0] + f[0] * step_x)
            slope = slope + weight * (rise[0] + f[0] * (rise[1] - rise[0]))
        ends = []
        for values in found:
            low, high = [jnp.zeros(shape, jnp.float32) for _ in range(2)]
            for tile in range(CY // 8):
                value = values[(CX + 1) * CY + tile * 8 : (CX + 1) * CY + tile * 8 + 8]
                layer = row + (tile * 8 if tile < 2 else 12)
                if tile == 1:
                    layer = jnp.where(layer < 12, layer, -5)
                low = jnp.where(layer == base_x, value, low)
                high = jnp.where(layer == base_x + 1, value, high)
            ends.append((low, high))
        edge = base_y == CY - 1
        weight = jnp.where(edge, f[1], 0.0)
        rise = [ends[1][k] - ends[0][k] for k in range(2)]
        level = [ends[0][k] + f[2] * rise[k] for k in range(2)]
        across = across + weight * (level[1] - level[0])
        along = along + jnp.where(edge, level[0] + f[0] * (0.0 - level[0]) + f[0] * level[1], 0.0)
        slope = slope + weight * (rise[0] + f[0] * (0.0 - rise[0]) + f[0] * rise[1])
        for k, value in enumerate((across, along, slope)):
            forces_ref[k, 0, :, part] = -charge * jnp.sum(value, axis=0, keepdims=True)

    def step(index, carry):
        for k in range(FORCE_UNROLL):
            chunk(index * FORCE_UNROLL + k)
        return carry

    width = FORCE_CHUNK * FORCE_UNROLL
    lax.fori_loop(0, jnp.minimum(pl.cdiv(count, width), slots // width), step, 0)


VMEM = pl.BlockSpec(memory_space=pltpu.VMEM)
ANY = pl.BlockSpec(memory_space=pl.ANY)


def solution(mesh):
    sizes = (mesh.shape["gx"], mesh.shape["gy"])
    constants, places = tables()

    def per_device(atom_cell, atom_frac, atom_charge, atom_count, fine_kernel, middle_kernel, coarse_kernel):
        slots = atom_cell.shape[-1]
        f32 = jnp.float32
        grid = (CX + 2, CY, LANES)
        scratch = [
            pltpu.VMEM(grid, f32),
            pltpu.VMEM((BX[1] + 1, ROWS[1], LANES), f32),
            pltpu.VMEM((BX[2] + 1, ROWS[1], LANES), f32),
            pltpu.VMEM((KERNEL, 16, LANES), f32),
        ]
        scratch += [pltpu.VMEM(table.shape, jnp.dtype(table.dtype)) for table in constants]
        scratch += [pltpu.VMEM((WINDOW[k], PERIOD[k], LANES), f32) for k in range(LEVELS)]
        scratch += [pltpu.VMEM((KERNEL, PERIOD[k], LANES), f32) for k in range(LEVELS)] * 2
        scratch += [pltpu.VMEM((WINDOW[k] * PERIOD[k], 2 * LANES), f32) for k in range(LEVELS)]
        scratch += [pltpu.VMEM((SPECTRA[k], 2 * PERIOD[k], LANES), f32) for k in range(LEVELS)]
        scratch += [pltpu.VMEM((PAIR[k], 2 * PERIOD[k], LANES), f32) for k in range(LEVELS)]
        scratch += [pltpu.VMEM((2 * REACH, PERIOD[0], LANES), f32)]
        scratch += [pltpu.VMEM((message.layers[1], message.rows[1], LANES), f32) for message in PLAN]
        scratch += [pltpu.SemaphoreType.DMA((len(PLAN),))] * 2 + [pltpu.SemaphoreType.DMA((len(constants),))]
        extended = pl.pallas_call(
            lambda *refs: grid_kernel(sizes, len(constants), places, *refs),
            out_shape=pltpu.VMEM(grid, f32),
            in_specs=[VMEM] * 7 + [ANY] * len(constants),
            out_specs=VMEM,
            scratch_shapes=scratch,
            compiler_params=pltpu.CompilerParams(collective_id=0, has_side_effects=True),
            name="grid",
        )(
            atom_count,
            atom_cell,
            atom_frac,
            atom_charge,
            fine_kernel,
            middle_kernel,
            coarse_kernel,
            *[jnp.asarray(table) for table in constants],
        )
        potential, forces = pl.pallas_call(
            force_kernel,
            out_shape=(jax.ShapeDtypeStruct((CX, CY, NZ), f32), jax.ShapeDtypeStruct((3, 1, 1, slots), f32)),
            in_specs=[VMEM] * 5,
            out_specs=(VMEM, VMEM),
            scratch_shapes=[pltpu.VMEM((GRID_ROWS, 2 * LANES), jnp.bfloat16)],
            name="forces",
        )(atom_count, *[pltpu.with_memory_space_constraint(x, pltpu.VMEM) for x in (atom_cell, atom_frac, atom_charge, extended)])
        return potential, forces

    return jax.shard_map(
        per_device,
        mesh=mesh,
        in_specs=(
            P("gx", "gy", None),
            P(None, "gx", "gy", None),
            P("gx", "gy", None),
            P("gx", "gy"),
            P(),
            P(),
            P(),
        ),
        out_specs=(P("gx", "gy", None), P(None, "gx", "gy", None)),
        check_vma=False,
    )
```

```python
import jax
import jax.numpy as jnp
import ml_dtypes
import numpy as np
from jax import lax
from jax.experimental import pallas as pl
from jax.experimental.pallas import tpu as pltpu
from jax.sharding import PartitionSpec as P

CX = 16
CY = 24
NZ = 128
KERNEL = 9
HALF = KERNEL // 2
REACH = HALF + 1
LANES = 128
LAYERS = CX + 1
TOP_ROWS = -(-LAYERS * (CY + 1) // 16) * 16
FORCE_CHUNK = 256
SPREAD_PART = 512
FORCE_UNROLL = 8
LEVELS = 3
MESH = pl.DeviceIdType.MESH

BX = tuple(CX >> k for k in range(LEVELS))
BY = tuple(CY >> k for k in range(LEVELS))
ZS = tuple(NZ >> k for k in range(LEVELS))
PAIR = tuple((size + 2) // 2 for size in BX)
PERIOD = tuple(-(-(size + 1 + 2 * HALF) // 8) * 8 for size in BY)
WINDOW = (CX + 1, *(size + 1 + 2 * HALF for size in BX[1:]))
SPECTRA = tuple(size + 2 * HALF for size in PAIR)
ROWS = (32, 16, 8)
FIRST_LANE = (0, 0, ZS[1])
GRID_ROWS = (CX + 2) * CY
LOW_ROWS = ((BX[1] + 1) * ROWS[1], (BX[2] + 1) * ROWS[2])


def strip_row(x):
    return x if x < 12 else x + 4


def np_hat(distance):
    return np.maximum(1.0 - np.abs(distance), 0.0)


def np_ring_hat(distance, period):
    distance = np.abs(distance)
    return np.maximum(1.0 - np.minimum(distance, period - distance), 0.0)


def np_split(value):
    high = value.astype(np.float32).astype(ml_dtypes.bfloat16)
    low = (value - high.astype(np.float64)).astype(ml_dtypes.bfloat16)
    return high, low


def fine_places():
    xs, ys = np.full(GRID_ROWS, -1e6), np.full(GRID_ROWS, -1e6)
    for x in range(CX + 1):
        for y in range(CY):
            xs[x * CY + y], ys[x * CY + y] = x, y
        xs[(CX + 1) * CY + strip_row(x)], ys[(CX + 1) * CY + strip_row(x)] = x, CY
    return xs, ys


def transfer_xy():
    xs, ys = fine_places()
    parts = []
    for level in (1, 2):
        scale = 0.5**level
        layers = np.repeat(np.arange(BX[level] + 1), ROWS[level])
        rows = np.tile(np.arange(ROWS[level]), BX[level] + 1)
        weight = np_hat(xs[:, None] * scale - layers[None, :]) * np_hat(ys[:, None] * scale - rows[None, :])
        parts.append(weight * (rows <= BY[level])[None, :])
    return np.concatenate(parts, axis=1)


def transfer_z():
    weight = np.zeros((NZ, LANES))
    for level in (1, 2):
        z, low = np.arange(NZ)[:, None], np.arange(ZS[level])[None, :]
        weight[:, FIRST_LANE[level] : FIRST_LANE[level] + ZS[level]] = np_ring_hat(z * 0.5**level - low, ZS[level])
    return weight


def z_forward(level):
    size = ZS[level]
    angle = 2 * np.pi * np.arange(size)[:, None] * np.arange(size)[None, :] / size
    c, s = np.cos(angle), np.sin(angle)
    table = np.zeros((LANES, 2 * LANES))
    first = FIRST_LANE[level]
    if level == 0:
        table[:, :LANES], table[:, LANES:] = c, -s
    else:
        rows = slice(first, first + size)
        table[rows, :size], table[rows, size : 2 * size] = c, -s
        table[rows, LANES : LANES + size], table[rows, LANES + size : LANES + 2 * size] = -s, -c
    high, low = np_split(table)
    return np.concatenate([high, high, low], axis=0)


def z_inverse(level):
    size = ZS[level]
    angle = 2 * np.pi * np.arange(size)[:, None] * np.arange(size)[None, :] / size
    raised = np_ring_hat(np.arange(NZ)[None, :] * 0.5**level - np.arange(size)[:, None], size)
    c, s = np.cos(angle) @ raised / size, np.sin(angle) @ raised / size
    table = np.concatenate([np.concatenate([c, s], axis=1), np.concatenate([-s, c], axis=1)], axis=0)
    rows = 2 * LANES if level == 0 else LANES
    table = np.concatenate([table, np.zeros((rows - table.shape[0], 2 * LANES))], axis=0)
    high, low = np_split(table)
    return np.concatenate([high, high, low], axis=0)


def y_forward(level):
    size = PERIOD[level]
    angle = 2 * np.pi * np.arange(size)[:, None] * np.arange(size)[None, :] / size
    c, s = np.cos(angle), np.sin(angle)
    high, low = np_split(np.block([[c, s], [-s, c]]))
    return np.concatenate([high, high, low], axis=1)


def y_inverse(level):
    size = PERIOD[level]
    angle = 2 * np.pi * np.arange(ROWS[level])[:, None] * np.arange(size)[None, :] / size
    keep = (np.arange(ROWS[level]) <= BY[level])[:, None]
    c, s = np.cos(angle) * keep / size, np.sin(angle) * keep / size
    table = np.block([[c, -s], [s, c]]) if level == 0 else np.block([[c, -s]])
    if table.shape[0] < 16:
        table = np.concatenate([table, np.zeros((16 - table.shape[0], 2 * size))], axis=0)
    high, low = np_split(table)
    return np.concatenate([high, high, low], axis=1)


def stack_split(table, axis):
    high, low = np_split(table)
    return np.concatenate([high, high, low], axis=axis)


def taps_z(level):
    size = ZS[level]
    angle = 2 * np.pi * (np.arange(KERNEL) - HALF)[:, None] * np.arange(size)[None, :] / size
    table = np.zeros((LANES, 2 * LANES))
    for copy in range(1 if level == 0 else 2):
        table[:KERNEL, copy * size : (copy + 1) * size] = np.cos(angle)
        table[:KERNEL, LANES + copy * size : LANES + (copy + 1) * size] = np.sin(angle)
    return stack_split(table, 0)


def taps_y(level):
    size = PERIOD[level]
    angle = 2 * np.pi * np.arange(size)[:, None] * (np.arange(16) - HALF)[None, :] / size
    keep = (np.arange(16) < KERNEL)[None, :]
    c, s = np.cos(angle) * keep, np.sin(angle) * keep
    return stack_split(np.block([[c, -s], [s, c]]), 1)


def tables():
    xy = transfer_xy()
    z = transfer_z()
    bf16 = ml_dtypes.bfloat16
    stacked = [xy.astype(bf16)]
    for level in range(LEVELS):
        stacked += [z_forward(level), z_inverse(level), y_forward(level), y_inverse(level), taps_z(level), taps_y(level)]
    places, first = [], 0
    for table in stacked:
        places.append((slice(first, first + table.shape[0]), slice(0, table.shape[1])))
        first += table.shape[0]
    whole = np.zeros((first, 2 * LANES), bf16)
    for place, table in zip(places, stacked):
        whole[place] = table
    return [xy.T.astype(bf16), np.concatenate([z, z], axis=0).astype(bf16), whole], places


class Part:
    def __init__(self, ref, place):
        self.ref, self.place = ref, place

    def __getitem__(self, _):
        return self.ref[self.place]


def split(value):
    high = value.astype(jnp.bfloat16)
    return high, (value - high.astype(jnp.float32)).astype(jnp.bfloat16)


def matmul(a, b):
    return jnp.dot(a, b, preferred_element_type=jnp.float32)


def matmul_nt(a, b):
    return lax.dot_general(a, b, (((1,), (1,)), ((), ())), preferred_element_type=jnp.float32)


def rows_iota(rows, columns):
    return lax.broadcasted_iota(jnp.int32, (rows, columns), 0)


def bases(cell):
    return cell // (CY * NZ), (cell // NZ) % CY, cell % NZ


def wide(value, dtype):
    return jnp.broadcast_to(value, (16, value.shape[1])).astype(dtype)


def row_patterns(columns):
    row = rows_iota(16, columns)
    patterns = []
    for tile in range(TOP_ROWS // 16):
        xs, ys = [], []
        for part in range(2):
            first = tile * 16 + part * 8
            if first < LAYERS * CY:
                xs.append(first // CY)
                ys.append(row + (first % CY - 8 * part))
            else:
                at = row + (first - LAYERS * CY - 8 * part)
                xs.append(jnp.where(at < LAYERS, at, -9))
                ys.append(jnp.full_like(row, CY))
        if all(isinstance(x, int) for x in xs) and xs[0] == xs[1]:
            x = jnp.full((16, columns), xs[0], jnp.int16)
        else:
            x = jnp.where(row < 8, xs[0], xs[1]).astype(jnp.int16)
        patterns.append((x, jnp.where(row < 8, ys[0], ys[1]).astype(jnp.int16)))
    return patterns


def spread_sides(count_ref, cell_ref, frac_ref, charge_ref, start, patterns, row_z):
    bf16, i16 = jnp.bfloat16, jnp.int16
    part = slice(start, start + SPREAD_PART)
    base_x, base_y, base_z = bases(cell_ref[0, :, part])
    f = [frac_ref[k, 0, :, part] for k in range(3)]
    slot = start + lax.broadcasted_iota(jnp.int32, (1, SPREAD_PART), 1)
    charge = jnp.where(slot < count_ref[0, 0], charge_ref[0, :, part], 0.0)
    nothing = jnp.zeros((16, SPREAD_PART), bf16)
    x_at, x_next = wide(base_x, i16), wide(base_x + 1, i16)
    y_at, y_next = wide(base_y, i16), wide(base_y + 1, i16)
    corner = {}
    for a, along_x in enumerate((charge * (1.0 - f[0]), charge * f[0])):
        for b, along_y in enumerate((1.0 - f[1], f[1])):
            high, low = split(along_x * along_y)
            corner[a, b] = (wide(high, bf16), wide(low, bf16))
    highs, lows = [], []
    known = {}
    for tile, (xs, ys) in enumerate(patterns):
        key = tile % 3 if (tile + 1) * 16 <= LAYERS * CY else tile
        if key not in known:
            here, above = ys == y_at, ys == y_next
            known[key] = [
                [jnp.where(here, corner[a, 0][k], jnp.where(above, corner[a, 1][k], nothing)) for k in range(2)]
                for a in range(2)
            ]
        here, above = xs == x_at, xs == x_next
        for k, target in enumerate((highs, lows)):
            target.append(jnp.where(here, known[key][0][k], jnp.where(above, known[key][1][k], nothing)))
    weights = [[wide(piece, bf16) for piece in split(value)] for value in (1.0 - f[2], f[2])]
    sides = ([], [])
    z_at, z_next = wide(base_z, i16), wide((base_z + 1) & (NZ - 1), i16)
    for rows in row_z:
        here, above = rows == z_at, rows == z_next
        for k in range(2):
            sides[k].append(jnp.where(here, weights[0][k], jnp.where(above, weights[1][k], nothing)))
    return [jnp.concatenate(pieces, axis=0) for pieces in (highs, lows, *sides)]


def spread(count_ref, cell_ref, frac_ref, charge_ref, grid_ref):
    slots = cell_ref.shape[-1]
    patterns = row_patterns(SPREAD_PART)
    row_z = [(rows_iota(16, SPREAD_PART) + first).astype(jnp.int16) for first in range(0, NZ, 16)]
    parts = [
        spread_sides(count_ref, cell_ref, frac_ref, charge_ref, start, patterns, row_z)
        for start in range(0, slots, SPREAD_PART)
    ]
    top_high, top_low, z_high, z_low = [jnp.concatenate(pieces, axis=1) for pieces in zip(*parts)]
    both = matmul_nt(top_high, jnp.concatenate([z_high, z_low], axis=0))
    value = both[:, :LANES] + both[:, LANES:] + matmul_nt(top_low, z_high)
    layers = LAYERS * CY
    grid_ref[:LAYERS] = value[:layers].reshape(LAYERS, CY, LANES)
    grid_ref[LAYERS] = jnp.zeros((CY, LANES), jnp.float32)
    for x in range(LAYERS):
        grid_ref[LAYERS, strip_row(x) : strip_row(x) + 1, :] = value[layers + x : layers + x + 1]


def lane_iota():
    return lax.broadcasted_iota(jnp.int32, (1, 1, LANES), 2)


def restrict(grid_ref, down_ref, down_z_ref, middle_ref, low_ref):
    high, low = split(grid_ref[...].reshape(GRID_ROWS, LANES))
    both = matmul(down_ref[...], jnp.concatenate([high, low], axis=1))
    high, low = split(both[:, :LANES] + both[:, LANES:])
    value = matmul(jnp.concatenate([high, low], axis=1), down_z_ref[...])
    middle = value[: LOW_ROWS[0]].reshape(BX[1] + 1, ROWS[1], LANES)
    coarse = value[LOW_ROWS[0] :].reshape(BX[2] + 1, ROWS[2], LANES)
    twice = jnp.concatenate([coarse, coarse], axis=1)
    first = BX[1] - BX[2]
    mine = lane_iota() < FIRST_LANE[2]
    middle_ref[:first] = middle[:first]
    middle_ref[first:] = jnp.where(mine, middle[first:], twice)
    low_ref[...] = jnp.where(mine, middle[: BX[2] + 1], twice)


def build_taps(level, kernel_ref, padded_ref, z_ref, y_ref, real_ref, imag_ref):
    padded_ref[...] = jnp.zeros_like(padded_ref)
    padded_ref[:, :KERNEL, :KERNEL] = kernel_ref[...]
    along_z = matmul(three(padded_ref[...].reshape(KERNEL * 16, LANES), 1), z_ref[...])
    size = PERIOD[level]
    for shift in range(0, KERNEL, 2):
        pieces = []
        for one in range(shift, min(shift + 2, KERNEL)):
            rows = along_z[one * 16 : (one + 1) * 16]
            pieces.append(three(jnp.concatenate([rows[:, :LANES], rows[:, LANES:]], axis=0), 0))
        both = matmul(y_ref[...], jnp.concatenate(pieces, axis=1))
        for k in range(len(pieces)):
            real_ref[shift + k] = both[:size, k * LANES : (k + 1) * LANES]
            imag_ref[shift + k] = both[size:, k * LANES : (k + 1) * LANES]


def three(value, axis):
    high, low = split(value)
    return jnp.concatenate([high, low, high], axis=axis)


def add_spectra(level, source_ref, slots, taps, tables, along_z_ref, spectrum_ref, sums_ref, fresh):
    forward_z, _, forward_y, _ = tables
    size, pair = PERIOD[level], PAIR[level]
    used = len(slots)
    flat = source_ref[...].reshape(used * size, LANES)
    half = (used // 2 + 1) * size
    for rows in (slice(0, half), slice(half, used * size)):
        along_z_ref[rows] = matmul(three(flat[rows], 1), forward_z[...])

    def part(layer, which):
        slot = slots[layer]
        return along_z_ref[slot * size : (slot + 1) * size, which * LANES : (which + 1) * LANES]

    def combined(layer):
        if layer not in slots:
            return [-part(layer + pair, 1), part(layer + pair, 0)]
        if layer + pair not in slots:
            return [part(layer, 0), part(layer, 1)]
        return [part(layer, 0) - part(layer + pair, 1), part(layer, 1) + part(layer + pair, 0)]

    present = [layer for layer in range(SPECTRA[level]) if layer in slots or layer + pair in slots]
    for first in range(0, len(present), 2):
        group = present[first : first + 2]
        pieces = [three(jnp.concatenate(combined(layer), axis=0), 0) for layer in group]
        both = matmul(forward_y[...], jnp.concatenate(pieces, axis=1))
        for k, layer in enumerate(group):
            spectrum_ref[layer] = both[:, k * LANES : (k + 1) * LANES]
    real_ref, imag_ref = taps
    for out in range(pair):
        for tile in range(0, size, 8):
            rows, rest = slice(tile, tile + 8), slice(size + tile, size + tile + 8)
            real = jnp.zeros((8, LANES), jnp.float32) if fresh else sums_ref[out, rows]
            imag = jnp.zeros((8, LANES), jnp.float32) if fresh else sums_ref[out, rest]
            for shift in range(KERNEL):
                if out + shift in present:
                    a, b = spectrum_ref[out + shift, rows], spectrum_ref[out + shift, rest]
                    c, s = real_ref[shift, rows], imag_ref[shift, rows]
                    real = real + a * c - b * s
                    imag = imag + a * s + b * c
            sums_ref[out, rows] = real
            sums_ref[out, rest] = imag


def from_spectra(level, tables, sums_ref):
    _, inverse_z, _, inverse_y = tables
    pair, rows = PAIR[level], ROWS[level]
    lines = []
    for first in range(0, pair, 2):
        group = range(first, min(first + 2, pair))
        both = matmul(inverse_y[...], jnp.concatenate([three(sums_ref[out], 0) for out in group], axis=1))
        for k in range(len(group)):
            line = both[:rows, k * LANES : (k + 1) * LANES]
            if level == 0:
                line = jnp.concatenate([line, both[rows:, k * LANES : (k + 1) * LANES]], axis=1)
            lines.append(line)
    half = pair // 2 + 1
    values = []
    for group in (lines[:half], lines[half:]):
        value = matmul(three(jnp.concatenate(group, axis=0), 1), inverse_z[...])
        values += [value[k * rows : (k + 1) * rows] for k in range(len(group))]
    layers = [value[:, :LANES] for value in values] + [value[:, LANES:] for value in values]
    return layers[: BX[level] + 1]


GRID, MIDDLE, LOW, LANDED = range(4)


def side(step, size):
    return {-1: (0, REACH), 0: (0, size + 1), 1: (size - HALF, REACH)}[step]


class Message:
    def __init__(self, kind, dx, dy, source, layers, rows, relayed=None):
        self.kind, self.dx, self.dy = kind, dx, dy
        self.source, self.layers, self.rows, self.relayed = source, layers, rows, relayed
        self.hop = (dx, dy) if relayed is None else (0, dy)
        self.local = (layers, rows)
        if relayed is not None:
            self.local = ((0, layers[1]), (rows[0] - relayed.rows[0], rows[1]))


def plan_messages():
    near, far, face, strip = {}, {}, {}, {}
    top, bottom = (CY - 8, 8), (0, 8)
    for dx, layer in ((-2, 0), (2, BX[1])):
        far[dx, 0] = Message("far", dx, 0, LOW if dx < 0 else MIDDLE, (layer, 1), (0, 8))
    for dx in (-1, 1):
        near[dx, 0] = Message("near", dx, 0, LOW if dx < 0 else MIDDLE, side(dx, BX[1]), (0, ROWS[1]))
        strip[dx, 0] = Message("strip", dx, 0, GRID, (CX + 1, 1), bottom if dx < 0 else top)
        for name, rows in (("top", top), ("bottom", bottom), ("centre", (8, CY - 16))):
            face[dx, name] = Message("face", dx, 0, GRID, side(dx, BX[0]), rows)
    for dy in (-1, 1):
        rows = bottom if dy < 0 else (ROWS[1] - 8, 8)
        near[0, dy] = Message("near", 0, dy, MIDDLE, side(0, BX[1]), rows)
        face[0, dy] = Message("face", 0, dy, GRID, side(0, BX[0]), bottom if dy < 0 else top)
        for dx in (-2, 2):
            far[dx, dy] = Message("far", dx, dy, LANDED, far[dx, 0].layers, (0, 8), far[dx, 0])
        for dx in (-1, 1):
            near[dx, dy] = Message("near", dx, dy, LANDED, near[dx, 0].layers, rows, near[dx, 0])
            first = face[dx, "bottom" if dy < 0 else "top"]
            face[dx, dy] = Message("face", dx, dy, LANDED, first.layers, first.rows, first)
    strip[0, 1] = Message("strip", 0, 1, GRID, (CX + 1, 1), (0, CY))
    for dx in (-1, 1):
        strip[dx, 1] = Message("strip", dx, 1, LANDED, (CX + 1, 1), strip[dx, 0].rows, strip[dx, 0])
    sides = (-1, 1)
    first = [near[dx, 0] for dx in sides]
    first += [face[dx, name] for name in ("top", "bottom") for dx in sides] + [strip[dx, 0] for dx in sides]
    first += [near[0, dy] for dy in sides] + [far[dx, 0] for dx in (-2, 2)]
    first += [face[0, dy] for dy in sides] + [strip[0, 1]] + [face[dx, "centre"] for dx in sides]
    second = [near[dx, dy] for dx in sides for dy in sides] + [far[dx, dy] for dx in (-2, 2) for dy in sides]
    second += [face[dx, dy] for dy in (1, -1) for dx in sides] + [strip[dx, 1] for dx in sides]
    return first, second


FIRST, SECOND = plan_messages()
PLAN = FIRST + SECOND


def add_rows(window_ref, layer, first, piece):
    rows = slice(first, first + piece.shape[-2])
    layers = slice(layer, layer + piece.shape[0])
    window_ref[layers, rows, :] = window_ref[layers, rows, :] + piece


def add_level_rows(window_ref, level, layer, dy, piece):
    size = BY[level]
    if dy == 0:
        add_rows(window_ref, layer, 0, piece[:, : size + 1])
    elif dy < 0:
        add_rows(window_ref, layer, size, piece[:, :REACH])
    else:
        base = piece.shape[-2] - 8 if piece.shape[-2] > 8 else (size // 8) * 8
        first = size - HALF - base
        add_rows(window_ref, layer, PERIOD[level] - HALF, piece[:, first : first + HALF])
        add_rows(window_ref, layer, 0, piece[:, first + HALF : first + HALF + 1])


def add_low(windows, message, landed):
    dx, dy, first = message.dx, message.dy, message.layers[0]
    if message.kind == "far":
        layer = HALF + (0 if dx < 0 else BX[2]) - dx * BX[2]
        add_level_rows(windows[2], 2, layer, dy, landed[...])
        return
    add_level_rows(windows[1], 1, HALF + first - dx * BX[1], dy, landed[...])
    ride = BX[1] - BX[2] if dx == 0 else 0
    add_level_rows(windows[2], 2, HALF - dx * BX[2], dy, landed[ride : ride + BX[2] + 1, :8, :])


def add_fine(window_ref, message, landed):
    dx, dy, rows = message.dx, message.dy, message.rows
    offset = {-1: REACH, 0: 0, 1: HALF - BX[0]}[dx]
    if message.kind == "strip":
        low, size = side(dx, BX[0])
        target = CY if dy == 0 else 0
        for k in range(size):
            place = strip_row(low + k) - rows[0]
            layer = offset + low + k
            window_ref[layer, target : target + 1, :] = (
                window_ref[layer, target : target + 1, :] + landed[0, place : place + 1, :]
            )
        return
    first, count = message.layers
    layers = slice(offset + first, offset + first + count)
    row = lax.broadcasted_iota(jnp.int32, (1, 8, LANES), 1)
    value = landed[...]
    at = slice(rows[0], rows[0] + rows[1])
    if dy < 0:
        at, value = slice(CY, CY + 8), jnp.where(row < REACH, value, 0.0)
    elif dy > 0:
        at, value = slice(PERIOD[0] - 8, PERIOD[0]), jnp.where(row >= 8 - HALF, value, 0.0)
    window_ref[layers, at, :] = window_ref[layers, at, :] + value


def grid_kernel(sizes, n_tables, places, *refs):
    count_ref, cell_ref, frac_ref, charge_ref = refs[:4]
    kernels = refs[4:7]
    table_sources = refs[7 : 7 + n_tables]
    out_ref = refs[7 + n_tables]
    scratch = list(refs[8 + n_tables :])

    def take(count):
        taken = scratch[:count]
        del scratch[:count]
        return taken

    grid_ref, middle_ref, low_ref, padded_ref = take(4)
    table_refs = take(n_tables)
    windows, reals, imags, along_z, spectra, sums = take(3), take(3), take(3), take(3), take(3), take(3)
    (edges_ref,) = take(1)
    landed = take(len(PLAN))
    send_sem, recv_sem, table_sem = take(3)

    me = (lax.axis_index("gx"), lax.axis_index("gy"))

    def device(dx, dy):
        return (lax.rem(me[0] + dx + sizes[0], sizes[0]), lax.rem(me[1] + dy + sizes[1], sizes[1]))

    barrier = pltpu.get_barrier_semaphore()
    around = sorted({message.hop for message in PLAN})
    for dx, dy in around:
        pl.semaphore_signal(barrier, inc=1, device_id=device(dx, dy), device_id_type=MESH)
    loads = [
        pltpu.make_async_copy(source, target, table_sem.at[index])
        for index, (source, target) in enumerate(zip(table_sources, table_refs))
    ]
    for load in loads:
        load.start()

    spread(count_ref, cell_ref, frac_ref, charge_ref, grid_ref)
    for load in loads[:2]:
        load.wait()
    down_ref, down_z_ref, stacked_ref = table_refs
    restrict(grid_ref, down_ref, down_z_ref, middle_ref, low_ref)
    pl.semaphore_wait(barrier, len(around))

    sources = (grid_ref, middle_ref, low_ref)
    copies = {}
    for index, message in enumerate(PLAN):
        relayed = message.relayed
        source = sources[message.source] if relayed is None else landed[PLAN.index(relayed)]
        (first, size), (low, rows) = message.local
        copies[message] = pltpu.make_async_remote_copy(
            src_ref=source.at[pl.ds(first, size), pl.ds(low, rows)],
            dst_ref=landed[index],
            send_sem=send_sem.at[index],
            recv_sem=recv_sem.at[index],
            device_id=device(*message.hop),
            device_id_type=MESH,
        )
    arrived = set()

    def arrive(message):
        if message not in arrived:
            arrived.add(message)
            copies[message].wait_recv()

    for message in FIRST:
        copies[message].start()
    loads[2].wait()
    up_ref, *parts = [Part(stacked_ref, place) for place in places]

    level_tables = [parts[6 * level : 6 * level + 6] for level in range(LEVELS)]
    for level in (2, 1, 0):
        build_taps(level, kernels[level], padded_ref, *level_tables[level][4:], reals[level], imags[level])

    for level in range(LEVELS):
        windows[level][...] = jnp.zeros_like(windows[level])
    edges_ref[...] = jnp.zeros_like(edges_ref)
    windows[0][:, :CY, :] = grid_ref[: CX + 1]
    for x in range(CX + 1):
        windows[0][x, CY : CY + 1, :] = grid_ref[CX + 1, strip_row(x) : strip_row(x) + 1, :]
    windows[1][HALF : HALF + BX[1] + 1, : ROWS[1], :] = middle_ref[...]
    windows[2][HALF : HALF + BX[2] + 1, : ROWS[2], :] = low_ref[:, : ROWS[2], :]

    for message in SECOND:
        if message.kind in ('near', 'far'):
            arrive(message.relayed)
            copies[message].start()
    def run(level, source_ref, layers, fresh):
        slots = {layer: slot for slot, layer in enumerate(layers)}
        taps = (reals[level], imags[level])
        tables = level_tables[level][:4]
        add_spectra(level, source_ref, slots, taps, tables, along_z[level], spectra[level], sums[level], fresh)

    fine = [message for message in PLAN if message.kind in ("face", "strip")]
    for message in fine:
        if message.dx == 0:
            arrive(message)
            add_fine(windows[0], message, landed[PLAN.index(message)])
    run(0, windows[0], range(HALF, HALF + CX + 1), True)
    for message in SECOND:
        if message.kind not in ('near', 'far'):
            arrive(message.relayed)
            copies[message].start()
    for message in PLAN:
        if message.kind in ("near", "far"):
            arrive(message)
            add_low(windows, message, landed[PLAN.index(message)])
    below = []
    for level in (1, 2):
        run(level, windows[level], range(BX[level] + 1 + 2 * HALF), True)
        below += from_spectra(level, level_tables[level][:4], sums[level])
    high, low = split(jnp.concatenate(below, axis=0))
    both = matmul(up_ref[...], jnp.concatenate([high, low], axis=1))
    out_ref[...] = (both[:, :LANES] + both[:, LANES:]).reshape(out_ref.shape)
    for message in PLAN:
        copies[message].wait_send()
    for message in fine:
        if message.dx != 0:
            arrive(message)
            add_fine(edges_ref, message, landed[PLAN.index(message)])
    last = CX + 1 + 2 * HALF
    run(0, edges_ref, [*range(REACH), *range(last - REACH, last)], False)
    layers = from_spectra(0, level_tables[0][:4], sums[0])
    for x in range(CX + 1):
        out_ref[x] = out_ref[x] + layers[x][:CY]
        at = slice(strip_row(x), strip_row(x) + 1)
        out_ref[CX + 1, at, :] = out_ref[CX + 1, at, :] + layers[x][CY : CY + 1]


def force_kernel(count_ref, cell_ref, frac_ref, charge_ref, grid_ref, potential_ref, forces_ref, left_ref):
    slots = cell_ref.shape[-1]
    potential_ref[...] = grid_ref[:CX]
    forces_ref[...] = jnp.zeros_like(forces_ref)
    left_ref[...] = jnp.concatenate(split(grid_ref[...].reshape(GRID_ROWS, LANES)), axis=1)
    count = count_ref[0, 0]

    def pick(values, base):
        width = CX // 2
        while width >= 1:
            bit = (base & width) != 0
            values = [jnp.where(bit, values[width + k], values[k]) for k in range(width + 1)]
            width //= 2
        return values

    def chunk(index):
        part = pl.ds(pl.multiple_of(index * FORCE_CHUNK, FORCE_CHUNK), FORCE_CHUNK)
        base_x, base_y, base_z = bases(cell_ref[0, :, part])
        row = rows_iota(16, FORCE_CHUNK)
        one, nothing = [jnp.full((16, FORCE_CHUNK), value, jnp.bfloat16) for value in (1.0, 0.0)]
        found = []
        for at_z in (base_z, (base_z + 1) & (NZ - 1)):
            target = wide(at_z, jnp.int16)
            chosen = [jnp.where((row + z).astype(jnp.int16) == target, one, nothing) for z in range(0, NZ, 16)]
            found.append(matmul(left_ref[...], jnp.concatenate(chosen * 2, axis=0)))
        shape = (8, FORCE_CHUNK)
        f = [jnp.broadcast_to(frac_ref[k, 0, :, part], shape) for k in range(3)]
        slot = index * FORCE_CHUNK + lax.broadcasted_iota(jnp.int32, (1, FORCE_CHUNK), 1)
        charge = jnp.where(slot < count, charge_ref[0, :, part], 0.0)
        base_x = jnp.broadcast_to(base_x, shape)
        base_y = jnp.broadcast_to(base_y, shape)
        row = rows_iota(*shape)
        across, along, slope = [jnp.zeros(shape, jnp.float32) for _ in range(3)]
        for tile in range(CY // 8):
            ends = []
            for values in found:
                rows = [values[x * CY + tile * 8 : x * CY + tile * 8 + 8] for x in range(CX + 1)]
                ends.append(pick(rows, base_x))
            rise = [ends[1][k] - ends[0][k] for k in range(2)]
            level = [ends[0][k] + f[2] * rise[k] for k in range(2)]
            step_x = level[1] - level[0]
            lower, upper = row + tile * 8 == base_y, row + tile * 8 == base_y + 1
            weight = jnp.where(lower, 1.0 - f[1], jnp.where(upper, f[1], 0.0))
            sign = jnp.where(lower, -1.0, jnp.where(upper, 1.0, 0.0))
            across = across + weight * step_x
            along = along + sign * (level[0] + f[0] * step_x)
            slope = slope + weight * (rise[0] + f[0] * (rise[1] - rise[0]))
        ends = []
        for values in found:
            low, high = [jnp.zeros(shape, jnp.float32) for _ in range(2)]
            for tile in range(CY // 8):
                value = values[(CX + 1) * CY + tile * 8 : (CX + 1) * CY + tile * 8 + 8]
                layer = row + (tile * 8 if tile < 2 else 12)
                if tile == 1:
                    layer = jnp.where(layer < 12, layer, -5)
                low = jnp.where(layer == base_x, value, low)
                high = jnp.where(layer == base_x + 1, value, high)
            ends.append((low, high))
        edge = base_y == CY - 1
        weight = jnp.where(edge, f[1], 0.0)
        rise = [ends[1][k] - ends[0][k] for k in range(2)]
        level = [ends[0][k] + f[2] * rise[k] for k in range(2)]
        across = across + weight * (level[1] - level[0])
        along = along + jnp.where(edge, level[0] + f[0] * (0.0 - level[0]) + f[0] * level[1], 0.0)
        slope = slope + weight * (rise[0] + f[0] * (0.0 - rise[0]) + f[0] * rise[1])
        for k, value in enumerate((across, along, slope)):
            forces_ref[k, 0, :, part] = -charge * jnp.sum(value, axis=0, keepdims=True)

    def step(index, carry):
        for k in range(FORCE_UNROLL):
            chunk(index * FORCE_UNROLL + k)
        return carry

    width = FORCE_CHUNK * FORCE_UNROLL
    lax.fori_loop(0, jnp.minimum(pl.cdiv(count, width), slots // width), step, 0)


VMEM = pl.BlockSpec(memory_space=pltpu.VMEM)
SMEM = pl.BlockSpec(memory_space=pltpu.SMEM)
ANY = pl.BlockSpec(memory_space=pl.ANY)


def solution(mesh):
    sizes = (mesh.shape["gx"], mesh.shape["gy"])
    constants, places = tables()

    def per_device(atom_cell, atom_frac, atom_charge, atom_count, fine_kernel, middle_kernel, coarse_kernel):
        slots = atom_cell.shape[-1]
        f32 = jnp.float32
        grid = (CX + 2, CY, LANES)
        scratch = [
            pltpu.VMEM(grid, f32),
            pltpu.VMEM((BX[1] + 1, ROWS[1], LANES), f32),
            pltpu.VMEM((BX[2] + 1, ROWS[1], LANES), f32),
            pltpu.VMEM((KERNEL, 16, LANES), f32),
        ]
        scratch += [pltpu.VMEM(table.shape, jnp.dtype(table.dtype)) for table in constants]
        scratch += [pltpu.VMEM((WINDOW[k], PERIOD[k], LANES), f32) for k in range(LEVELS)]
        scratch += [pltpu.VMEM((KERNEL, PERIOD[k], LANES), f32) for k in range(LEVELS)] * 2
        scratch += [pltpu.VMEM((WINDOW[k] * PERIOD[k], 2 * LANES), f32) for k in range(LEVELS)]
        scratch += [pltpu.VMEM((SPECTRA[k], 2 * PERIOD[k], LANES), f32) for k in range(LEVELS)]
        scratch += [pltpu.VMEM((PAIR[k], 2 * PERIOD[k], LANES), f32) for k in range(LEVELS)]
        scratch += [pltpu.VMEM((2 * REACH, PERIOD[0], LANES), f32)]
        scratch += [pltpu.VMEM((message.layers[1], message.rows[1], LANES), f32) for message in PLAN]
        scratch += [pltpu.SemaphoreType.DMA((len(PLAN),))] * 2 + [pltpu.SemaphoreType.DMA((len(constants),))]
        extended = pl.pallas_call(
            lambda *refs: grid_kernel(sizes, len(constants), places, *refs),
            out_shape=pltpu.VMEM(grid, f32),
            in_specs=[SMEM] + [VMEM] * 6 + [ANY] * len(constants),
            out_specs=VMEM,
            scratch_shapes=scratch,
            compiler_params=pltpu.CompilerParams(collective_id=0, has_side_effects=True),
            name="grid",
        )(
            atom_count,
            atom_cell,
            atom_frac,
            atom_charge,
            fine_kernel,
            middle_kernel,
            coarse_kernel,
            *[jnp.asarray(table) for table in constants],
        )
        potential, forces = pl.pallas_call(
            force_kernel,
            out_shape=(jax.ShapeDtypeStruct((CX, CY, NZ), f32), jax.ShapeDtypeStruct((3, 1, 1, slots), f32)),
            in_specs=[SMEM] + [VMEM] * 4,
            out_specs=(VMEM, VMEM),
            scratch_shapes=[pltpu.VMEM((GRID_ROWS, 2 * LANES), jnp.bfloat16)],
            name="forces",
        )(atom_count, *[pltpu.with_memory_space_constraint(x, pltpu.VMEM) for x in (atom_cell, atom_frac, atom_charge, extended)])
        return potential, forces

    return jax.shard_map(
        per_device,
        mesh=mesh,
        in_specs=(
            P("gx", "gy", None),
            P(None, "gx", "gy", None),
            P("gx", "gy", None),
            P("gx", "gy"),
            P(),
            P(),
            P(),
        ),
        out_specs=(P("gx", "gy", None), P(None, "gx", "gy", None)),
        check_vma=False,
    )
```
